32 devices in a mesh: seq: 8 (over z, x), gate: 4 (over y, core).
Axes of the slice: x: 2, y: 2, z: 4, core: 2. Of those that a mesh axis runs over, the one named last changes fastest.
Arguments:
- layer_input: bfloat16 [8192, 2304], P('seq', 'gate'), may hold values from -6 to 6
- keep: int32 [8192], P('seq'), may hold values from 0 to 1, as said below
- w_now: bfloat16 [3, 2304, 2304], P(None, 'seq', 'gate'), may hold values from -0.09375 to 0.09375
- w_prev: bfloat16 [3, 2304, 2304], P(None, 'seq', 'gate'), may hold values from -0.09375 to 0.09375
- bias: float32 [3, 2304], P(None, 'gate'), may hold values from -2 to 10
- grad_out: bfloat16 [8192, 2304], P('seq', 'gate'), may hold values from -6 to 6
Outputs:
- hidden: bfloat16 [8192, 2304], P('seq', 'gate')
- grad_x: bfloat16 [8192, 2304], P('seq', 'gate')
- grad_now: float32 [3, 2304, 2304], P(None, 'seq', 'gate')
- grad_prev: float32 [3, 2304, 2304], P(None, 'seq', 'gate')
- grad_bias: float32 [3, 2304], P(None, 'gate')
The draws below stay inside these ranges and needn't reach their ends.
Inputs may be any that keep to these rules, and one draw needn't show every extreme that they name: keep is 0 at the first token of every document and 1 elsewhere; the stream's first token begins a document; documents have uneven lengths and cross block ends.
All inputs are finite; a program needn't handle non-finite values.
Results may differ from the reference program's by a relative error of at most 0.0049.
Values may be sent and summed in bfloat16 or wider, within the bound.
No kernel may reach another device: no remote copies, remote signals or barrier semaphores. Data moves between devices by JAX's collectives and lax.ppermute only.
A program may use at most 320 MiB of HBM per device.

```python
import jax
import jax.numpy as jnp
from jax import lax

D = 2304
TOK_DEV = 1024
TOKENS = 8192


def draw_keep(key, part):
    starts = jax.random.randint(key, (TOKENS,), 0, 2 * TOK_DEV) == 0
    starts = starts.at[0].set(True)
    return jnp.where(starts, 0, 1).astype(jnp.int32)


def draw_bias(key, part):
    first, second, third, fourth = jax.random.split(key, 4)
    others = jnp.clip(0.5 * jax.random.normal(first, (2, D), jnp.float32), -2.0, 2.0)
    share = 0.5
    slow = jax.random.uniform(second, (D,), jnp.float32) < share
    fast_part = jax.random.uniform(third, (D,), jnp.float32, -1.0, 2.0)
    slow_part = jax.random.uniform(fourth, (D,), jnp.float32, 6.0, 10.0)
    forget_bias = jnp.where(slow, slow_part, fast_part)
    return jnp.stack([others[0], forget_bias, others[1]]).astype(jnp.float32)


def shard_levels(stream_key, shape, pieces, least, top_value):
    def one(position, blocks):
        heights = jax.random.uniform(jax.random.fold_in(jax.random.fold_in(stream_key, 6), position), (blocks,), jnp.float32, least / len(pieces), top_value / len(pieces))
        return jnp.repeat(jnp.exp(heights), shape[position] // blocks).reshape((-1,) + (1,) * (len(shape) - position - 1))

    gain = one(*pieces[0])
    for cut in pieces[1:]:
        gain = gain * one(*cut)
    return gain


def normal_values(own_key, dims, deviation, bound, cuts=(), kind=jnp.bfloat16):
    entries = jax.random.normal(own_key, dims, jnp.float32) * deviation
    if len(cuts) > 0:
        entries = shard_levels(own_key, dims, cuts, -0.22, 0.18) * entries
    return jnp.clip(entries, min=-bound, max=bound).astype(kind)


def setup_inputs(seed: int = 0) -> dict:
    key_of = jax.random.split(jax.random.key(seed), 7)
    layer_input = normal_values(key_of[0], (TOKENS, D), 1.0, 6.0, ((0, 8), (1, 4)))
    keep = draw_keep(jax.random.fold_in(key_of[6], 71), 0)
    w_now = normal_values(key_of[2], (3, D, D), (2 * D) ** -0.5, 0.09375, ((1, 8), (2, 4)))
    w_prev = normal_values(key_of[3], (3, D, D), (2 * D) ** -0.5, 0.09375, ((1, 8), (2, 4)))
    bias = draw_bias(jax.random.fold_in(key_of[6], 71), 0)
    grad_out = normal_values(key_of[5], (TOKENS, D), 1.0, 6.0, ((0, 8), (1, 4)))
    return {"layer_input": layer_input, "keep": keep, "w_now": w_now, "w_prev": w_prev, "bias": bias, "grad_out": grad_out}


@jax.custom_vjp
def low(v):
    return lax.optimization_barrier(v.astype(jnp.bfloat16)).astype(jnp.float32)

@jax.custom_vjp
def low_back(v):
    return v

def low_keep(v):
    return (low(v), None)

def low_pass(kept, grad):
    return (grad,)

def back_keep(v):
    return (v, None)

def back_low(kept, grad):
    return (low(grad),)
low.defvjp(low_keep, low_pass)
low_back.defvjp(back_keep, back_low)

def combine(early, late):
    return (early[0] * late[0], early[1] * late[0] + late[1])

def forward(inputs, tap_now, tap_prev, offsets, keep_mask):
    shifted = jnp.concatenate([jnp.zeros((1, inputs.shape[1]), jnp.float32), inputs[:-1]], axis=0)
    prev_rows = shifted * keep_mask[:, None]
    gates = jnp.einsum('td,kdc->tkc', inputs, tap_now, precision=lax.Precision.HIGHEST)
    gates = gates + jnp.einsum('td,kdc->tkc', prev_rows, tap_prev, precision=lax.Precision.HIGHEST)
    gates = low_back(gates + offsets[None])
    cand = jnp.tanh(gates[:, 0])
    forget = jax.nn.sigmoid(gates[:, 1])
    intake = jax.nn.sigmoid(-gates[:, 1])
    output = jax.nn.sigmoid(gates[:, 2])
    decays = keep_mask[:, None] * forget
    factor, states = lax.associative_scan(combine, (decays, intake * cand), axis=0)
    return output * states

def reference(layer_input, keep, w_now, w_prev, bias, grad_out):
    keep_mask = keep.astype(jnp.float32)

    def wrapped(inputs, tap_now, tap_prev, offsets):
        return forward(inputs, tap_now, tap_prev, offsets, keep_mask)
    hidden, pullback = jax.vjp(wrapped, layer_input.astype(jnp.float32), w_now.astype(jnp.float32), w_prev.astype(jnp.float32), bias.astype(jnp.float32))
    grad_x, grad_now, grad_prev, grad_bias = pullback(grad_out.astype(jnp.float32))
    return (hidden.astype(jnp.bfloat16), grad_x.astype(jnp.bfloat16), grad_now, grad_prev, grad_bias)
```

```python
import jax, jax.numpy as jnp
from jax import lax
from jax.experimental import pallas as pl
from jax.experimental.pallas import tpu as pltpu
from jax.sharding import PartitionSpec as P
F32=jnp.float32; BF=jnp.bfloat16
SEGS=8; LANES=128; TM=64

def both(g):
    e=jnp.exp(-jnp.abs(g)); r=1.0/(1.0+e); er=e*r
    up=g>=0
    return jnp.where(up,r,er), jnp.where(up,er,r)

def cuts(c):
    return [(l, l*LANES, min(LANES, c-l*LANES)) for l in range(-(-c//LANES))]

def tot_kernel(g_ref, up_ref, keep_ref, seg_ref, tot_ref, d_s, s_s, q_s, seg_s):
    _,t,c=g_ref.shape
    span=t//SEGS
    lanes=cuts(c)
    def act(r,_):
        rows=pl.ds(pl.multiple_of(r*TM,TM),TM)
        for l,lo,w in lanes:
            ch=slice(lo,lo+w)
            f,i=both(g_ref[1,rows,ch])
            o,_=both(g_ref[2,rows,ch])
            d=keep_ref[rows,:w]*f
            d_s[l,rows,:w]=d
            s_s[l,rows,:w]=i*jnp.tanh(g_ref[0,rows,ch])
            q_s[l,rows,:w]=d*(up_ref[rows,ch].astype(F32)*o)
        return 0
    lax.fori_loop(0,t//TM,act,0)
    one=jnp.ones((SEGS,LANES),F32); zero=jnp.zeros((SEGS,LANES),F32)
    def step(j,carry):
        at=pl.ds(j,SEGS,stride=span); back=pl.ds(span-1-j,SEGS,stride=span)
        new=[]
        for l,_,_ in lanes:
            a,s,r=carry[l]
            d=d_s[l,at,:]
            new.append((a*d, d*s+s_s[l,at,:], d_s[l,back,:]*r+q_s[l,back,:]))
        return tuple(new)
    res=lax.fori_loop(0,span,step,tuple((one,zero,zero) for _ in lanes),unroll=4)
    for l,lo,w in lanes:
        for k in range(3):
            seg_s[k]=res[l][k]
            seg_ref[k,:,lo:lo+w]=res[l][k][:,:w]
        a=jnp.ones((1,LANES),F32); s=jnp.zeros((1,LANES),F32); r=jnp.zeros((1,LANES),F32)
        for k in range(SEGS):
            m=seg_s[0,k:k+1,:]
            s=m*s+seg_s[1,k:k+1,:]
            a=a*m
            b=SEGS-1-k
            r=seg_s[0,b:b+1,:]*r+seg_s[2,b:b+1,:]
        for k,v in enumerate((a,s,r)): tot_ref[k:k+1,lo:lo+w]=v[:,:w]

def totals(gates, up, keep):
    _,t,c=gates.shape
    lt=len(cuts(c))
    return pl.pallas_call(tot_kernel,
        out_shape=(jax.ShapeDtypeStruct((3,SEGS,c),F32),jax.ShapeDtypeStruct((3,c),F32)),
        scratch_shapes=[pltpu.VMEM((lt,t,LANES),F32)]*3+[pltpu.VMEM((3,SEGS,LANES),F32)],
        compiler_params=pltpu.CompilerParams(vmem_limit_bytes=60<<20),
        name="pool_totals")(gates,up,keep)

def fin_kernel(me_ref, g_ref, up_ref, keep_ref, seg_ref, all_ref, hid_ref, gg_ref, gb_ref, d_s, s_s, q_s, p_s, c_s):
    _,t,c=g_ref.shape
    n=all_ref.shape[0]
    span=t//SEGS
    lanes=cuts(c)
    me=me_ref[0]
    def act(r,_):
        rows=pl.ds(pl.multiple_of(r*TM,TM),TM)
        for l,lo,w in lanes:
            ch=slice(lo,lo+w)
            f,i=both(g_ref[1,rows,ch])
            o,_=both(g_ref[2,rows,ch])
            d_s[l,rows,:w]=keep_ref[rows,:w]*f
            s_s[l,rows,:w]=i*jnp.tanh(g_ref[0,rows,ch])
            q_s[l,rows,:w]=up_ref[rows,ch].astype(F32)*o
        return 0
    lax.fori_loop(0,t//TM,act,0)
    h=jnp.zeros((1,c),F32); r=jnp.zeros((1,c),F32)
    for k in range(n):
        h=jnp.where(k<me, all_ref[k,0:1,:]*h+all_ref[k,1:2,:], h)
        b=n-1-k
        r=jnp.where(b>me, all_ref[b,0:1,:]*r+all_ref[b,2:3,:], r)
    for k in range(SEGS):
        b=SEGS-1-k
        for l,lo,w in lanes:
            c_s[0,l,k:k+1,:w]=h[:,lo:lo+w]
            c_s[1,l,b:b+1,:w]=r[:,lo:lo+w]
        h=seg_ref[0,k:k+1,:]*h+seg_ref[1,k:k+1,:]
        r=seg_ref[0,b:b+1,:]*r+seg_ref[2,b:b+1,:]
    def step(j,carry):
        at=pl.ds(j,SEGS,stride=span); back=pl.ds(span-1-j,SEGS,stride=span)
        new=[]
        for l,_,_ in lanes:
            h,r=carry[l]
            dh=d_s[l,at,:]*h
            h=dh+s_s[l,at,:]
            p_s[l,at,:]=dh
            s_s[l,at,:]=h
            g=q_s[l,back,:]+r
            q_s[l,back,:]=g
            new.append((h, d_s[l,back,:]*g))
        return tuple(new)
    lax.fori_loop(0,span,step,tuple((c_s[0,l],c_s[1,l]) for l,_,_ in lanes),unroll=4)
    def out(r,acc):
        rows=pl.ds(pl.multiple_of(r*TM,TM),TM)
        new=[]
        for l,lo,w in lanes:
            ch=slice(lo,lo+w)
            f,i=both(g_ref[1,rows,ch])
            o,cl=both(g_ref[2,rows,ch])
            z=jnp.tanh(g_ref[0,rows,ch])
            gs=q_s[l,rows,:w]; oh=o*s_s[l,rows,:w]
            hid_ref[rows,ch]=oh.astype(BF)
            gi=gs*i
            for k,v in enumerate((gi*(1.0-z*z), gi*(p_s[l,rows,:w]-f*z), up_ref[rows,ch].astype(F32)*oh*cl)):
                gg_ref[k,rows,ch]=v.astype(BF)
                new.append(acc[len(new)]+jnp.sum(v.reshape(TM//8,8,w),axis=0))
        return tuple(new)
    acc=lax.fori_loop(0,t//TM,out,tuple(jnp.zeros((8,w),F32) for _,_,w in lanes for _ in range(3)))
    for l,lo,w in lanes:
        for k in range(3): gb_ref[k:k+1,lo:lo+w]=jnp.sum(acc[3*l+k],axis=0,keepdims=True)

def finish(me, gates, up, keep, seg, every):
    _,t,c=gates.shape
    lt=len(cuts(c))
    V=pl.BlockSpec(memory_space=pltpu.VMEM)
    return pl.pallas_call(fin_kernel,
        in_specs=[pl.BlockSpec(memory_space=pltpu.SMEM)]+[V]*5,
        out_shape=(jax.ShapeDtypeStruct((t,c),BF),jax.ShapeDtypeStruct((3,t,c),BF),jax.ShapeDtypeStruct((3,c),F32)),
        scratch_shapes=[pltpu.VMEM((lt,t,LANES),F32)]*4+[pltpu.VMEM((2,lt,SEGS,LANES),F32)],
        compiler_params=pltpu.CompilerParams(vmem_limit_bytes=60<<20),
        name="pool_finish")(me,gates,up,keep,seg,every)


def on_device(layer_input, keep, w_now, w_prev, bias, grad_out):
    me = lax.axis_index("seq")
    n = lax.axis_size("seq")
    x = lax.all_gather(layer_input, "gate", axis=1, tiled=True)
    ahead = [(i, i + 1) for i in range(n - 1)]
    back = [(i + 1, i) for i in range(n - 1)]
    halo = lax.ppermute(x[-1:], "seq", ahead)
    xp = jnp.concatenate([halo, x[:-1]], axis=0)
    xp = jnp.where(keep[:, None] > 0, xp, jnp.zeros_like(xp))
    wn = lax.all_gather(w_now, "seq", axis=1, tiled=True)
    wp = lax.all_gather(w_prev, "seq", axis=1, tiled=True)
    gates = jnp.einsum("td,kdc->ktc", x, wn, preferred_element_type=F32)
    gates = gates + jnp.einsum("td,kdc->ktc", xp, wp, preferred_element_type=F32)
    gates = gates + bias[:, None, :]
    keep_f = keep.astype(F32)
    keep_w = jnp.broadcast_to(keep_f[:, None], (keep.shape[0], LANES))
    seg, tot = totals(gates, grad_out, keep_w)
    every = lax.all_gather(tot, "seq", axis=0)
    hidden, g, gb = finish(me[None].astype(jnp.int32), gates, grad_out, keep_w, seg, every)
    kb = keep.astype(BF)
    follow = lax.ppermute(g[:, :1] * kb[0], "seq", back)
    gs = jnp.concatenate([g[:, 1:] * kb[None, 1:, None], follow], axis=1)
    part_now = jnp.einsum("td,ktc->kdc", x, g, preferred_element_type=F32).astype(BF)
    grad_now = lax.psum_scatter(part_now, "seq", scatter_dimension=1, tiled=True).astype(F32)
    part_prev = jnp.einsum("td,ktc->kdc", x, gs, preferred_element_type=F32).astype(BF)
    grad_prev = lax.psum_scatter(part_prev, "seq", scatter_dimension=1, tiled=True).astype(F32)
    grad_bias = lax.psum(gb, "seq")
    dx = jnp.einsum("ktc,kdc->td", g, wn, preferred_element_type=F32)
    dx = dx + jnp.einsum("ktc,kdc->td", gs, wp, preferred_element_type=F32)
    grad_x = lax.psum_scatter(dx.astype(BF), "gate", scatter_dimension=1, tiled=True)
    return hidden, grad_x, grad_now, grad_prev, grad_bias


def solution(mesh):
    return jax.shard_map(
        on_device,
        mesh=mesh,
        in_specs=(P("seq", "gate"), P("seq"), P(None, "seq", "gate"), P(None, "seq", "gate"), P(None, "gate"), P("seq", "gate")),
        out_specs=(P("seq", "gate"), P("seq", "gate"), P(None, "seq", "gate"), P(None, "seq", "gate"), P(None, "gate")),
        check_vma=False,
    )
```

```python
import functools

import jax
import jax.numpy as jnp
from jax import lax
from jax.experimental import pallas as pl
from jax.experimental.pallas import tpu as pltpu
from jax.sharding import PartitionSpec as P

F32 = jnp.float32
BF = jnp.bfloat16
SEGS = 8
LANES = 128
TM = 64
ROWS = 256
EDGE = 16
VMEM = 62 << 20
WIDTHS = (128, 160)


def ceil_to(value, unit):
    return -(-value // unit) * unit


def both(g):
    e = jnp.exp(-jnp.abs(g))
    r = 1.0 / (1.0 + e)
    er = e * r
    pos = g >= 0
    return jnp.where(pos, r, er), jnp.where(pos, er, r)


def load_up(ref, rows, lo, w):
    return ref[rows, lo : lo + w].astype(F32)


def cuts(c):
    return [(i, i * LANES, min(LANES, c - i * LANES)) for i in range(-(-c // LANES))]


def params():
    return pltpu.CompilerParams(vmem_limit_bytes=VMEM)


URGENT, LATER = 100, 50
TINY = pl.CostEstimate(flops=1 << 10, bytes_accessed=1 << 10, transcendentals=0)
SMEM_SPEC = pl.BlockSpec(memory_space=pltpu.SMEM)
VMEM_SPEC = pl.BlockSpec(memory_space=pltpu.VMEM)
ANY_SPEC = pl.BlockSpec(memory_space=pl.ANY)


def offsets(widths):
    at = 0
    for w in widths:
        yield at, w
        at += w


def pack_w_kernel(widths, share, place, now_ref, prev_ref, *outs):
    half = now_ref.shape[2] // 2
    low = place[1] == 0
    for tap, ref in enumerate((now_ref, prev_ref)):
        for k in range(3):
            v = ref[k].astype(F32)
            mine = jnp.where(low, v[:, :half], v[:, half:])
            other = jnp.where(low, v[:, half:], v[:, :half])
            at, w = list(offsets(widths))[share]
            lo = (tap * 3 + k) * w
            outs[0][:, lo : lo + w] = mine[:, at : at + w].astype(BF)
            outs[1][:, lo : lo + w] = other[:, at : at + w].astype(BF)


def pack_weights(widths, share, place, w_now, w_prev):
    rows, w = w_now.shape[1], widths[share]
    return pl.pallas_call(
        functools.partial(pack_w_kernel, widths, share),
        in_specs=[SMEM_SPEC, VMEM_SPEC, VMEM_SPEC],
        out_shape=[jax.ShapeDtypeStruct((rows, 6 * w), BF)] * 2,
        compiler_params=params(),
        cost_estimate=TINY,
        name="pack_weights",
    )(place, w_now, w_prev)


def pack_up_kernel(widths, place, up_ref, *outs):
    half = up_ref.shape[1] // 2
    low = place[1] == 0

    def body(r, _):
        rows = pl.ds(pl.multiple_of(r * TM, TM), TM)
        v = up_ref[rows, :].astype(F32)
        mine = jnp.where(low, v[:, :half], v[:, half:])
        other = jnp.where(low, v[:, half:], v[:, :half])
        for i, (at, w) in enumerate(offsets(widths)):
            outs[2 * i][rows, :] = mine[:, at : at + w].astype(BF)
            outs[2 * i + 1][rows, :w] = other[:, at : at + w].astype(BF)
        return 0

    lax.fori_loop(0, up_ref.shape[0] // TM, body, 0)


def pack_up(widths, place, grad_out):
    t = grad_out.shape[0]
    return pl.pallas_call(
        functools.partial(pack_up_kernel, widths),
        in_specs=[SMEM_SPEC, VMEM_SPEC],
        out_shape=[jax.ShapeDtypeStruct((t, w), BF) for v in widths for w in (v, ceil_to(v, LANES))],
        compiler_params=params(),
        cost_estimate=TINY,
        name="pack_up",
    )(place, grad_out)


def gates_kernel(plan, place, *refs):
    n, m, dw, dl, t, c, up_at, wrel, xrel = plan
    n_w, n_x = len(wrel) or 1, len(xrel) or 1
    w_in, refs = refs[:n_w], refs[n_w:]
    x_in, refs = refs[:n_x], refs[n_x:]
    if not xrel:
        halo_in, refs = refs[0], refs[1:]
    bias_ref, up0, up1 = refs[:3]
    refs = refs[3:]
    if not xrel:
        keep_w, refs = refs[0], refs[1:]
    g_ref, seg_ref, tot_ref, refs = refs[0], refs[1], refs[2], refs[3:]
    if xrel:
        x_out, halo_out, keep_w, refs = refs[0], refs[1], refs[2], refs[3:]
    w_out, refs = refs[0], refs[1:]
    xs, halo, ws, p_s, d_s, s_s, q_s, seg_s, xsem, hsem, wsem, osem = refs
    pad = ws.shape[1]
    width = ws.shape[2]
    wide = n // m
    h, l, p, a, b = (place[i] for i in range(5))
    heads = n // 4
    copies = []
    if wrel:
        for i, (kh, d_p) in enumerate(wrel):
            for d_l in range(2):
                block = (lax.rem(h - kh + heads, heads) * 2 + (l ^ d_l)) * 2 + (p ^ d_p)
                at = pl.multiple_of(lax.rem(block, wide) * dw, 16)
                copies.append(
                    pltpu.make_async_copy(
                        w_in[i].at[d_l], ws.at[block // wide, pl.ds(at, dw), :], wsem.at[2 * i + d_l]
                    )
                )
        if pad > dl:
            for g in range(m):
                ws[g, dl:, :] = jnp.zeros((pad - dl, width), BF)
    else:
        copies.append(pltpu.make_async_copy(w_in[0], ws, wsem.at[0]))
    xcopies = [[], []]
    if xrel:
        for i, (slot, d_a, d_b) in enumerate(xrel):
            at = pl.multiple_of(((a ^ d_a) * 2 + (b ^ d_b)) * pad, LANES)
            xcopies[slot].append(
                pltpu.make_async_copy(
                    x_in[i].at[pl.ds(0, t)], xs.at[pl.ds(slot * t, t), pl.ds(at, pad)], xsem.at[i]
                )
            )
            copies.append(
                pltpu.make_async_copy(
                    x_in[i].at[pl.ds(t, EDGE)], halo.at[pl.ds(slot * EDGE, EDGE), pl.ds(at, pad)], hsem.at[i]
                )
            )
    else:
        for slot in range(2):
            rows = pl.ds(slot * t, t)
            xcopies[slot].append(pltpu.make_async_copy(x_in[0].at[rows], xs.at[rows], xsem.at[slot]))
        copies.append(pltpu.make_async_copy(halo_in, halo, hsem.at[0]))
    for copy in copies + xcopies[0] + xcopies[1]:
        copy.start()
    for copy in copies:
        copy.wait()
    outs = []
    for g in range(m):
        outs.append(pltpu.make_async_copy(ws.at[g], w_out.at[(a * 2 + b) ^ g], osem.at[g]))
    for copy in outs:
        copy.start()
    lanes = cuts(c)
    weights = ws[...].reshape(m * pad, width)
    if xrel:
        out = pltpu.make_async_copy(halo, halo_out, osem.at[m + 2])
        out.start()
        outs.append(out)
    edge = jnp.dot(halo[...], weights, preferred_element_type=F32)
    for slot, up_ref in enumerate((up0, up1)):
        for copy in xcopies[slot]:
            copy.wait()
        if xrel:
            rows = pl.ds(slot * t, t)
            out = pltpu.make_async_copy(xs.at[rows], x_out.at[rows], osem.at[m + slot])
            out.start()
            outs.append(out)
        p_s[7:8, :] = edge[slot * EDGE : slot * EDGE + 1, :]

        def tile(i, _, slot=slot, up_ref=up_ref):
            base = pl.multiple_of(i * ROWS, ROWS)
            x = xs[pl.ds(pl.multiple_of(slot * t + base, ROWS), ROWS), :]
            p_s[8:, :] = jnp.dot(x, ws[...].reshape(m * pad, width), preferred_element_type=F32)
            for r in range(ROWS // TM):
                rows = pl.ds(pl.multiple_of(base + r * TM, TM), TM)
                full = pl.ds(pl.multiple_of(slot * t + base + r * TM, TM), TM)
                if xrel:
                    flags = xs[full, dl:pad].astype(F32)
                    keep = jnp.concatenate([flags] * (LANES // (pad - dl)), axis=1)
                    keep_w[full, :] = keep
                else:
                    keep = keep_w[full, :]
                for k_l, lo, w in lanes:
                    g = []
                    for k in range(3):
                        now = p_s[8 + r * TM : 8 + (r + 1) * TM, k * c + lo : k * c + lo + w]
                        before = p_s[7 + r * TM : 7 + (r + 1) * TM, (3 + k) * c + lo : (3 + k) * c + lo + w]
                        v = now + keep[:, :w] * before + bias_ref[k : k + 1, lo : lo + w]
                        g_ref[k, full, lo : lo + w] = v
                        g.append(v)
                    f, intake = both(g[1])
                    o, _ = both(g[2])
                    d = keep[:, :w] * f
                    d_s[slot, k_l, rows, :w] = d
                    s_s[slot, k_l, rows, :w] = intake * jnp.tanh(g[0])
                    q_s[slot, k_l, rows, :w] = d * (load_up(up_ref, rows, slot * up_at + lo, w) * o)
            p_s[7:8, :] = p_s[ROWS + 7 : ROWS + 8, :]
            return 0

        lax.fori_loop(0, t // ROWS, tile, 0)
    span = t // SEGS
    chains = [(slot, k_l) for slot in range(2) for k_l, _, _ in lanes]
    one, zero = jnp.ones((SEGS, LANES), F32), jnp.zeros((SEGS, LANES), F32)

    def step(j, carry):
        at, back = pl.ds(j, SEGS, stride=span), pl.ds(span - 1 - j, SEGS, stride=span)
        new = []
        for (slot, k_l), (pa, ps, pr) in zip(chains, carry):
            d = d_s[slot, k_l, at, :]
            new.append(
                (
                    pa * d,
                    d * ps + s_s[slot, k_l, at, :],
                    d_s[slot, k_l, back, :] * pr + q_s[slot, k_l, back, :],
                )
            )
        return tuple(new)

    res = lax.fori_loop(0, span, step, tuple((one, zero, zero) for _ in chains), unroll=4)
    for (slot, k_l), triple in zip(chains, res):
        _, lo, w = lanes[k_l]
        for k in range(3):
            seg_s[k] = triple[k]
            seg_ref[slot, k, :, lo : lo + w] = triple[k][:, :w]
        pa, ps, pr = one[:1], zero[:1], zero[:1]
        for k in range(SEGS):
            d = seg_s[0, k : k + 1, :]
            ps = d * ps + seg_s[1, k : k + 1, :]
            pa = pa * d
            r = SEGS - 1 - k
            pr = seg_s[0, r : r + 1, :] * pr + seg_s[2, r : r + 1, :]
        for k, v in enumerate((pa, ps, pr)):
            tot_ref[slot, k : k + 1, lo : lo + w] = v[:, :w]
    for copy in outs:
        copy.wait()


def after(v, *needs):
    return lax.optimization_barrier((v, *needs))[0]


def gates_and_totals(dims, up_at, place, w, wrel, x, xrel, bias, ups, keep_w=None):
    n, m, dw, dl, t, c = dims
    pad = ceil_to(dl, LANES)
    lt = len(cuts(c))
    width = 6 * c
    plan = (n, m, dw, dl, t, c, up_at, tuple(wrel), tuple(xrel))
    shape = jax.ShapeDtypeStruct
    outs = [shape((3, 2 * t, c), F32), shape((2, 3, SEGS, c), F32), shape((2, 3, c), F32)]
    specs = [VMEM_SPEC] * 3
    if xrel:
        outs += [shape((2 * t, m * pad), BF), shape((2 * EDGE, m * pad), BF), shape((2 * t, LANES), F32)]
        specs += [ANY_SPEC, ANY_SPEC, VMEM_SPEC]
    outs.append(shape((m, pad, width), BF))
    specs.append(ANY_SPEC)
    return pl.pallas_call(
        functools.partial(gates_kernel, plan),
        in_specs=[SMEM_SPEC] + [ANY_SPEC] * (len(w) + len(x)) + [VMEM_SPEC] * (3 if xrel else 4),
        out_specs=specs,
        out_shape=outs,
        scratch_shapes=[
            pltpu.VMEM((2 * t, m * pad), BF),
            pltpu.VMEM((2 * EDGE, m * pad), BF),
            pltpu.VMEM((m, pad, width), BF),
            pltpu.VMEM((ROWS + 8, width), F32),
            pltpu.VMEM((2, lt, t, LANES), F32),
            pltpu.VMEM((2, lt, t, LANES), F32),
            pltpu.VMEM((2, lt, t, LANES), F32),
            pltpu.VMEM((3, SEGS, LANES), F32),
            pltpu.SemaphoreType.DMA((max(2, len(x)),)),
            pltpu.SemaphoreType.DMA((max(1, len(x)),)),
            pltpu.SemaphoreType.DMA((2 * len(w),)),
            pltpu.SemaphoreType.DMA((m + 3,)),
        ],
        compiler_params=params(),
        cost_estimate=TINY,
        name="gates_and_totals",
    )(place, *w, *x, bias, *ups, *([] if xrel else [keep_w]))


def finish_kernel(n, up_at, place, g_ref, up0, up1, keep_ref, seg_ref, all_ref, h0, h1, gg_ref, gf_ref, gp_ref, gb_ref, d_s, s_s, q_s, p_s, c_s):
    t, c = up0.shape
    span = t // SEGS
    lanes = cuts(c)
    heads = n // 4
    hh, ll, pp = place[0], place[1], place[2]
    ups, hids = (up0, up1), (h0, h1)
    for slot in range(2):

        def act(r, _, slot=slot):
            rows = pl.ds(pl.multiple_of(r * TM, TM), TM)
            full = pl.ds(pl.multiple_of(slot * t + r * TM, TM), TM)
            for k_l, lo, w in lanes:
                ch = slice(lo, lo + w)
                f, i = both(g_ref[1, full, ch])
                o, _ = both(g_ref[2, full, ch])
                d_s[slot, k_l, rows, :w] = keep_ref[full, :w] * f
                s_s[slot, k_l, rows, :w] = i * jnp.tanh(g_ref[0, full, ch])
                q_s[slot, k_l, rows, :w] = load_up(ups[slot], rows, slot * up_at + lo, w) * o
            return 0

        lax.fori_loop(0, t // TM, act, 0)
    zrow = jnp.zeros((1, c), F32)
    mine = [(hh * 2 + (ll ^ slot)) * 2 + pp for slot in range(2)]

    def total(block, k):
        p_b, l_b, h_b = block % 2, block // 2 % 2, block // 4
        member = lax.rem(hh - h_b + heads, heads) * 2 + (pp ^ p_b)
        return all_ref[member, ll ^ l_b, k : k + 1, :]

    h, r = zrow, zrow
    h_in, r_in = [zrow, zrow], [zrow, zrow]
    for k in range(n):
        b = n - 1 - k
        h_in = [jnp.where(mine[s] == k, h, h_in[s]) for s in range(2)]
        r_in = [jnp.where(mine[s] == b, r, r_in[s]) for s in range(2)]
        h = total(k, 0) * h + total(k, 1)
        r = total(b, 0) * r + total(b, 2)
    for slot in range(2):
        h, r = h_in[slot], r_in[slot]
        for k in range(SEGS):
            b = SEGS - 1 - k
            for k_l, lo, w in lanes:
                c_s[0, slot, k_l, k : k + 1, :w] = h[:, lo : lo + w]
                c_s[1, slot, k_l, b : b + 1, :w] = r[:, lo : lo + w]
            h = seg_ref[slot, 0, k : k + 1, :] * h + seg_ref[slot, 1, k : k + 1, :]
            r = seg_ref[slot, 0, b : b + 1, :] * r + seg_ref[slot, 2, b : b + 1, :]
    chains = [(slot, k_l) for slot in range(2) for k_l, _, _ in lanes]

    def step(j, carry):
        at, back = pl.ds(j, SEGS, stride=span), pl.ds(span - 1 - j, SEGS, stride=span)
        new = []
        for (slot, k_l), (h, r) in zip(chains, carry):
            dh = d_s[slot, k_l, at, :] * h
            h = dh + s_s[slot, k_l, at, :]
            p_s[slot, k_l, at, :] = dh
            s_s[slot, k_l, at, :] = h
            g = q_s[slot, k_l, back, :] + r
            q_s[slot, k_l, back, :] = g
            new.append((h, d_s[slot, k_l, back, :] * g))
        return tuple(new)

    lax.fori_loop(0, span, step, tuple((c_s[0, s, k_l], c_s[1, s, k_l]) for s, k_l in chains), unroll=4)
    sums = [jnp.zeros((8, w), F32) for _, _, w in lanes for _ in range(3)]
    top = lax.broadcasted_iota(jnp.int32, (EDGE, LANES), 0) == 0
    gp_ref[...] = jnp.zeros(gp_ref.shape, BF)
    for slot in range(2):

        def out(i, state, slot=slot):
            acc, nxt = state
            r = t // TM - 1 - i
            rows = pl.ds(pl.multiple_of(r * TM, TM), TM)
            full = pl.ds(pl.multiple_of(slot * t + r * TM, TM), TM)
            last = lax.broadcasted_iota(jnp.int32, (TM, LANES), 0) == TM - 1
            new, first = [], []
            for k_l, lo, w in lanes:
                ch = slice(lo, lo + w)
                f, intake = both(g_ref[1, full, ch])
                o, cl = both(g_ref[2, full, ch])
                z = jnp.tanh(g_ref[0, full, ch])
                keep = keep_ref[full, :w]
                gs = q_s[slot, k_l, rows, :w]
                oh = o * s_s[slot, k_l, rows, :w]
                hids[slot][rows, ch] = oh.astype(BF)
                gi = gs * intake
                grads = (
                    gi * (1.0 - z * z),
                    gi * (p_s[slot, k_l, rows, :w] - f * z),
                    load_up(ups[slot], rows, slot * up_at + lo, w) * oh * cl,
                )
                for k, v in enumerate(grads):
                    gg_ref[full, k * c + lo : k * c + lo + w] = v.astype(BF)
                    kept = keep * v
                    moved = jnp.where(last[:, :w], nxt[len(new)], pltpu.roll(kept, TM - 1, 0))
                    gg_ref[full, (3 + k) * c + lo : (3 + k) * c + lo + w] = moved.astype(BF)
                    first.append(kept[:1])
                    new.append(acc[len(new)] + jnp.sum(v.reshape(TM // 8, 8, w), axis=0))
            return tuple(new), tuple(first)

        zeros = tuple(jnp.zeros((1, w), F32) for _, _, w in lanes for _ in range(3))
        sums, firsts = lax.fori_loop(0, t // TM, out, (tuple(sums), zeros))
        for k_l, lo, w in lanes:
            for k in range(3):
                gf_ref[slot : slot + 1, k * c + lo : k * c + lo + w] = firsts[3 * k_l + k]
                gp_ref[slot * EDGE : slot * EDGE + EDGE, (3 + k) * c + lo : (3 + k) * c + lo + w] = jnp.where(
                    top[:, :w], firsts[3 * k_l + k], 0.0
                ).astype(BF)
    for k_l, lo, w in lanes:
        for k in range(3):
            gb_ref[0:1, k * c + lo : k * c + lo + w] = jnp.sum(sums[3 * k_l + k], axis=0, keepdims=True)


def finish(n, up_at, place, gates, ups, keep_w, seg, every):
    t, c = ups[0].shape
    lt = len(cuts(c))
    shape = jax.ShapeDtypeStruct
    return pl.pallas_call(
        functools.partial(finish_kernel, n, up_at),
        in_specs=[SMEM_SPEC] + [VMEM_SPEC] * 6,
        out_shape=[
            shape((t, c), BF),
            shape((t, c), BF),
            shape((2 * t, 6 * c), BF),
            shape((2, 3 * c), F32),
            shape((2 * EDGE, 6 * c), BF),
            shape((1, 3 * c), F32),
        ],
        scratch_shapes=[pltpu.VMEM((2, lt, t, LANES), F32)] * 4 + [pltpu.VMEM((2, 2, lt, SEGS, LANES), F32)],
        compiler_params=params(),
        cost_estimate=TINY,
        name="finish",
    )(place, gates, *ups, keep_w, seg, every)


def wgrad_kernel(dw, place, x_ref, halo_ref, gg_ref, gp_ref, here_ref, away_ref, acc):
    over_tokens = (((0,), (0,)), ((), ()))
    v = lax.dot_general(x_ref[...], gg_ref[...], over_tokens, preferred_element_type=F32)
    acc[...] = v + lax.dot_general(halo_ref[...], gp_ref[...], over_tokens, preferred_element_type=F32)
    p = place[2]
    here_ref[0] = acc[pl.ds(pl.multiple_of(p * dw, 16), dw), :].astype(BF)
    away_ref[0] = acc[pl.ds(pl.multiple_of((1 - p) * dw, 16), dw), :].astype(BF)


def weight_grads(heads, kh, dw, pad, place, x_all, halo, gg, gp):
    width = gg.shape[1]

    def lanes(i, at):
        return (0, lax.rem(at[0] + kh, heads) * 2 + (at[1] ^ (1 - i)))

    whole = lambda i, at: (0, 0)
    return pl.pallas_call(
        functools.partial(wgrad_kernel, dw),
        grid_spec=pltpu.PrefetchScalarGridSpec(
            num_scalar_prefetch=1,
            grid=(2,),
            in_specs=[
                pl.BlockSpec((x_all.shape[0], pad), lanes),
                pl.BlockSpec((halo.shape[0], pad), lanes),
                pl.BlockSpec(gg.shape, whole),
                pl.BlockSpec(gp.shape, whole),
            ],
            out_specs=[pl.BlockSpec((1, dw, width), lambda i, at: (i, 0, 0))] * 2,
            scratch_shapes=[pltpu.VMEM((pad, width), F32)],
        ),
        out_shape=[jax.ShapeDtypeStruct((2, dw, width), BF)] * 2,
        compiler_params=params(),
        cost_estimate=TINY,
        name="weight_grads",
    )(place, x_all, halo, gg, gp)


def xgrad_kernel(slot, place, *refs):
    count = (len(refs) - 3) // 4
    gg_in, nx, w_in = refs[:count], refs[count : 2 * count], refs[2 * count : 3 * count]
    send_ref, keep_ref = refs[3 * count : 3 * count + 2]
    gg_s, sem = refs[3 * count + 2 : 4 * count + 2], refs[4 * count + 2]
    i = pl.program_id(0)
    t = gg_s[0].shape[0]

    @pl.when(i == 0)
    def _():
        copies = [
            pltpu.make_async_copy(gg_in[k].at[pl.ds(slot * t, t)], gg_s[k], sem.at[k]) for k in range(count)
        ]
        for copy in copies:
            copy.start()
        for k, copy in enumerate(copies):
            copy.wait()
            c3 = nx[k].shape[1]
            old = gg_s[k][t - EDGE :, c3:].astype(F32)
            last = lax.broadcasted_iota(jnp.int32, (EDGE, c3), 0) == EDGE - 1
            gg_s[k][t - EDGE :, c3:] = jnp.where(last, nx[k][slot : slot + 1, :], old).astype(BF)

    v = 0.0
    for k in range(count):
        v = v + lax.dot_general(gg_s[k][...], w_in[k][0], (((1,), (1,)), ((), ())), preferred_element_type=F32)

    @pl.when(i < 2)
    def _():
        send_ref[0] = v.astype(BF)

    @pl.when(i >= 2)
    def _():
        keep_ref[0] = v.astype(BF)


def input_grads(slot, place, ggs, nexts, ws):
    count = len(ggs)
    t = ggs[0].shape[0] // 2
    m, pad, _ = ws[0].shape
    order = lambda i: jnp.where(i < 2, 2 * i + 1, 2 * i - 4)
    return pl.pallas_call(
        functools.partial(xgrad_kernel, slot),
        grid_spec=pltpu.PrefetchScalarGridSpec(
            num_scalar_prefetch=1,
            grid=(m,),
            in_specs=[ANY_SPEC] * count
            + [pl.BlockSpec(v.shape, lambda i, at: (0, 0)) for v in nexts]
            + [pl.BlockSpec((1, pad, w.shape[2]), lambda i, at: (order(i), 0, 0)) for w in ws],
            out_specs=[
                pl.BlockSpec((1, t, pad), lambda i, at: (jnp.minimum(i, 1), 0, 0)),
                pl.BlockSpec((1, t, pad), lambda i, at: (jnp.maximum(i - 2, 0), 0, 0)),
            ],
            scratch_shapes=[pltpu.VMEM((t, gg.shape[1]), BF) for gg in ggs]
            + [pltpu.SemaphoreType.DMA((count,))],
        ),
        out_shape=[jax.ShapeDtypeStruct((2, t, pad), BF)] * 2,
        compiler_params=params(),
        cost_estimate=TINY,
        name="input_grads",
    )(place, *ggs, *nexts, *ws)


def join_kernel(*refs):
    *terms, out = refs
    v = terms[0][...].astype(F32)
    for ref in terms[1:]:
        v = v + ref[...].astype(F32)
    out[...] = v.astype(BF)


def join(terms, urgency):
    arrays = [v for v, _ in terms]
    shape = arrays[0].shape[-2:]
    steps = 2 if shape[0] % 32 == 0 else 1
    blocks = shape[0] // steps

    def spec(v, at):
        if at is None:
            return pl.BlockSpec((blocks, shape[1]), lambda i: (i, 0))
        return pl.BlockSpec((None, blocks, shape[1]), lambda i, at=at: (at, i, 0))

    return pl.pallas_call(
        join_kernel,
        grid=(steps,),
        in_specs=[spec(v, at) for v, at in terms],
        out_specs=pl.BlockSpec((blocks, shape[1]), lambda i: (i, 0)),
        out_shape=jax.ShapeDtypeStruct(shape, BF),
        compiler_params=params(),
        cost_estimate=pl.CostEstimate(flops=0, bytes_accessed=urgency * 3690000, transcendentals=0),
        name="join",
    )(*arrays)


def unpack_w_kernel(widths, place, *refs):
    count = len(widths)
    outs = refs[2 * count :]
    low = place[1] == 0
    for tap in range(2):
        for k in range(3):
            mine, other = [], []
            for i, w in enumerate(widths):
                lo = (tap * 3 + k) * w
                mine.append(refs[2 * i][:, lo : lo + w].astype(F32))
                other.append(refs[2 * i + 1][:, lo : lo + w].astype(F32))
            mine, other = jnp.concatenate(mine, axis=1), jnp.concatenate(other, axis=1)
            outs[tap][k] = jnp.concatenate([jnp.where(low, mine, other), jnp.where(low, other, mine)], axis=1)


def unpack_weights(widths, place, pairs):
    rows = pairs[0].shape[0]
    shape = jax.ShapeDtypeStruct((3, rows, 2 * sum(widths)), F32)
    return pl.pallas_call(
        functools.partial(unpack_w_kernel, widths),
        in_specs=[SMEM_SPEC] + [VMEM_SPEC] * len(pairs),
        out_shape=[shape, shape],
        compiler_params=params(),
        cost_estimate=TINY,
        name="unpack_weights",
    )(place, *pairs)


def unpack_h_kernel(widths, place, *refs):
    out_ref = refs[-1]
    low = place[1] == 0

    def body(r, _):
        rows = pl.ds(pl.multiple_of(r * TM, TM), TM)
        mine = jnp.concatenate([refs[i][rows, :].astype(F32) for i in range(len(widths))], axis=1)
        other = refs[len(widths)][rows, :].astype(F32)
        both_halves = jnp.concatenate([jnp.where(low, mine, other), jnp.where(low, other, mine)], axis=1)
        out_ref[rows, :] = both_halves.astype(BF)
        return 0

    lax.fori_loop(0, out_ref.shape[0] // TM, body, 0)


def unpack_hidden(widths, place, mine, other):
    t = other.shape[0]
    return pl.pallas_call(
        functools.partial(unpack_h_kernel, widths),
        in_specs=[SMEM_SPEC] + [VMEM_SPEC] * (len(mine) + 1),
        out_shape=jax.ShapeDtypeStruct((t, 2 * sum(widths)), BF),
        compiler_params=params(),
        cost_estimate=TINY,
        name="unpack_hidden",
    )(place, *mine, other)


def on_device(layer_input, keep, w_now, w_prev, bias, grad_out):
    n, m = lax.axis_size("seq"), lax.axis_size("gate")
    heads = n // 4
    s, g = lax.axis_index("seq"), lax.axis_index("gate")
    h, l, p, a, b = s // 4, s // 2 % 2, s % 2, g // 2, g % 2
    place = jnp.stack([h, l, p, a, b]).astype(jnp.int32)
    t, dl = layer_input.shape
    dw = w_now.shape[1]
    half = dl // 2
    pad = ceil_to(dl, LANES)
    widths = tuple(w for w in WIDTHS) if sum(WIDTHS) == half else (half,)
    low = l == 0

    def seq_to(v, kh, d_l, d_p):
        route = []
        for i in range(n):
            i_h, i_l, i_p = i // 4, i // 2 % 2, i % 2
            route.append((i, ((i_h + kh) % heads * 2 + (i_l ^ d_l)) * 2 + (i_p ^ d_p)))
        return lax.ppermute(v, "seq", route)

    def gate_to(v, d_a, d_b):
        return lax.ppermute(v, "gate", [(i, i ^ (d_a * 2 + d_b)) for i in range(m)])

    group = [(kh, d_p) for kh in range(heads) for d_p in range(2)]

    packed = pack_weights(widths, 0, place, w_now, w_prev)
    behind = lax.ppermute(layer_input[-1:], "seq", [(i, i + 1) for i in range(n - 1)])
    flags = jnp.broadcast_to(jnp.pad(keep, (0, EDGE)).astype(BF)[:, None], (t + EDGE, pad - dl))
    rows = jnp.concatenate([layer_input, jnp.pad(behind, ((0, EDGE - 1), (0, 0)))], axis=0)
    x0 = after(jnp.concatenate([rows, flags], axis=1), packed[0])
    def share_w(pair, *needs):
        got = {(0, 0): pair, (0, 1): seq_to(pair, 0, 0, 1)}
        for kh in range(1, heads):
            got[kh, 0] = seq_to(after(pair, *needs) if needs else pair, kh, 0, 0)
        return got

    def finish_share(got, *needs):
        for kh in range(1, heads):
            got[kh, 1] = seq_to(after(got[kh, 0], *needs) if needs else got[kh, 0], 0, 0, 1)

    def weights_in(got, c):
        if dw % 16 == 0:
            return [got[r] for r in got], list(got)
        stacked = jnp.stack([got[kh, d_p][d_l] for kh in range(heads) for d_l in range(2) for d_p in range(2)])
        blocks = jnp.arange(n)
        rel = (((h - blocks // 4) % heads) * 2 + (l ^ (blocks // 2 % 2))) * 2 + (p ^ (blocks % 2))
        whole = jnp.take(stacked, rel, axis=0).reshape(m, dl, 6 * c)
        return [jnp.pad(whole, ((0, 0), (0, pad - dl), (0, 0)))], []

    half_bias = jnp.where(low, bias[:, :half], bias[:, half:])
    count = len(widths)
    spans = list(offsets(widths))
    near = seq_to(packed[1], 0, 1, 0)
    got = [share_w(jnp.stack([packed[0], near]))]
    y0 = gate_to(x0, 1, 0)
    x1 = seq_to(after(x0, near), 0, 1, 0)
    first_p = got[0][0, 1]
    c0, cy0 = gate_to(after(x0, y0, first_p), 0, 1), gate_to(after(y0, first_p), 0, 1)
    up_packed = pack_up(widths, place, after(grad_out, x0))
    ups = [[up_packed[0], seq_to(after(up_packed[1], first_p), 0, 1, 0)]]
    x1_here = after(x1, c0, cy0)
    y1, c1 = gate_to(x1_here, 1, 0), gate_to(x1_here, 0, 1)
    finish_share(got[0], c1)
    for i in range(1, count):
        packed = pack_weights(widths, i, place, after(w_now, near), w_prev)
        near = seq_to(after(packed[1], c0, cy0, x1), 0, 1, 0)
        got.append(share_w(jnp.stack([packed[0], near]), c1, *[got[i - 1][kh, 0] for kh in range(1, heads)]))
        ups.append([up_packed[2 * i], seq_to(after(up_packed[2 * i + 1], near), 0, 1, 0)])
    cy1 = gate_to(after(y1, ups[0][1]), 0, 1)
    xs = {(0, 0, 0): x0, (0, 1, 0): y0, (0, 0, 1): c0, (0, 1, 1): cy0}
    xs |= {(1, 0, 0): x1, (1, 1, 0): y1, (1, 0, 1): c1, (1, 1, 1): cy1}
    hidden_mine, hidden_other, grads, wide_w, g_first, g_bias, w_pairs = [], [], [], [], [], [], []

    def spread_totals(tot):
        return jnp.stack([tot if r == (0, 0) else seq_to(tot, r[0], 0, r[1]) for r in group])

    def weight_parts(gg, gp, *needs):
        if dw % 16 == 0 and n == 2 * m:
            parts = [
                (kh, *weight_grads(heads, kh, dw, pad, place, x_all, halo, gg, gp)) for kh in range(1, heads)
            ]
            gp = after(gp, parts[-1][1], *needs)
            return parts + [(0, *weight_grads(heads, 0, dw, pad, place, x_all, halo, gg, gp))]
        dots = jnp.einsum("td,tn->dn", x_all, gg, preferred_element_type=F32)
        dots = dots + jnp.einsum("td,tn->dn", halo, gp, preferred_element_type=F32)
        v = dots.astype(BF).reshape(m, pad, -1)[:, :dl].reshape(heads, 2, 2, dw, gg.shape[1])
        away = jnp.where(p == 0, v[:, :, 1], v[:, :, 0])
        here = jnp.where(p == 0, v[:, :, 0], v[:, :, 1])

        def block(v, kh):
            row = lax.dynamic_index_in_dim(v, (h + kh) % heads, 0, keepdims=False)
            return jnp.where(low, row[::-1], row)

        return [(kh, block(here, kh), block(away, kh)) for kh in list(range(1, heads)) + [0]]

    def over_p(parts, *needs):
        came = []
        for _, _, away in parts:
            came.append(after(seq_to(away, 0, 0, 1), *came[-1:], *needs))
        return [here.astype(F32) + v.astype(F32) for (_, here, _), v in zip(parts, came)]

    def over_h(parts, sums, *needs):
        total = sums[-1]
        for (kh, _, _), v in zip(parts[:-1], sums[:-1]):
            total = total + after(seq_to(v.astype(BF), kh, 0, 0), *needs).astype(F32)
        return total.astype(BF)

    waiting = None
    for i, (at, c) in enumerate(spans):
        dims = (n, m, dw, dl, t, c)
        bias_i = half_bias[:, at : at + c]
        if i > 0:
            finish_share(got[i], every)
        w_in, wrel = weights_in(got[i], c)
        if i == 0:
            xrel = list(xs)
            gates, seg, tot, x_all, halo, keep_w, w_rel = gates_and_totals(
                dims, 0, place, w_in, wrel, [xs[r] for r in xrel], xrel, bias_i, ups[i]
            )
        else:
            w_in[0] = after(w_in[0], *[v[2] for v in waiting])
            gates, seg, tot, w_rel = gates_and_totals(
                dims, 0, place, w_in, wrel, [x_all, halo], [], bias_i, ups[i], keep_w
            )
        every = spread_totals(tot)
        wide_w.append(w_rel)
        if i > 0:
            sums = over_p(waiting, tot)
            h_sums = [after(v, every) for v in sums]
            every = after(every, *sums)
        h0, h1, gg, gf, gp, gb = finish(n, 0, place, gates, ups[i], keep_w, seg, every)
        hidden_mine.append(h0)
        hidden_other.append(h1)
        g_first.append(gf)
        g_bias.append(gb)
        needs = []
        if i == count - 1:
            parts = jnp.concatenate([jnp.concatenate(g_first, axis=1), jnp.concatenate(g_bias, axis=1)], axis=0)
            came = [parts if r == (0, 0) else seq_to(parts, r[0], 0, r[1]) for r in group]
            hidden_came = seq_to(after(jnp.concatenate(hidden_other, axis=1), parts), 0, 1, 0)
        if i > 0:
            total = over_h(waiting, h_sums, gg)
            needs.append(total)
        if i == count - 1:
            came = [after(v, *needs) for v in came]
            around = jnp.stack(came)
            needs += [around, hidden_came]
        waiting_next = weight_parts(gg, gp, *needs)
        if i > 0:
            w_pairs += [total[1], seq_to(after(total[0], waiting_next[-1][1]), 0, 1, 0)]
        waiting = waiting_next
        grads.append(gg)
    full_bias = jnp.sum(around[:, 2], axis=0)
    nexts = []
    for slot in range(2):
        block_id = (h * 2 + (l ^ slot)) * 2 + p + 1
        n_h, n_l, n_p = block_id // 4, block_id // 2 % 2, block_id % 2
        member = ((h - n_h) % heads) * 2 + (p ^ n_p)
        row = lax.dynamic_index_in_dim(around, member, 0, keepdims=False)
        row = lax.dynamic_index_in_dim(row, l ^ n_l, 0, keepdims=False)
        nexts.append(jnp.where(block_id < n, row, jnp.zeros_like(row)))
    nexts = jnp.stack(nexts)
    nexts = [nexts[:, 3 * at : 3 * (at + c)] for at, c in spans]
    bias_half = []
    at = 0
    for c in widths:
        bias_half.append(full_bias[at : at + 3 * c].reshape(3, c))
        at += 3 * c
    bias_half = jnp.concatenate(bias_half, axis=1)
    bias_other = seq_to(bias_half, 0, 1, 0)
    nexts[0] = after(nexts[0], bias_other, *[v[2] for v in waiting])
    sent1, kept1 = input_grads(1, place, grads, nexts, wide_w)

    p_came = []
    for v in waiting:
        p_came.append(after(seq_to(v[2], 0, 0, 1), *p_came[-1:]))
    c_came1 = gate_to(after(sent1, p_came[0]), 0, 1)
    nexts[0] = after(nexts[0], c_came1, *w_pairs)
    h_came = []
    for k, (kh, here, _) in enumerate(waiting[:-1]):
        both_l = jnp.stack([join([(here, d), (p_came[k], d)], URGENT) for d in range(2)])
        h_came.append(seq_to(both_l, kh, 0, 0))
    y_came1 = gate_to(join([(kept1, 1), (c_came1, 1)], URGENT), 1, 0)
    sent0, kept0 = input_grads(0, place, grads, nexts, wide_w)
    c_came0 = gate_to(sent0, 0, 1)
    l_came = seq_to(join([(kept1, 0), (c_came1, 0), (y_came1, None)], URGENT), 0, 1, 0)
    total = [
        join([(waiting[-1][1], d), (p_came[-1], d)] + [(v, d) for v in h_came], LATER) for d in range(2)
    ]
    w_pairs += [total[1], seq_to(total[0], 0, 1, 0)]
    y_came0 = gate_to(join([(kept0, 1), (c_came0, 1)], 1), 1, 0)
    grad_x = kept0[0].astype(F32) + c_came0[0].astype(F32) + y_came0.astype(F32) + l_came.astype(F32)
    grad_x = grad_x[:, :dl].astype(BF)

    grad_bias = jnp.concatenate(
        [jnp.where(low, bias_half, bias_other), jnp.where(low, bias_other, bias_half)], axis=1
    )
    hidden = unpack_hidden(widths, place, hidden_mine, hidden_came)
    grad_now, grad_prev = unpack_weights(widths, place, w_pairs)
    return hidden, grad_x, grad_now, grad_prev, grad_bias


def solution(mesh):
    tokens, matrix = P("seq", "gate"), P(None, "seq", "gate")
    return jax.shard_map(
        on_device,
        mesh=mesh,
        in_specs=(tokens, P("seq"), matrix, matrix, P(None, "gate"), tokens),
        out_specs=(tokens, tokens, matrix, matrix, P(None, "gate")),
        check_vma=False,
    )
```

```python
import functools

import jax
import jax.numpy as jnp
from jax import lax
from jax.experimental import pallas as pl
from jax.experimental.pallas import tpu as pltpu
from jax.sharding import PartitionSpec as P

F32 = jnp.float32
BF = jnp.bfloat16
SEGS = 8
LANES = 128
TM = 64
ROWS = 256
EDGE = 16
GAP = 8
VMEM = 62 << 20
WIDTHS = (128, 160)


def ceil_to(value, unit):
    return -(-value // unit) * unit


def both(g):
    e = jnp.exp(-jnp.abs(g))
    r = 1.0 / (1.0 + e)
    er = e * r
    pos = g >= 0
    return jnp.where(pos, r, er), jnp.where(pos, er, r)


def group(k, lo, w, count=6):
    return slice(count * lo + k * w, count * lo + (k + 1) * w)


def load_up(ref, rows, lo, w):
    return ref[rows, lo : lo + w].astype(F32)


def spread(row, span):
    return pl.ds(pl.multiple_of(row + row // span * GAP, 8), TM)


def cuts(c):
    return [(i, i * LANES, min(LANES, c - i * LANES)) for i in range(-(-c // LANES))]


def params():
    return pltpu.CompilerParams(vmem_limit_bytes=VMEM)


URGENT, LATER = 100, 50
TINY = pl.CostEstimate(flops=1 << 10, bytes_accessed=1 << 10, transcendentals=0)
SMEM_SPEC = pl.BlockSpec(memory_space=pltpu.SMEM)
VMEM_SPEC = pl.BlockSpec(memory_space=pltpu.VMEM)
ANY_SPEC = pl.BlockSpec(memory_space=pl.ANY)


def offsets(widths):
    at = 0
    for w in widths:
        yield at, w
        at += w


def pack_w_kernel(widths, share, place, now_ref, prev_ref, *outs):
    half = now_ref.shape[2] // 2
    low = place[1] == 0
    for tap, ref in enumerate((now_ref, prev_ref)):
        for k in range(3):
            v = ref[k].astype(F32)
            mine = jnp.where(low, v[:, :half], v[:, half:])
            other = jnp.where(low, v[:, half:], v[:, :half])
            at, c = list(offsets(widths))[share]
            for _, lo, w in cuts(c):
                to = group(tap * 3 + k, lo, w)
                outs[0][:, to] = mine[:, at + lo : at + lo + w].astype(BF)
                outs[1][:, to] = other[:, at + lo : at + lo + w].astype(BF)


def pack_weights(widths, share, place, w_now, w_prev):
    rows, w = w_now.shape[1], widths[share]
    return pl.pallas_call(
        functools.partial(pack_w_kernel, widths, share),
        in_specs=[SMEM_SPEC, VMEM_SPEC, VMEM_SPEC],
        out_shape=[jax.ShapeDtypeStruct((rows, 6 * w), BF)] * 2,
        compiler_params=params(),
        cost_estimate=TINY,
        name="pack_weights",
    )(place, w_now, w_prev)


def pack_up_kernel(widths, place, up_ref, *outs):
    half = up_ref.shape[1] // 2
    low = place[1] == 0

    def body(r, _):
        rows = pl.ds(pl.multiple_of(r * TM, TM), TM)
        v = up_ref[rows, :].astype(F32)
        mine = jnp.where(low, v[:, :half], v[:, half:])
        other = jnp.where(low, v[:, half:], v[:, :half])
        for i, (at, w) in enumerate(offsets(widths)):
            outs[2 * i][rows, :] = mine[:, at : at + w].astype(BF)
            outs[2 * i + 1][rows, :w] = other[:, at : at + w].astype(BF)
        return 0

    lax.fori_loop(0, up_ref.shape[0] // TM, body, 0)


def pack_up(widths, place, grad_out):
    t = grad_out.shape[0]
    return pl.pallas_call(
        functools.partial(pack_up_kernel, widths),
        in_specs=[SMEM_SPEC, VMEM_SPEC],
        out_shape=[jax.ShapeDtypeStruct((t, w), BF) for v in widths for w in (v, ceil_to(v, LANES))],
        compiler_params=params(),
        cost_estimate=TINY,
        name="pack_up",
    )(place, grad_out)


def gates_kernel(plan, place, *refs):
    n, m, dw, dl, t, c, up_at, wrel, xrel = plan
    n_w, n_x = len(wrel) or 1, len(xrel) or 1
    w_in, refs = refs[:n_w], refs[n_w:]
    x_in, refs = refs[:n_x], refs[n_x:]
    if not xrel:
        halo_in, refs = refs[0], refs[1:]
    bias_ref, up0, up1 = refs[:3]
    refs = refs[3:]
    if not xrel:
        keep_w, refs = refs[0], refs[1:]
    g_ref, seg_ref, tot_ref, refs = refs[0], refs[1], refs[2], refs[3:]
    if xrel:
        x_out, halo_out, keep_w, refs = refs[0], refs[1], refs[2], refs[3:]
    w_out, refs = refs[0], refs[1:]
    xs, halo, ws, p_s, d_s, s_s, q_s, seg_s, xsem, hsem, wsem, osem = refs
    pad = ws.shape[1]
    width = ws.shape[2]
    wide = n // m
    h, l, p, a, b = (place[i] for i in range(5))
    heads = n // 4
    copies = []
    if wrel:
        for i, (kh, d_p) in enumerate(wrel):
            for d_l in range(2):
                block = (lax.rem(h - kh + heads, heads) * 2 + (l ^ d_l)) * 2 + (p ^ d_p)
                at = pl.multiple_of(lax.rem(block, wide) * dw, 16)
                copies.append(
                    pltpu.make_async_copy(
                        w_in[i].at[d_l], ws.at[block // wide, pl.ds(at, dw), :], wsem.at[2 * i + d_l]
                    )
                )
        if pad > dl:
            for g in range(m):
                ws[g, dl:, :] = jnp.zeros((pad - dl, width), BF)
    else:
        copies.append(pltpu.make_async_copy(w_in[0], ws, wsem.at[0]))
    xcopies = [[], []]
    if xrel:
        for i, (slot, d_a, d_b) in enumerate(xrel):
            at = pl.multiple_of(((a ^ d_a) * 2 + (b ^ d_b)) * pad, LANES)
            xcopies[slot].append(
                pltpu.make_async_copy(
                    x_in[i].at[pl.ds(0, t)], xs.at[pl.ds(slot * t, t), pl.ds(at, pad)], xsem.at[i]
                )
            )
            copies.append(
                pltpu.make_async_copy(
                    x_in[i].at[pl.ds(t, EDGE)], halo.at[pl.ds(slot * EDGE, EDGE), pl.ds(at, pad)], hsem.at[i]
                )
            )
    else:
        for slot in range(2):
            rows = pl.ds(slot * t, t)
            xcopies[slot].append(pltpu.make_async_copy(x_in[0].at[rows], xs.at[rows], xsem.at[slot]))
        copies.append(pltpu.make_async_copy(halo_in, halo, hsem.at[0]))
    for copy in copies + xcopies[0] + xcopies[1]:
        copy.start()
    for copy in copies:
        copy.wait()
    outs = []
    for g in range(m):
        outs.append(pltpu.make_async_copy(ws.at[g], w_out.at[(a * 2 + b) ^ g], osem.at[g]))
    for copy in outs:
        copy.start()
    lanes = cuts(c)
    weights = ws[...].reshape(m * pad, width)
    if xrel:
        out = pltpu.make_async_copy(halo, halo_out, osem.at[m + 2])
        out.start()
        outs.append(out)
    edge = jnp.dot(halo[...], weights, preferred_element_type=F32)
    for slot, up_ref in enumerate((up0, up1)):
        for copy in xcopies[slot]:
            copy.wait()
        if xrel:
            rows = pl.ds(slot * t, t)
            out = pltpu.make_async_copy(xs.at[rows], x_out.at[rows], osem.at[m + slot])
            out.start()
            outs.append(out)
        p_s[7:8, :] = edge[slot * EDGE : slot * EDGE + 1, :]

        def tile(i, _, slot=slot, up_ref=up_ref):
            base = pl.multiple_of(i * ROWS, ROWS)
            x = xs[pl.ds(pl.multiple_of(slot * t + base, ROWS), ROWS), :]
            p_s[8:, :] = jnp.dot(x, ws[...].reshape(m * pad, width), preferred_element_type=F32)
            for r in range(ROWS // TM):
                rows = pl.ds(pl.multiple_of(base + r * TM, TM), TM)
                full = pl.ds(pl.multiple_of(slot * t + base + r * TM, TM), TM)
                apart = spread(base + r * TM, t // SEGS)
                if xrel:
                    flags = xs[full, dl:pad].astype(F32)
                    keep = jnp.concatenate([flags] * (LANES // (pad - dl)), axis=1)
                    keep_w[full, :] = keep
                else:
                    keep = keep_w[full, :]
                for k_l, lo, w in lanes:
                    g = []
                    for k in range(3):
                        now = p_s[8 + r * TM : 8 + (r + 1) * TM, group(k, lo, w)]
                        before = p_s[7 + r * TM : 7 + (r + 1) * TM, group(3 + k, lo, w)]
                        v = now + keep[:, :w] * before + bias_ref[k : k + 1, lo : lo + w]
                        g_ref[k, full, lo : lo + w] = v
                        g.append(v)
                    f, intake = both(g[1])
                    o, _ = both(g[2])
                    d = keep[:, :w] * f
                    d_s[slot, k_l, apart, :w] = d
                    s_s[slot, k_l, apart, :w] = intake * jnp.tanh(g[0])
                    q_s[slot, k_l, apart, :w] = d * (load_up(up_ref, rows, slot * up_at + lo, w) * o)
            p_s[7:8, :] = p_s[ROWS + 7 : ROWS + 8, :]
            return 0

        lax.fori_loop(0, t // ROWS, tile, 0)
    span = t // SEGS
    chains = [(slot, k_l) for slot in range(2) for k_l, _, _ in lanes]
    one, zero = jnp.ones((SEGS, LANES), F32), jnp.zeros((SEGS, LANES), F32)

    def step(j, carry):
        at, back = pl.ds(j, SEGS, stride=span + GAP), pl.ds(span - 1 - j, SEGS, stride=span + GAP)
        new = []
        for (slot, k_l), (pa, ps, pr) in zip(chains, carry):
            d = d_s[slot, k_l, at, :]
            new.append(
                (
                    pa * d,
                    d * ps + s_s[slot, k_l, at, :],
                    d_s[slot, k_l, back, :] * pr + q_s[slot, k_l, back, :],
                )
            )
        return tuple(new)

    res = lax.fori_loop(0, span, step, tuple((one, zero, zero) for _ in chains), unroll=4)
    for (slot, k_l), triple in zip(chains, res):
        _, lo, w = lanes[k_l]
        for k in range(3):
            seg_s[k] = triple[k]
            seg_ref[slot, k, :, lo : lo + w] = triple[k][:, :w]
        pa, ps, pr = one[:1], zero[:1], zero[:1]
        for k in range(SEGS):
            d = seg_s[0, k : k + 1, :]
            ps = d * ps + seg_s[1, k : k + 1, :]
            pa = pa * d
            r = SEGS - 1 - k
            pr = seg_s[0, r : r + 1, :] * pr + seg_s[2, r : r + 1, :]
        for k, v in enumerate((pa, ps, pr)):
            tot_ref[slot, k : k + 1, lo : lo + w] = v[:, :w]
    for copy in outs:
        copy.wait()


def after(v, *needs):
    return lax.optimization_barrier((v, *needs))[0]


def gates_and_totals(dims, up_at, place, w, wrel, x, xrel, bias, ups, keep_w=None):
    n, m, dw, dl, t, c = dims
    pad = ceil_to(dl, LANES)
    lt = len(cuts(c))
    width = 6 * c
    plan = (n, m, dw, dl, t, c, up_at, tuple(wrel), tuple(xrel))
    shape = jax.ShapeDtypeStruct
    outs = [shape((3, 2 * t, c), F32), shape((2, 3, SEGS, c), F32), shape((2, 3, c), F32)]
    specs = [VMEM_SPEC] * 3
    if xrel:
        outs += [shape((2 * t, m * pad), BF), shape((2 * EDGE, m * pad), BF), shape((2 * t, LANES), F32)]
        specs += [ANY_SPEC, ANY_SPEC, VMEM_SPEC]
    outs.append(shape((m, pad, width), BF))
    specs.append(ANY_SPEC)
    return pl.pallas_call(
        functools.partial(gates_kernel, plan),
        in_specs=[SMEM_SPEC] + [ANY_SPEC] * (len(w) + len(x)) + [VMEM_SPEC] * (3 if xrel else 4),
        out_specs=specs,
        out_shape=outs,
        scratch_shapes=[
            pltpu.VMEM((2 * t, m * pad), BF),
            pltpu.VMEM((2 * EDGE, m * pad), BF),
            pltpu.VMEM((m, pad, width), BF),
            pltpu.VMEM((ROWS + 8, width), F32),
            pltpu.VMEM((2, lt, t + SEGS * GAP, LANES), F32),
            pltpu.VMEM((2, lt, t + SEGS * GAP, LANES), F32),
            pltpu.VMEM((2, lt, t + SEGS * GAP, LANES), F32),
            pltpu.VMEM((3, SEGS, LANES), F32),
            pltpu.SemaphoreType.DMA((max(2, len(x)),)),
            pltpu.SemaphoreType.DMA((max(1, len(x)),)),
            pltpu.SemaphoreType.DMA((2 * len(w),)),
            pltpu.SemaphoreType.DMA((m + 3,)),
        ],
        compiler_params=params(),
        cost_estimate=TINY,
        name="gates_and_totals",
    )(place, *w, *x, bias, *ups, *([] if xrel else [keep_w]))


def finish_kernel(n, up_at, place, g_ref, up0, up1, keep_ref, seg_ref, all_ref, h0, h1, gg_ref, gf_ref, gp_ref, gb_ref, d_s, s_s, q_s, p_s, c_s):
    t, c = up0.shape
    span = t // SEGS
    lanes = cuts(c)
    heads = n // 4
    hh, ll, pp = place[0], place[1], place[2]
    ups, hids = (up0, up1), (h0, h1)
    for slot in range(2):

        def act(r, _, slot=slot):
            rows = pl.ds(pl.multiple_of(r * TM, TM), TM)
            full = pl.ds(pl.multiple_of(slot * t + r * TM, TM), TM)
            apart = spread(r * TM, span)
            for k_l, lo, w in lanes:
                ch = slice(lo, lo + w)
                f, i = both(g_ref[1, full, ch])
                o, _ = both(g_ref[2, full, ch])
                d_s[slot, k_l, apart, :w] = keep_ref[full, :w] * f
                s_s[slot, k_l, apart, :w] = i * jnp.tanh(g_ref[0, full, ch])
                q_s[slot, k_l, apart, :w] = load_up(ups[slot], rows, slot * up_at + lo, w) * o
            return 0

        lax.fori_loop(0, t // TM, act, 0)
    zrow = jnp.zeros((1, c), F32)
    mine = [(hh * 2 + (ll ^ slot)) * 2 + pp for slot in range(2)]

    def total(block, k):
        p_b, l_b, h_b = block % 2, block // 2 % 2, block // 4
        member = lax.rem(hh - h_b + heads, heads) * 2 + (pp ^ p_b)
        return all_ref[member, ll ^ l_b, k : k + 1, :]

    h, r = zrow, zrow
    h_in, r_in = [zrow, zrow], [zrow, zrow]
    for k in range(n):
        b = n - 1 - k
        h_in = [jnp.where(mine[s] == k, h, h_in[s]) for s in range(2)]
        r_in = [jnp.where(mine[s] == b, r, r_in[s]) for s in range(2)]
        h = total(k, 0) * h + total(k, 1)
        r = total(b, 0) * r + total(b, 2)
    for slot in range(2):
        h, r = h_in[slot], r_in[slot]
        for k in range(SEGS):
            b = SEGS - 1 - k
            for k_l, lo, w in lanes:
                c_s[0, slot, k_l, k : k + 1, :w] = h[:, lo : lo + w]
                c_s[1, slot, k_l, b : b + 1, :w] = r[:, lo : lo + w]
            h = seg_ref[slot, 0, k : k + 1, :] * h + seg_ref[slot, 1, k : k + 1, :]
            r = seg_ref[slot, 0, b : b + 1, :] * r + seg_ref[slot, 2, b : b + 1, :]
    chains = [(slot, k_l) for slot in range(2) for k_l, _, _ in lanes]

    def step(j, carry):
        at, back = pl.ds(j, SEGS, stride=span + GAP), pl.ds(span - 1 - j, SEGS, stride=span + GAP)
        new = []
        for (slot, k_l), (h, r) in zip(chains, carry):
            dh = d_s[slot, k_l, at, :] * h
            h = dh + s_s[slot, k_l, at, :]
            p_s[slot, k_l, at, :] = dh
            s_s[slot, k_l, at, :] = h
            g = q_s[slot, k_l, back, :] + r
            q_s[slot, k_l, back, :] = g
            new.append((h, d_s[slot, k_l, back, :] * g))
        return tuple(new)

    lax.fori_loop(0, span, step, tuple((c_s[0, s, k_l], c_s[1, s, k_l]) for s, k_l in chains), unroll=4)
    sums = [jnp.zeros((8, w), F32) for _, _, w in lanes for _ in range(3)]
    top = lax.broadcasted_iota(jnp.int32, (EDGE, LANES), 0) == 0
    gp_ref[...] = jnp.zeros(gp_ref.shape, BF)
    for slot in range(2):

        def out(i, state, slot=slot):
            acc, nxt = state
            r = t // TM - 1 - i
            rows = pl.ds(pl.multiple_of(r * TM, TM), TM)
            full = pl.ds(pl.multiple_of(slot * t + r * TM, TM), TM)
            apart = spread(r * TM, span)
            last = lax.broadcasted_iota(jnp.int32, (TM, LANES), 0) == TM - 1
            new, first = [], []
            for k_l, lo, w in lanes:
                ch = slice(lo, lo + w)
                f, intake = both(g_ref[1, full, ch])
                o, cl = both(g_ref[2, full, ch])
                z = jnp.tanh(g_ref[0, full, ch])
                keep = keep_ref[full, :w]
                gs = q_s[slot, k_l, apart, :w]
                oh = o * s_s[slot, k_l, apart, :w]
                hids[slot][rows, ch] = oh.astype(BF)
                gi = gs * intake
                grads = (
                    gi * (1.0 - z * z),
                    gi * (p_s[slot, k_l, apart, :w] - f * z),
                    load_up(ups[slot], rows, slot * up_at + lo, w) * oh * cl,
                )
                for k, v in enumerate(grads):
                    gg_ref[full, group(k, lo, w)] = v.astype(BF)
                    kept = keep * v
                    moved = jnp.where(last[:, :w], nxt[len(new)], pltpu.roll(kept, TM - 1, 0))
                    gg_ref[full, group(3 + k, lo, w)] = moved.astype(BF)
                    first.append(kept[:1])
                    new.append(acc[len(new)] + jnp.sum(v.reshape(TM // 8, 8, w), axis=0))
            return tuple(new), tuple(first)

        zeros = tuple(jnp.zeros((1, w), F32) for _, _, w in lanes for _ in range(3))
        sums, firsts = lax.fori_loop(0, t // TM, out, (tuple(sums), zeros))
        for k_l, lo, w in lanes:
            for k in range(3):
                gf_ref[slot : slot + 1, group(k, lo, w, 3)] = firsts[3 * k_l + k]
                gp_ref[slot * EDGE : slot * EDGE + EDGE, group(3 + k, lo, w)] = jnp.where(
                    top[:, :w], firsts[3 * k_l + k], 0.0
                ).astype(BF)
    for k_l, lo, w in lanes:
        for k in range(3):
            gb_ref[0:1, k * c + lo : k * c + lo + w] = jnp.sum(sums[3 * k_l + k], axis=0, keepdims=True)


def finish(n, up_at, place, gates, ups, keep_w, seg, every):
    t, c = ups[0].shape
    lt = len(cuts(c))
    shape = jax.ShapeDtypeStruct
    return pl.pallas_call(
        functools.partial(finish_kernel, n, up_at),
        in_specs=[SMEM_SPEC] + [VMEM_SPEC] * 6,
        out_shape=[
            shape((t, c), BF),
            shape((t, c), BF),
            shape((2 * t, 6 * c), BF),
            shape((2, 3 * c), F32),
            shape((2 * EDGE, 6 * c), BF),
            shape((1, 3 * c), F32),
        ],
        scratch_shapes=[pltpu.VMEM((2, lt, t + SEGS * GAP, LANES), F32)] * 4 + [pltpu.VMEM((2, 2, lt, SEGS, LANES), F32)],
        compiler_params=params(),
        cost_estimate=TINY,
        name="finish",
    )(place, gates, *ups, keep_w, seg, every)


def wgrad_kernel(dw, place, x_ref, halo_ref, gg_ref, gp_ref, *refs):
    *outs, acc = refs
    over_tokens = (((0,), (0,)), ((), ()))
    v = lax.dot_general(x_ref[...], gg_ref[...], over_tokens, preferred_element_type=F32)
    acc[...] = v + lax.dot_general(halo_ref[...], gp_ref[...], over_tokens, preferred_element_type=F32)
    p = place[2]
    step = pl.program_id(0)
    for k in range(len(outs) // 2):

        @pl.when(step // 2 == k)
        def _(k=k):
            outs[2 * k][0] = acc[pl.ds(pl.multiple_of(p * dw, 16), dw), :].astype(BF)
            outs[2 * k + 1][0] = acc[pl.ds(pl.multiple_of((1 - p) * dw, 16), dw), :].astype(BF)


def weight_grads(heads, dw, pad, place, x_all, halo, gg, gp):
    width = gg.shape[1]

    def lanes(i, at):
        kh = lax.rem(i // 2 + 1, heads)
        return (0, lax.rem(at[0] + kh, heads) * 2 + (at[1] ^ (1 - lax.rem(i, 2))))

    def out(k):
        return pl.BlockSpec((1, dw, width), lambda i, at: (jnp.clip(i - 2 * k, 0, 1), 0, 0))

    whole = lambda i, at: (0, 0)
    res = pl.pallas_call(
        functools.partial(wgrad_kernel, dw),
        grid_spec=pltpu.PrefetchScalarGridSpec(
            num_scalar_prefetch=1,
            grid=(2 * heads,),
            in_specs=[
                pl.BlockSpec((x_all.shape[0], pad), lanes),
                pl.BlockSpec((halo.shape[0], pad), lanes),
                pl.BlockSpec(gg.shape, whole),
                pl.BlockSpec(gp.shape, whole),
            ],
            out_specs=[out(k) for k in range(heads) for _ in range(2)],
            scratch_shapes=[pltpu.VMEM((pad, width), F32)],
        ),
        out_shape=[jax.ShapeDtypeStruct((2, dw, width), BF)] * (2 * heads),
        compiler_params=params(),
        cost_estimate=TINY,
        name="weight_grads",
    )(place, x_all, halo, gg, gp)
    return [((k + 1) % heads, res[2 * k], res[2 * k + 1]) for k in range(heads)]


def xgrad_kernel(place, *refs):
    count = (len(refs) - 5) // 4
    gg_in, nx, w_in = refs[:count], refs[count : 2 * count], refs[2 * count : 3 * count]
    outs = refs[3 * count : 3 * count + 4]
    gg_s, sem = refs[3 * count + 4 : 4 * count + 4], refs[4 * count + 4]
    i, turn = pl.program_id(0), pl.program_id(1)
    t = gg_s[0].shape[0] // 2

    @pl.when((i == 0) & (turn == 0))
    def _():
        copies = [pltpu.make_async_copy(gg_in[k], gg_s[k], sem.at[k]) for k in range(count)]
        for copy in copies:
            copy.start()
        for k, copy in enumerate(copies):
            copy.wait()
            for _, lo, w in cuts(nx[k].shape[1] // 3):
                last = lax.broadcasted_iota(jnp.int32, (EDGE, 3 * w), 0) == EDGE - 1
                there = slice(6 * lo + 3 * w, 6 * lo + 6 * w)
                for slot in range(2):
                    rows = slice((slot + 1) * t - EDGE, (slot + 1) * t)
                    old = gg_s[k][rows, there].astype(F32)
                    new = nx[k][slot : slot + 1, 3 * lo : 3 * lo + 3 * w]
                    gg_s[k][rows, there] = jnp.where(last, new, old).astype(BF)

    rows = pl.ds(pl.multiple_of((1 - turn) * t, t), t)
    v = 0.0
    for k in range(count):
        v = v + lax.dot_general(
            gg_s[k][rows, :], w_in[k][0], (((1,), (1,)), ((), ())), preferred_element_type=F32
        )
    v = v.astype(BF)
    for k in range(4):

        @pl.when((turn == k // 2) & ((i < 2) == (k % 2 == 0)))
        def _(k=k):
            outs[k][0] = v


def input_grads(place, ggs, nexts, ws):
    count = len(ggs)
    t = ggs[0].shape[0] // 2
    m, pad, _ = ws[0].shape
    order = lambda i: jnp.where(i < 2, 2 * i + 1, 2 * i - 4)
    sent = pl.BlockSpec((1, t, pad), lambda i, turn, at: (jnp.minimum(i, 1), 0, 0))
    kept = pl.BlockSpec((1, t, pad), lambda i, turn, at: (jnp.maximum(i - 2, 0), 0, 0))
    return pl.pallas_call(
        xgrad_kernel,
        grid_spec=pltpu.PrefetchScalarGridSpec(
            num_scalar_prefetch=1,
            grid=(m, 2),
            in_specs=[ANY_SPEC] * count
            + [pl.BlockSpec(v.shape, lambda i, turn, at: (0, 0)) for v in nexts]
            + [pl.BlockSpec((1, pad, w.shape[2]), lambda i, turn, at: (order(i), 0, 0)) for w in ws],
            out_specs=[sent, kept, sent, kept],
            scratch_shapes=[pltpu.VMEM(gg.shape, BF) for gg in ggs] + [pltpu.SemaphoreType.DMA((count,))],
        ),
        out_shape=[jax.ShapeDtypeStruct((2, t, pad), BF)] * 4,
        compiler_params=params(),
        cost_estimate=TINY,
        name="input_grads",
    )(place, *ggs, *nexts, *ws)


def join_kernel(*refs):
    *terms, out = refs
    v = terms[0][...].astype(F32)
    for ref in terms[1:]:
        v = v + ref[...].astype(F32)
    out[...] = v.astype(BF)


def join(terms, urgency):
    arrays = [v for v, _ in terms]
    shape = arrays[0].shape[-2:]
    steps = 2 if shape[0] % 32 == 0 else 1
    blocks = shape[0] // steps

    def spec(v, at):
        if at is None:
            return pl.BlockSpec((blocks, shape[1]), lambda i: (i, 0))
        return pl.BlockSpec((None, blocks, shape[1]), lambda i, at=at: (at, i, 0))

    return pl.pallas_call(
        join_kernel,
        grid=(steps,),
        in_specs=[spec(v, at) for v, at in terms],
        out_specs=pl.BlockSpec((blocks, shape[1]), lambda i: (i, 0)),
        out_shape=jax.ShapeDtypeStruct(shape, BF),
        compiler_params=params(),
        cost_estimate=pl.CostEstimate(flops=0, bytes_accessed=urgency * 3690000, transcendentals=0),
        name="join",
    )(*arrays)


def unpack_w_kernel(widths, place, *refs):
    count = len(widths)
    outs = refs[2 * count :]
    low = place[1] == 0
    for tap in range(2):
        for k in range(3):
            mine, other = [], []
            for i, c in enumerate(widths):
                for _, lo, w in cuts(c):
                    mine.append(refs[2 * i][:, group(tap * 3 + k, lo, w)].astype(F32))
                    other.append(refs[2 * i + 1][:, group(tap * 3 + k, lo, w)].astype(F32))
            mine, other = jnp.concatenate(mine, axis=1), jnp.concatenate(other, axis=1)
            outs[tap][k] = jnp.concatenate([jnp.where(low, mine, other), jnp.where(low, other, mine)], axis=1)


def unpack_weights(widths, place, pairs):
    rows = pairs[0].shape[0]
    shape = jax.ShapeDtypeStruct((3, rows, 2 * sum(widths)), F32)
    return pl.pallas_call(
        functools.partial(unpack_w_kernel, widths),
        in_specs=[SMEM_SPEC] + [VMEM_SPEC] * len(pairs),
        out_shape=[shape, shape],
        compiler_params=params(),
        cost_estimate=TINY,
        name="unpack_weights",
    )(place, *pairs)


def unpack_h_kernel(widths, place, *refs):
    out_ref = refs[-1]
    low = place[1] == 0

    def body(r, _):
        rows = pl.ds(pl.multiple_of(r * TM, TM), TM)
        mine = jnp.concatenate([refs[i][rows, :].astype(F32) for i in range(len(widths))], axis=1)
        other = refs[len(widths)][rows, :].astype(F32)
        both_halves = jnp.concatenate([jnp.where(low, mine, other), jnp.where(low, other, mine)], axis=1)
        out_ref[rows, :] = both_halves.astype(BF)
        return 0

    lax.fori_loop(0, out_ref.shape[0] // TM, body, 0)


def unpack_hidden(widths, place, mine, other):
    t = other.shape[0]
    return pl.pallas_call(
        functools.partial(unpack_h_kernel, widths),
        in_specs=[SMEM_SPEC] + [VMEM_SPEC] * (len(mine) + 1),
        out_shape=jax.ShapeDtypeStruct((t, 2 * sum(widths)), BF),
        compiler_params=params(),
        cost_estimate=TINY,
        name="unpack_hidden",
    )(place, *mine, other)


def on_device(layer_input, keep, w_now, w_prev, bias, grad_out):
    n, m = lax.axis_size("seq"), lax.axis_size("gate")
    heads = n // 4
    s, g = lax.axis_index("seq"), lax.axis_index("gate")
    h, l, p, a, b = s // 4, s // 2 % 2, s % 2, g // 2, g % 2
    place = jnp.stack([h, l, p, a, b]).astype(jnp.int32)
    t, dl = layer_input.shape
    dw = w_now.shape[1]
    half = dl // 2
    pad = ceil_to(dl, LANES)
    widths = tuple(w for w in WIDTHS) if sum(WIDTHS) == half else (half,)
    low = l == 0

    def seq_to(v, kh, d_l, d_p):
        route = []
        for i in range(n):
            i_h, i_l, i_p = i // 4, i // 2 % 2, i % 2
            route.append((i, ((i_h + kh) % heads * 2 + (i_l ^ d_l)) * 2 + (i_p ^ d_p)))
        return lax.ppermute(v, "seq", route)

    def gate_to(v, d_a, d_b):
        return lax.ppermute(v, "gate", [(i, i ^ (d_a * 2 + d_b)) for i in range(m)])

    group = [(kh, d_p) for kh in range(heads) for d_p in range(2)]

    packed = pack_weights(widths, 0, place, w_now, w_prev)
    behind = lax.ppermute(layer_input[-1:], "seq", [(i, i + 1) for i in range(n - 1)])
    flags = jnp.broadcast_to(jnp.pad(keep, (0, EDGE)).astype(BF)[:, None], (t + EDGE, pad - dl))
    rows = jnp.concatenate([layer_input, jnp.pad(behind, ((0, EDGE - 1), (0, 0)))], axis=0)
    x0 = after(jnp.concatenate([rows, flags], axis=1), packed[0])
    def share_w(pair, *needs):
        got = {(0, 0): pair, (0, 1): seq_to(pair, 0, 0, 1)}
        for kh in range(1, heads):
            got[kh, 0] = seq_to(after(pair, *needs) if needs else pair, kh, 0, 0)
        return got

    def finish_share(got, *needs):
        for kh in range(1, heads):
            got[kh, 1] = seq_to(after(got[kh, 0], *needs) if needs else got[kh, 0], 0, 0, 1)

    def weights_in(got, c):
        if dw % 16 == 0:
            return [got[r] for r in got], list(got)
        stacked = jnp.stack([got[kh, d_p][d_l] for kh in range(heads) for d_l in range(2) for d_p in range(2)])
        blocks = jnp.arange(n)
        rel = (((h - blocks // 4) % heads) * 2 + (l ^ (blocks // 2 % 2))) * 2 + (p ^ (blocks % 2))
        whole = jnp.take(stacked, rel, axis=0).reshape(m, dl, 6 * c)
        return [jnp.pad(whole, ((0, 0), (0, pad - dl), (0, 0)))], []

    half_bias = jnp.where(low, bias[:, :half], bias[:, half:])
    count = len(widths)
    spans = list(offsets(widths))
    near = seq_to(packed[1], 0, 1, 0)
    got = [share_w(jnp.stack([packed[0], near]))]
    y0 = gate_to(x0, 1, 0)
    x1 = seq_to(after(x0, near), 0, 1, 0)
    first_p = got[0][0, 1]
    up_packed = pack_up(widths, place, after(grad_out, x0))
    ups = [[up_packed[0], seq_to(after(up_packed[1], near), 0, 1, 0)]]
    hop = [got[0][kh, 0] for kh in range(1, heads)]
    c0, cy0 = gate_to(after(x0, y0, first_p, *hop), 0, 1), gate_to(after(y0, first_p, *hop), 0, 1)
    x1_here = after(x1, y0, first_p)
    y1, c1 = gate_to(x1_here, 1, 0), gate_to(x1_here, 0, 1)
    finish_share(got[0])
    for i in range(1, count):
        packed = pack_weights(widths, i, place, after(w_now, near), w_prev)
        near = seq_to(packed[1], 0, 1, 0)
        got.append(share_w(jnp.stack([packed[0], near]), c1, *[got[i - 1][kh, 0] for kh in range(1, heads)]))
        ups.append([up_packed[2 * i], seq_to(after(up_packed[2 * i + 1], near), 0, 1, 0)])
    cy1 = gate_to(after(y1, ups[0][1], *[got[0][kh, 1] for kh in range(1, heads)]), 0, 1)
    xs = {(0, 0, 0): x0, (0, 1, 0): y0, (0, 0, 1): c0, (0, 1, 1): cy0}
    xs |= {(1, 0, 0): x1, (1, 1, 0): y1, (1, 0, 1): c1, (1, 1, 1): cy1}
    hidden_mine, hidden_other, grads, wide_w, g_first, g_bias, w_pairs = [], [], [], [], [], [], []

    def spread_totals(tot):
        return jnp.stack([tot if r == (0, 0) else seq_to(tot, r[0], 0, r[1]) for r in group])

    def weight_parts(gg, gp, *needs):
        if dw % 16 == 0 and n == 2 * m:
            return weight_grads(heads, dw, pad, place, x_all, halo, gg, after(gp, *needs) if needs else gp)
        dots = jnp.einsum("td,tn->dn", x_all, gg, preferred_element_type=F32)
        dots = dots + jnp.einsum("td,tn->dn", halo, gp, preferred_element_type=F32)
        v = dots.astype(BF).reshape(m, pad, -1)[:, :dl].reshape(heads, 2, 2, dw, gg.shape[1])
        away = jnp.where(p == 0, v[:, :, 1], v[:, :, 0])
        here = jnp.where(p == 0, v[:, :, 0], v[:, :, 1])

        def block(v, kh):
            row = lax.dynamic_index_in_dim(v, (h + kh) % heads, 0, keepdims=False)
            return jnp.where(low, row[::-1], row)

        return [(kh, block(here, kh), block(away, kh)) for kh in list(range(1, heads)) + [0]]

    def over_p(parts, *needs):
        came = []
        for _, _, away in parts:
            came.append(after(seq_to(away, 0, 0, 1), *came[-1:], *needs))
        return [here.astype(F32) + v.astype(F32) for (_, here, _), v in zip(parts, came)]

    def over_h(parts, sums, *needs):
        total = sums[-1]
        for (kh, _, _), v in zip(parts[:-1], sums[:-1]):
            total = total + after(seq_to(v.astype(BF), kh, 0, 0), *needs).astype(F32)
        return total.astype(BF)

    waiting = None
    for i, (at, c) in enumerate(spans):
        dims = (n, m, dw, dl, t, c)
        bias_i = half_bias[:, at : at + c]
        if i > 0:
            finish_share(got[i], every, ups[i][1])
        w_in, wrel = weights_in(got[i], c)
        if i == 0:
            xrel = list(xs)
            gates, seg, tot, x_all, halo, keep_w, w_rel = gates_and_totals(
                dims, 0, place, w_in, wrel, [xs[r] for r in xrel], xrel, bias_i, ups[i]
            )
        else:
            w_in[0] = after(w_in[0], *[v[2] for v in waiting])
            gates, seg, tot, w_rel = gates_and_totals(
                dims, 0, place, w_in, wrel, [x_all, halo], [], bias_i, ups[i], keep_w
            )
        every = spread_totals(after(tot, *[g[0, 1] for g in got[i + 1 : i + 2]]) if i + 1 < count else tot)
        wide_w.append(w_rel)
        if i > 0:
            sums = over_p(waiting, tot)
            h_sums = [after(v, every) for v in sums]
            every = after(every, *sums)
        h0, h1, gg, gf, gp, gb = finish(n, 0, place, gates, ups[i], keep_w, seg, every)
        hidden_mine.append(h0)
        hidden_other.append(h1)
        g_first.append(gf)
        g_bias.append(gb)
        if i == count - 1:
            parts = jnp.concatenate([jnp.concatenate(g_first, axis=1), jnp.concatenate(g_bias, axis=1)], axis=0)
            around = [parts if r == (0, 0) else seq_to(parts, r[0], 0, r[1]) for r in group]
            hidden_came = seq_to(after(jnp.concatenate(hidden_other, axis=1), parts), 0, 1, 0)
        needs = list(around) if i == count - 1 else []
        if i > 0:
            total = over_h(waiting, h_sums)
            needs.append(total)
        waiting_next = weight_parts(gg, gp)
        if needs:
            waiting_next = [(kh, here, after(away, *needs)) for kh, here, away in waiting_next]
        if i > 0:
            w_pairs += [total[1], seq_to(total[0], 0, 1, 0)]
        waiting = waiting_next
        grads.append(gg)
    around = jnp.stack(around)

    full_bias = jnp.sum(around[:, 2], axis=0)
    nexts = []
    for slot in range(2):
        block_id = (h * 2 + (l ^ slot)) * 2 + p + 1
        n_h, n_l, n_p = block_id // 4, block_id // 2 % 2, block_id % 2
        member = ((h - n_h) % heads) * 2 + (p ^ n_p)
        row = lax.dynamic_index_in_dim(around, member, 0, keepdims=False)
        row = lax.dynamic_index_in_dim(row, l ^ n_l, 0, keepdims=False)
        nexts.append(jnp.where(block_id < n, row, jnp.zeros_like(row)))
    nexts = jnp.stack(nexts)
    nexts = [nexts[:, 3 * at : 3 * (at + c)] for at, c in spans]
    bias_half = []
    at = 0
    for c in widths:
        bias_half.append(full_bias[at : at + 3 * c].reshape(3, c))
        at += 3 * c
    bias_half = jnp.concatenate(bias_half, axis=1)
    bias_other = seq_to(bias_half, 0, 1, 0)
    nexts[0] = after(nexts[0], *[v[2] for v in waiting])
    sent1, kept1, sent0, kept0 = input_grads(place, grads, nexts, wide_w)
    p_came = []
    for v in waiting:
        p_came.append(after(seq_to(v[2], 0, 0, 1), *p_came[-1:]))
    sent1, sent0, *_ = lax.optimization_barrier((sent1, sent0, p_came[0], hidden_came, bias_other, *w_pairs))
    c_came1, c_came0 = gate_to(sent1, 0, 1), gate_to(sent0, 0, 1)
    h_came = []
    for k, (kh, here, _) in enumerate(waiting[:-1]):
        both_l = (here.astype(F32) + p_came[k].astype(F32)).astype(BF)
        c_came1 = after(c_came1, both_l)
        h_came.append(seq_to(both_l, kh, 0, 0))
    y_came1 = gate_to(join([(kept1, 1), (c_came1, 1)], LATER), 1, 0)
    y_came0 = gate_to(join([(kept0, 1), (c_came0, 1)], LATER), 1, 0)
    l_came = seq_to(join([(kept1, 0), (c_came1, 0), (y_came1, None)], LATER), 0, 1, 0)
    total = [
        join([(waiting[-1][1], d), (p_came[-1], d)] + [(v, d) for v in h_came], LATER) for d in range(2)
    ]
    w_pairs += [total[1], seq_to(total[0], 0, 1, 0)]
    grad_x = kept0[0].astype(F32) + c_came0[0].astype(F32) + y_came0.astype(F32) + l_came.astype(F32)
    grad_x = grad_x[:, :dl].astype(BF)

    grad_bias = jnp.concatenate(
        [jnp.where(low, bias_half, bias_other), jnp.where(low, bias_other, bias_half)], axis=1
    )
    hidden = unpack_hidden(widths, place, hidden_mine, hidden_came)
    grad_now, grad_prev = unpack_weights(widths, place, w_pairs)
    return hidden, grad_x, grad_now, grad_prev, grad_bias


def solution(mesh):
    tokens, matrix = P("seq", "gate"), P(None, "seq", "gate")
    return jax.shard_map(
        on_device,
        mesh=mesh,
        in_specs=(tokens, P("seq"), matrix, matrix, P(None, "gate"), tokens),
        out_specs=(tokens, tokens, matrix, matrix, P(None, "gate")),
        check_vma=False,
    )
```

```python
import functools

import jax
import jax.numpy as jnp
from jax import lax
from jax.experimental import pallas as pl
from jax.experimental.pallas import tpu as pltpu
from jax.sharding import PartitionSpec as P

F32 = jnp.float32
BF = jnp.bfloat16
SEGS = 8
LANES = 128
TM = 64
ROWS = 256
EDGE = 16
GAP = 8
VMEM = 62 << 20
WIDTHS = (128, 160)


def ceil_to(value, unit):
    return -(-value // unit) * unit


def both(g):
    e = jnp.exp(-jnp.abs(g))
    r = 1.0 / (1.0 + e)
    er = e * r
    pos = g >= 0
    return jnp.where(pos, r, er), jnp.where(pos, er, r)


def group(k, lo, w, count=6):
    return slice(count * lo + k * w, count * lo + (k + 1) * w)


def load_up(ref, rows, lo, w):
    return ref[rows, lo : lo + w].astype(F32)


def spread(row, span):
    return pl.ds(pl.multiple_of(row + row // span * GAP, 8), TM)


def cuts(c):
    return [(i, i * LANES, min(LANES, c - i * LANES)) for i in range(-(-c // LANES))]


def params():
    return pltpu.CompilerParams(vmem_limit_bytes=VMEM)


URGENT, LATER = 100, 50
TINY = pl.CostEstimate(flops=1 << 10, bytes_accessed=1 << 10, transcendentals=0)
SMEM_SPEC = pl.BlockSpec(memory_space=pltpu.SMEM)
VMEM_SPEC = pl.BlockSpec(memory_space=pltpu.VMEM)
ANY_SPEC = pl.BlockSpec(memory_space=pl.ANY)


def offsets(widths):
    at = 0
    for w in widths:
        yield at, w
        at += w


def pack_w_kernel(widths, share, place, now_ref, prev_ref, *outs):
    half = now_ref.shape[2] // 2
    low = place[1] == 0
    for tap, ref in enumerate((now_ref, prev_ref)):
        for k in range(3):
            v = ref[k].astype(F32)
            mine = jnp.where(low, v[:, :half], v[:, half:])
            other = jnp.where(low, v[:, half:], v[:, :half])
            at, c = list(offsets(widths))[share]
            for _, lo, w in cuts(c):
                to = group(tap * 3 + k, lo, w)
                outs[0][:, to] = mine[:, at + lo : at + lo + w].astype(BF)
                outs[1][:, to] = other[:, at + lo : at + lo + w].astype(BF)


def pack_weights(widths, share, place, w_now, w_prev):
    rows, w = w_now.shape[1], widths[share]
    return pl.pallas_call(
        functools.partial(pack_w_kernel, widths, share),
        in_specs=[SMEM_SPEC, VMEM_SPEC, VMEM_SPEC],
        out_shape=[jax.ShapeDtypeStruct((rows, 6 * w), BF)] * 2,
        compiler_params=params(),
        cost_estimate=TINY,
        name="pack_weights",
    )(place, w_now, w_prev)


def pack_up_kernel(widths, place, up_ref, *outs):
    half = up_ref.shape[1] // 2
    low = place[1] == 0

    def body(r, _):
        rows = pl.ds(pl.multiple_of(r * TM, TM), TM)
        v = up_ref[rows, :].astype(F32)
        mine = jnp.where(low, v[:, :half], v[:, half:])
        other = jnp.where(low, v[:, half:], v[:, :half])
        for i, (at, w) in enumerate(offsets(widths)):
            outs[2 * i][rows, :] = mine[:, at : at + w].astype(BF)
            outs[2 * i + 1][rows, :w] = other[:, at : at + w].astype(BF)
        return 0

    lax.fori_loop(0, up_ref.shape[0] // TM, body, 0)


def pack_up(widths, place, grad_out):
    t = grad_out.shape[0]
    return pl.pallas_call(
        functools.partial(pack_up_kernel, widths),
        in_specs=[SMEM_SPEC, VMEM_SPEC],
        out_shape=[jax.ShapeDtypeStruct((t, w), BF) for v in widths for w in (v, ceil_to(v, LANES))],
        compiler_params=params(),
        cost_estimate=TINY,
        name="pack_up",
    )(place, grad_out)


def gates_kernel(plan, place, *refs):
    n, m, dw, dl, t, c, up_at, wrel, xrel = plan
    n_w, n_x = len(wrel) or 1, len(xrel) or 1
    w_in, refs = refs[:n_w], refs[n_w:]
    x_in, refs = refs[:n_x], refs[n_x:]
    if not xrel:
        halo_in, refs = refs[0], refs[1:]
    bias_ref, up0, up1 = refs[:3]
    refs = refs[3:]
    if not xrel:
        keep_w, refs = refs[0], refs[1:]
    g_ref, seg_ref, tot_ref, refs = refs[0], refs[1], refs[2], refs[3:]
    if xrel:
        x_out, halo_out, keep_w, refs = refs[0], refs[1], refs[2], refs[3:]
    w_out, refs = refs[0], refs[1:]
    xs, halo, ws, p_s, d_s, s_s, q_s, seg_s, xsem, hsem, wsem, osem = refs
    pad = ws.shape[1]
    width = ws.shape[2]
    wide = n // m
    h, l, p, a, b = (place[i] for i in range(5))
    heads = n // 4
    copies = []
    if wrel:
        for i, (kh, d_p) in enumerate(wrel):
            for d_l in range(2):
                block = (lax.rem(h - kh + heads, heads) * 2 + (l ^ d_l)) * 2 + (p ^ d_p)
                at = pl.multiple_of(lax.rem(block, wide) * dw, 16)
                copies.append(
                    pltpu.make_async_copy(
                        w_in[i].at[d_l], ws.at[block // wide, pl.ds(at, dw), :], wsem.at[2 * i + d_l]
                    )
                )
        if pad > dl:
            for g in range(m):
                ws[g, dl:, :] = jnp.zeros((pad - dl, width), BF)
    else:
        copies.append(pltpu.make_async_copy(w_in[0], ws, wsem.at[0]))
    xcopies = [[], []]
    if xrel:
        for i, (slot, d_a, d_b) in enumerate(xrel):
            at = pl.multiple_of(((a ^ d_a) * 2 + (b ^ d_b)) * pad, LANES)
            xcopies[slot].append(
                pltpu.make_async_copy(
                    x_in[i].at[pl.ds(0, t)], xs.at[pl.ds(slot * t, t), pl.ds(at, pad)], xsem.at[i]
                )
            )
            copies.append(
                pltpu.make_async_copy(
                    x_in[i].at[pl.ds(t, EDGE)], halo.at[pl.ds(slot * EDGE, EDGE), pl.ds(at, pad)], hsem.at[i]
                )
            )
    else:
        for slot in range(2):
            rows = pl.ds(slot * t, t)
            xcopies[slot].append(pltpu.make_async_copy(x_in[0].at[rows], xs.at[rows], xsem.at[slot]))
        copies.append(pltpu.make_async_copy(halo_in, halo, hsem.at[0]))
    for copy in copies + xcopies[0] + xcopies[1]:
        copy.start()
    for copy in copies:
        copy.wait()
    outs = []
    for g in range(m):
        outs.append(pltpu.make_async_copy(ws.at[g], w_out.at[(a * 2 + b) ^ g], osem.at[g]))
    for copy in outs:
        copy.start()
    lanes = cuts(c)
    weights = ws[...].reshape(m * pad, width)
    if xrel:
        out = pltpu.make_async_copy(halo, halo_out, osem.at[m + 2])
        out.start()
        outs.append(out)
    edge = jnp.dot(halo[...], weights, preferred_element_type=F32)
    for slot, up_ref in enumerate((up0, up1)):
        for copy in xcopies[slot]:
            copy.wait()
        if xrel:
            rows = pl.ds(slot * t, t)
            out = pltpu.make_async_copy(xs.at[rows], x_out.at[rows], osem.at[m + slot])
            out.start()
            outs.append(out)
        p_s[7:8, :] = edge[slot * EDGE : slot * EDGE + 1, :]

        def tile(i, _, slot=slot, up_ref=up_ref):
            base = pl.multiple_of(i * ROWS, ROWS)
            x = xs[pl.ds(pl.multiple_of(slot * t + base, ROWS), ROWS), :]
            p_s[8:, :] = jnp.dot(x, ws[...].reshape(m * pad, width), preferred_element_type=F32)
            for r in range(ROWS // TM):
                rows = pl.ds(pl.multiple_of(base + r * TM, TM), TM)
                full = pl.ds(pl.multiple_of(slot * t + base + r * TM, TM), TM)
                apart = spread(base + r * TM, t // SEGS)
                if xrel:
                    flags = xs[full, dl:pad].astype(F32)
                    keep = jnp.concatenate([flags] * (LANES // (pad - dl)), axis=1)
                    keep_w[full, :] = keep
                else:
                    keep = keep_w[full, :]
                for k_l, lo, w in lanes:
                    g = []
                    for k in range(3):
                        now = p_s[8 + r * TM : 8 + (r + 1) * TM, group(k, lo, w)]
                        before = p_s[7 + r * TM : 7 + (r + 1) * TM, group(3 + k, lo, w)]
                        v = now + keep[:, :w] * before + bias_ref[k : k + 1, lo : lo + w]
                        g_ref[k, full, lo : lo + w] = v
                        g.append(v)
                    f, intake = both(g[1])
                    o, _ = both(g[2])
                    d = keep[:, :w] * f
                    d_s[slot, k_l, apart, :w] = d
                    s_s[slot, k_l, apart, :w] = intake * jnp.tanh(g[0])
                    q_s[slot, k_l, apart, :w] = d * (load_up(up_ref, rows, slot * up_at + lo, w) * o)
            p_s[7:8, :] = p_s[ROWS + 7 : ROWS + 8, :]
            return 0

        lax.fori_loop(0, t // ROWS, tile, 0)
    span = t // SEGS
    chains = [(slot, k_l) for slot in range(2) for k_l, _, _ in lanes]
    one, zero = jnp.ones((SEGS, LANES), F32), jnp.zeros((SEGS, LANES), F32)

    def step(j, carry):
        at, back = pl.ds(j, SEGS, stride=span + GAP), pl.ds(span - 1 - j, SEGS, stride=span + GAP)
        new = []
        for (slot, k_l), (pa, ps, pr) in zip(chains, carry):
            d = d_s[slot, k_l, at, :]
            new.append(
                (
                    pa * d,
                    d * ps + s_s[slot, k_l, at, :],
                    d_s[slot, k_l, back, :] * pr + q_s[slot, k_l, back, :],
                )
            )
        return tuple(new)

    res = lax.fori_loop(0, span, step, tuple((one, zero, zero) for _ in chains), unroll=4)
    for (slot, k_l), triple in zip(chains, res):
        _, lo, w = lanes[k_l]
        for k in range(3):
            seg_s[k] = triple[k]
            seg_ref[slot, k, :, lo : lo + w] = triple[k][:, :w]
        pa, ps, pr = one[:1], zero[:1], zero[:1]
        for k in range(SEGS):
            d = seg_s[0, k : k + 1, :]
            ps = d * ps + seg_s[1, k : k + 1, :]
            pa = pa * d
            r = SEGS - 1 - k
            pr = seg_s[0, r : r + 1, :] * pr + seg_s[2, r : r + 1, :]
        for k, v in enumerate((pa, ps, pr)):
            tot_ref[slot, k : k + 1, lo : lo + w] = v[:, :w]
    for copy in outs:
        copy.wait()


def after(v, *needs):
    return lax.optimization_barrier((v, *needs))[0]


def gates_and_totals(dims, up_at, place, w, wrel, x, xrel, bias, ups, keep_w=None):
    n, m, dw, dl, t, c = dims
    pad = ceil_to(dl, LANES)
    lt = len(cuts(c))
    width = 6 * c
    plan = (n, m, dw, dl, t, c, up_at, tuple(wrel), tuple(xrel))
    shape = jax.ShapeDtypeStruct
    outs = [shape((3, 2 * t, c), F32), shape((2, 3, SEGS, c), F32), shape((2, 3, c), F32)]
    specs = [VMEM_SPEC] * 3
    if xrel:
        outs += [shape((2 * t, m * pad), BF), shape((2 * EDGE, m * pad), BF), shape((2 * t, LANES), F32)]
        specs += [ANY_SPEC, ANY_SPEC, VMEM_SPEC]
    outs.append(shape((m, pad, width), BF))
    specs.append(ANY_SPEC)
    return pl.pallas_call(
        functools.partial(gates_kernel, plan),
        in_specs=[SMEM_SPEC] + [ANY_SPEC] * (len(w) + len(x)) + [VMEM_SPEC] * (3 if xrel else 4),
        out_specs=specs,
        out_shape=outs,
        scratch_shapes=[
            pltpu.VMEM((2 * t, m * pad), BF),
            pltpu.VMEM((2 * EDGE, m * pad), BF),
            pltpu.VMEM((m, pad, width), BF),
            pltpu.VMEM((ROWS + 8, width), F32),
            pltpu.VMEM((2, lt, t + SEGS * GAP, LANES), F32),
            pltpu.VMEM((2, lt, t + SEGS * GAP, LANES), F32),
            pltpu.VMEM((2, lt, t + SEGS * GAP, LANES), F32),
            pltpu.VMEM((3, SEGS, LANES), F32),
            pltpu.SemaphoreType.DMA((max(2, len(x)),)),
            pltpu.SemaphoreType.DMA((max(1, len(x)),)),
            pltpu.SemaphoreType.DMA((2 * len(w),)),
            pltpu.SemaphoreType.DMA((m + 3,)),
        ],
        compiler_params=params(),
        cost_estimate=TINY,
        name="gates_and_totals",
    )(place, *w, *x, bias, *ups, *([] if xrel else [keep_w]))


def finish_kernel(n, up_at, place, g_ref, up0, up1, keep_ref, seg_ref, all_ref, h0, h1, gg_ref, gf_ref, gp_ref, gb_ref, d_s, s_s, q_s, p_s, c_s):
    t, c = up0.shape
    span = t // SEGS
    lanes = cuts(c)
    heads = n // 4
    hh, ll, pp = place[0], place[1], place[2]
    ups, hids = (up0, up1), (h0, h1)
    for slot in range(2):

        def act(r, _, slot=slot):
            rows = pl.ds(pl.multiple_of(r * TM, TM), TM)
            full = pl.ds(pl.multiple_of(slot * t + r * TM, TM), TM)
            apart = spread(r * TM, span)
            for k_l, lo, w in lanes:
                ch = slice(lo, lo + w)
                f, i = both(g_ref[1, full, ch])
                o, _ = both(g_ref[2, full, ch])
                d_s[slot, k_l, apart, :w] = keep_ref[full, :w] * f
                s_s[slot, k_l, apart, :w] = i * jnp.tanh(g_ref[0, full, ch])
                q_s[slot, k_l, apart, :w] = load_up(ups[slot], rows, slot * up_at + lo, w) * o
            return 0

        lax.fori_loop(0, t // TM, act, 0)
    zrow = jnp.zeros((1, c), F32)
    mine = [(hh * 2 + (ll ^ slot)) * 2 + pp for slot in range(2)]

    def total(block, k):
        p_b, l_b, h_b = block % 2, block // 2 % 2, block // 4
        member = lax.rem(hh - h_b + heads, heads) * 2 + (pp ^ p_b)
        return all_ref[member, ll ^ l_b, k : k + 1, :]

    h, r = zrow, zrow
    h_in, r_in = [zrow, zrow], [zrow, zrow]
    for k in range(n):
        b = n - 1 - k
        h_in = [jnp.where(mine[s] == k, h, h_in[s]) for s in range(2)]
        r_in = [jnp.where(mine[s] == b, r, r_in[s]) for s in range(2)]
        h = total(k, 0) * h + total(k, 1)
        r = total(b, 0) * r + total(b, 2)
    for slot in range(2):
        h, r = h_in[slot], r_in[slot]
        for k in range(SEGS):
            b = SEGS - 1 - k
            for k_l, lo, w in lanes:
                c_s[0, slot, k_l, k : k + 1, :w] = h[:, lo : lo + w]
                c_s[1, slot, k_l, b : b + 1, :w] = r[:, lo : lo + w]
            h = seg_ref[slot, 0, k : k + 1, :] * h + seg_ref[slot, 1, k : k + 1, :]
            r = seg_ref[slot, 0, b : b + 1, :] * r + seg_ref[slot, 2, b : b + 1, :]
    chains = [(slot, k_l) for slot in range(2) for k_l, _, _ in lanes]

    def step(j, carry):
        at, back = pl.ds(j, SEGS, stride=span + GAP), pl.ds(span - 1 - j, SEGS, stride=span + GAP)
        new = []
        for (slot, k_l), (h, r) in zip(chains, carry):
            dh = d_s[slot, k_l, at, :] * h
            h = dh + s_s[slot, k_l, at, :]
            p_s[slot, k_l, at, :] = dh
            s_s[slot, k_l, at, :] = h
            g = q_s[slot, k_l, back, :] + r
            q_s[slot, k_l, back, :] = g
            new.append((h, d_s[slot, k_l, back, :] * g))
        return tuple(new)

    lax.fori_loop(0, span, step, tuple((c_s[0, s, k_l], c_s[1, s, k_l]) for s, k_l in chains), unroll=4)
    sums = [jnp.zeros((8, w), F32) for _, _, w in lanes for _ in range(3)]
    top = lax.broadcasted_iota(jnp.int32, (EDGE, LANES), 0) == 0
    gp_ref[...] = jnp.zeros(gp_ref.shape, BF)
    for slot in range(2):

        def out(i, state, slot=slot):
            acc, nxt = state
            r = t // TM - 1 - i
            rows = pl.ds(pl.multiple_of(r * TM, TM), TM)
            full = pl.ds(pl.multiple_of(slot * t + r * TM, TM), TM)
            apart = spread(r * TM, span)
            last = lax.broadcasted_iota(jnp.int32, (TM, LANES), 0) == TM - 1
            new, first = [], []
            for k_l, lo, w in lanes:
                ch = slice(lo, lo + w)
                f, intake = both(g_ref[1, full, ch])
                o, cl = both(g_ref[2, full, ch])
                z = jnp.tanh(g_ref[0, full, ch])
                keep = keep_ref[full, :w]
                gs = q_s[slot, k_l, apart, :w]
                oh = o * s_s[slot, k_l, apart, :w]
                hids[slot][rows, ch] = oh.astype(BF)
                gi = gs * intake
                grads = (
                    gi * (1.0 - z * z),
                    gi * (p_s[slot, k_l, apart, :w] - f * z),
                    load_up(ups[slot], rows, slot * up_at + lo, w) * oh * cl,
                )
                for k, v in enumerate(grads):
                    gg_ref[full, group(k, lo, w)] = v.astype(BF)
                    kept = keep * v
                    moved = jnp.where(last[:, :w], nxt[len(new)], pltpu.roll(kept, TM - 1, 0))
                    gg_ref[full, group(3 + k, lo, w)] = moved.astype(BF)
                    first.append(kept[:1])
                    new.append(acc[len(new)] + jnp.sum(v.reshape(TM // 8, 8, w), axis=0))
            return tuple(new), tuple(first)

        zeros = tuple(jnp.zeros((1, w), F32) for _, _, w in lanes for _ in range(3))
        sums, firsts = lax.fori_loop(0, t // TM, out, (tuple(sums), zeros))
        for k_l, lo, w in lanes:
            for k in range(3):
                gf_ref[slot : slot + 1, group(k, lo, w, 3)] = firsts[3 * k_l + k]
                gp_ref[slot * EDGE : slot * EDGE + EDGE, group(3 + k, lo, w)] = jnp.where(
                    top[:, :w], firsts[3 * k_l + k], 0.0
                ).astype(BF)
    for k_l, lo, w in lanes:
        for k in range(3):
            gb_ref[0:1, k * c + lo : k * c + lo + w] = jnp.sum(sums[3 * k_l + k], axis=0, keepdims=True)


def finish(n, up_at, place, gates, ups, keep_w, seg, every):
    t, c = ups[0].shape
    lt = len(cuts(c))
    shape = jax.ShapeDtypeStruct
    return pl.pallas_call(
        functools.partial(finish_kernel, n, up_at),
        in_specs=[SMEM_SPEC] + [VMEM_SPEC] * 6,
        out_shape=[
            shape((t, c), BF),
            shape((t, c), BF),
            shape((2 * t, 6 * c), BF),
            shape((2, 3 * c), F32),
            shape((2 * EDGE, 6 * c), BF),
            shape((1, 3 * c), F32),
        ],
        scratch_shapes=[pltpu.VMEM((2, lt, t + SEGS * GAP, LANES), F32)] * 4 + [pltpu.VMEM((2, 2, lt, SEGS, LANES), F32)],
        compiler_params=params(),
        cost_estimate=TINY,
        name="finish",
    )(place, gates, *ups, keep_w, seg, every)


def wgrad_kernel(dw, place, x_ref, halo_ref, gg_ref, gp_ref, *refs):
    *outs, acc = refs
    over_tokens = (((0,), (0,)), ((), ()))
    v = lax.dot_general(x_ref[...], gg_ref[...], over_tokens, preferred_element_type=F32)
    acc[...] = v + lax.dot_general(halo_ref[...], gp_ref[...], over_tokens, preferred_element_type=F32)
    p = place[2]
    step = pl.program_id(0)
    for k in range(len(outs) // 2):

        @pl.when(step // 2 == k)
        def _(k=k):
            outs[2 * k][0] = acc[pl.ds(pl.multiple_of(p * dw, 16), dw), :].astype(BF)
            outs[2 * k + 1][0] = acc[pl.ds(pl.multiple_of((1 - p) * dw, 16), dw), :].astype(BF)


def weight_grads(heads, dw, pad, place, x_all, halo, gg, gp):
    width = gg.shape[1]

    def lanes(i, at):
        kh = lax.rem(i // 2 + 1, heads)
        return (0, lax.rem(at[0] + kh, heads) * 2 + (at[1] ^ (1 - lax.rem(i, 2))))

    def out(k):
        return pl.BlockSpec((1, dw, width), lambda i, at: (jnp.clip(i - 2 * k, 0, 1), 0, 0))

    whole = lambda i, at: (0, 0)
    res = pl.pallas_call(
        functools.partial(wgrad_kernel, dw),
        grid_spec=pltpu.PrefetchScalarGridSpec(
            num_scalar_prefetch=1,
            grid=(2 * heads,),
            in_specs=[
                pl.BlockSpec((x_all.shape[0], pad), lanes),
                pl.BlockSpec((halo.shape[0], pad), lanes),
                pl.BlockSpec(gg.shape, whole),
                pl.BlockSpec(gp.shape, whole),
            ],
            out_specs=[out(k) for k in range(heads) for _ in range(2)],
            scratch_shapes=[pltpu.VMEM((pad, width), F32)],
        ),
        out_shape=[jax.ShapeDtypeStruct((2, dw, width), BF)] * (2 * heads),
        compiler_params=params(),
        cost_estimate=TINY,
        name="weight_grads",
    )(place, x_all, halo, gg, gp)
    return [((k + 1) % heads, res[2 * k], res[2 * k + 1]) for k in range(heads)]


def xgrad_kernel(place, *refs):
    count = (len(refs) - 5) // 4
    gg_in, nx, w_in = refs[:count], refs[count : 2 * count], refs[2 * count : 3 * count]
    outs = refs[3 * count : 3 * count + 4]
    gg_s, sem = refs[3 * count + 4 : 4 * count + 4], refs[4 * count + 4]
    i, turn = pl.program_id(0), pl.program_id(1)
    t = gg_s[0].shape[0] // 2

    @pl.when((i == 0) & (turn == 0))
    def _():
        copies = [pltpu.make_async_copy(gg_in[k], gg_s[k], sem.at[k]) for k in range(count)]
        for copy in copies:
            copy.start()
        for k, copy in enumerate(copies):
            copy.wait()
            for _, lo, w in cuts(nx[k].shape[1] // 3):
                last = lax.broadcasted_iota(jnp.int32, (EDGE, 3 * w), 0) == EDGE - 1
                there = slice(6 * lo + 3 * w, 6 * lo + 6 * w)
                for slot in range(2):
                    rows = slice((slot + 1) * t - EDGE, (slot + 1) * t)
                    old = gg_s[k][rows, there].astype(F32)
                    new = nx[k][slot : slot + 1, 3 * lo : 3 * lo + 3 * w]
                    gg_s[k][rows, there] = jnp.where(last, new, old).astype(BF)

    rows = pl.ds(pl.multiple_of((1 - turn) * t, t), t)
    v = 0.0
    for k in range(count):
        v = v + lax.dot_general(
            gg_s[k][rows, :], w_in[k][0], (((1,), (1,)), ((), ())), preferred_element_type=F32
        )
    v = v.astype(BF)
    for k in range(4):

        @pl.when((turn == k // 2) & ((i < 2) == (k % 2 == 0)))
        def _(k=k):
            outs[k][0] = v


def input_grads(place, ggs, nexts, ws):
    count = len(ggs)
    t = ggs[0].shape[0] // 2
    m, pad, _ = ws[0].shape
    order = lambda i: jnp.where(i < 2, 2 * i + 1, 2 * i - 4)
    sent = pl.BlockSpec((1, t, pad), lambda i, turn, at: (jnp.minimum(i, 1), 0, 0))
    kept = pl.BlockSpec((1, t, pad), lambda i, turn, at: (jnp.maximum(i - 2, 0), 0, 0))
    return pl.pallas_call(
        xgrad_kernel,
        grid_spec=pltpu.PrefetchScalarGridSpec(
            num_scalar_prefetch=1,
            grid=(m, 2),
            in_specs=[ANY_SPEC] * count
            + [pl.BlockSpec(v.shape, lambda i, turn, at: (0, 0)) for v in nexts]
            + [pl.BlockSpec((1, pad, w.shape[2]), lambda i, turn, at: (order(i), 0, 0)) for w in ws],
            out_specs=[sent, kept, sent, kept],
            scratch_shapes=[pltpu.VMEM(gg.shape, BF) for gg in ggs] + [pltpu.SemaphoreType.DMA((count,))],
        ),
        out_shape=[jax.ShapeDtypeStruct((2, t, pad), BF)] * 4,
        compiler_params=params(),
        cost_estimate=TINY,
        name="input_grads",
    )(place, *ggs, *nexts, *ws)


def join_kernel(*refs):
    *terms, out = refs
    v = terms[0][...].astype(F32)
    for ref in terms[1:]:
        v = v + ref[...].astype(F32)
    out[...] = v.astype(BF)


def join(terms, urgency):
    arrays = [v for v, _ in terms]
    shape = arrays[0].shape[-2:]
    steps = 2 if shape[0] % 32 == 0 else 1
    blocks = shape[0] // steps

    def spec(v, at):
        if at is None:
            return pl.BlockSpec((blocks, shape[1]), lambda i: (i, 0))
        return pl.BlockSpec((None, blocks, shape[1]), lambda i, at=at: (at, i, 0))

    return pl.pallas_call(
        join_kernel,
        grid=(steps,),
        in_specs=[spec(v, at) for v, at in terms],
        out_specs=pl.BlockSpec((blocks, shape[1]), lambda i: (i, 0)),
        out_shape=jax.ShapeDtypeStruct(shape, BF),
        compiler_params=params(),
        cost_estimate=pl.CostEstimate(flops=0, bytes_accessed=urgency * 3690000, transcendentals=0),
        name="join",
    )(*arrays)


def unpack_w_kernel(widths, place, *refs):
    count = len(widths)
    outs = refs[2 * count :]
    low = place[1] == 0
    for tap in range(2):
        for k in range(3):
            mine, other = [], []
            for i, c in enumerate(widths):
                for _, lo, w in cuts(c):
                    mine.append(refs[2 * i][:, group(tap * 3 + k, lo, w)].astype(F32))
                    other.append(refs[2 * i + 1][:, group(tap * 3 + k, lo, w)].astype(F32))
            mine, other = jnp.concatenate(mine, axis=1), jnp.concatenate(other, axis=1)
            outs[tap][k] = jnp.concatenate([jnp.where(low, mine, other), jnp.where(low, other, mine)], axis=1)


def unpack_weights(widths, place, pairs):
    rows = pairs[0].shape[0]
    shape = jax.ShapeDtypeStruct((3, rows, 2 * sum(widths)), F32)
    return pl.pallas_call(
        functools.partial(unpack_w_kernel, widths),
        in_specs=[SMEM_SPEC] + [VMEM_SPEC] * len(pairs),
        out_shape=[shape, shape],
        compiler_params=params(),
        cost_estimate=TINY,
        name="unpack_weights",
    )(place, *pairs)


def unpack_h_kernel(widths, place, *refs):
    out_ref = refs[-1]
    low = place[1] == 0

    def body(r, _):
        rows = pl.ds(pl.multiple_of(r * TM, TM), TM)
        mine = jnp.concatenate([refs[i][rows, :].astype(F32) for i in range(len(widths))], axis=1)
        other = refs[len(widths)][rows, :].astype(F32)
        both_halves = jnp.concatenate([jnp.where(low, mine, other), jnp.where(low, other, mine)], axis=1)
        out_ref[rows, :] = both_halves.astype(BF)
        return 0

    lax.fori_loop(0, out_ref.shape[0] // TM, body, 0)


def unpack_hidden(widths, place, mine, other):
    t = other.shape[0]
    return pl.pallas_call(
        functools.partial(unpack_h_kernel, widths),
        in_specs=[SMEM_SPEC] + [VMEM_SPEC] * (len(mine) + 1),
        out_shape=jax.ShapeDtypeStruct((t, 2 * sum(widths)), BF),
        compiler_params=params(),
        cost_estimate=TINY,
        name="unpack_hidden",
    )(place, *mine, other)


def on_device(layer_input, keep, w_now, w_prev, bias, grad_out):
    n, m = lax.axis_size("seq"), lax.axis_size("gate")
    heads = n // 4
    s, g = lax.axis_index("seq"), lax.axis_index("gate")
    h, l, p, a, b = s // 4, s // 2 % 2, s % 2, g // 2, g % 2
    place = jnp.stack([h, l, p, a, b]).astype(jnp.int32)
    t, dl = layer_input.shape
    dw = w_now.shape[1]
    half = dl // 2
    pad = ceil_to(dl, LANES)
    widths = tuple(w for w in WIDTHS) if sum(WIDTHS) == half else (half,)
    low = l == 0

    def seq_to(v, kh, d_l, d_p):
        route = []
        for i in range(n):
            i_h, i_l, i_p = i // 4, i // 2 % 2, i % 2
            route.append((i, ((i_h + kh) % heads * 2 + (i_l ^ d_l)) * 2 + (i_p ^ d_p)))
        return lax.ppermute(v, "seq", route)

    def gate_to(v, d_a, d_b):
        return lax.ppermute(v, "gate", [(i, i ^ (d_a * 2 + d_b)) for i in range(m)])

    group = [(kh, d_p) for kh in range(heads) for d_p in range(2)]

    packed = pack_weights(widths, 0, place, w_now, w_prev)
    behind = lax.ppermute(layer_input[-1:], "seq", [(i, i + 1) for i in range(n - 1)])
    flags = jnp.broadcast_to(jnp.pad(keep, (0, EDGE)).astype(BF)[:, None], (t + EDGE, pad - dl))
    rows = jnp.concatenate([layer_input, jnp.pad(behind, ((0, EDGE - 1), (0, 0)))], axis=0)
    x0 = after(jnp.concatenate([rows, flags], axis=1), packed[0])
    def share_w(pair, *needs):
        got = {(0, 0): pair, (0, 1): seq_to(pair, 0, 0, 1)}
        for kh in range(1, heads):
            got[kh, 0] = seq_to(after(pair, *needs) if needs else pair, kh, 0, 0)
        return got

    def finish_share(got, *needs):
        for kh in range(1, heads):
            got[kh, 1] = seq_to(after(got[kh, 0], *needs) if needs else got[kh, 0], 0, 0, 1)

    def weights_in(got, c):
        if dw % 16 == 0:
            return [got[r] for r in got], list(got)
        stacked = jnp.stack([got[kh, d_p][d_l] for kh in range(heads) for d_l in range(2) for d_p in range(2)])
        blocks = jnp.arange(n)
        rel = (((h - blocks // 4) % heads) * 2 + (l ^ (blocks // 2 % 2))) * 2 + (p ^ (blocks % 2))
        whole = jnp.take(stacked, rel, axis=0).reshape(m, dl, 6 * c)
        return [jnp.pad(whole, ((0, 0), (0, pad - dl), (0, 0)))], []

    half_bias = jnp.where(low, bias[:, :half], bias[:, half:])
    count = len(widths)
    spans = list(offsets(widths))
    near = seq_to(packed[1], 0, 1, 0)
    got = [share_w(jnp.stack([packed[0], near]))]
    y0 = gate_to(x0, 1, 0)
    x1 = seq_to(after(x0, near), 0, 1, 0)
    first_p = got[0][0, 1]
    up_packed = pack_up(widths, place, after(grad_out, x0))
    ups = [[up_packed[0], seq_to(after(up_packed[1], near), 0, 1, 0)]]
    hop = [got[0][kh, 0] for kh in range(1, heads)]
    c0, cy0 = gate_to(after(x0, y0, first_p, *hop), 0, 1), gate_to(after(y0, first_p, *hop), 0, 1)
    x1_here = after(x1, y0, first_p)
    y1, c1 = gate_to(x1_here, 1, 0), gate_to(x1_here, 0, 1)
    finish_share(got[0])
    for i in range(1, count):
        packed = pack_weights(widths, i, place, after(w_now, near), w_prev)
        near = seq_to(packed[1], 0, 1, 0)
        got.append(share_w(jnp.stack([packed[0], near]), c1, *[got[i - 1][kh, 0] for kh in range(1, heads)]))
        ups.append([up_packed[2 * i], seq_to(after(up_packed[2 * i + 1], near), 0, 1, 0)])
    cy1 = gate_to(after(y1, ups[0][1], *[got[0][kh, 1] for kh in range(1, heads)]), 0, 1)
    xs = {(0, 0, 0): x0, (0, 1, 0): y0, (0, 0, 1): c0, (0, 1, 1): cy0}
    xs |= {(1, 0, 0): x1, (1, 1, 0): y1, (1, 0, 1): c1, (1, 1, 1): cy1}
    hidden_mine, hidden_other, grads, wide_w, g_first, g_bias, w_pairs = [], [], [], [], [], [], []

    def spread_totals(tot):
        return jnp.stack([tot if r == (0, 0) else seq_to(tot, r[0], 0, r[1]) for r in group])

    def weight_parts(gg, gp, *needs):
        if dw % 16 == 0 and n == 2 * m:
            return weight_grads(heads, dw, pad, place, x_all, halo, gg, after(gp, *needs) if needs else gp)
        dots = jnp.einsum("td,tn->dn", x_all, gg, preferred_element_type=F32)
        dots = dots + jnp.einsum("td,tn->dn", halo, gp, preferred_element_type=F32)
        v = dots.astype(BF).reshape(m, pad, -1)[:, :dl].reshape(heads, 2, 2, dw, gg.shape[1])
        away = jnp.where(p == 0, v[:, :, 1], v[:, :, 0])
        here = jnp.where(p == 0, v[:, :, 0], v[:, :, 1])

        def block(v, kh):
            row = lax.dynamic_index_in_dim(v, (h + kh) % heads, 0, keepdims=False)
            return jnp.where(low, row[::-1], row)

        return [(kh, block(here, kh), block(away, kh)) for kh in list(range(1, heads)) + [0]]

    def over_p(parts, *needs):
        came = []
        for _, _, away in parts:
            came.append(after(seq_to(away, 0, 0, 1), *came[-1:], *needs))
        return [here.astype(F32) + v.astype(F32) for (_, here, _), v in zip(parts, came)]

    def over_h(parts, sums, *needs):
        total = sums[-1]
        for (kh, _, _), v in zip(parts[:-1], sums[:-1]):
            total = total + after(seq_to(v.astype(BF), kh, 0, 0), *needs).astype(F32)
        return total.astype(BF)

    waiting = None
    for i, (at, c) in enumerate(spans):
        dims = (n, m, dw, dl, t, c)
        bias_i = half_bias[:, at : at + c]
        if i > 0:
            finish_share(got[i], every, ups[i][1])
        w_in, wrel = weights_in(got[i], c)
        if i == 0:
            xrel = list(xs)
            gates, seg, tot, x_all, halo, keep_w, w_rel = gates_and_totals(
                dims, 0, place, w_in, wrel, [xs[r] for r in xrel], xrel, bias_i, ups[i]
            )
        else:
            w_in[0] = after(w_in[0], *[v[2] for v in waiting[:-1]])
            gates, seg, tot, w_rel = gates_and_totals(
                dims, 0, place, w_in, wrel, [x_all, halo], [], bias_i, ups[i], keep_w
            )
        every = spread_totals(after(tot, *[g[0, 1] for g in got[i + 1 : i + 2]]) if i + 1 < count else tot)
        wide_w.append(w_rel)
        if i > 0:
            (kh0, here0, away0), *others = waiting[::-1]
            others = others[::-1]
            sums = over_p(others, tot)
            every_now = after(every, *sums)
            h_sums = [after(v, every) for v in sums]
            (near_sum,) = over_p([(kh0, here0, after(away0, every))])
            h_sums.append(near_sum)
            every = every_now
        h0, h1, gg, gf, gp, gb = finish(n, 0, place, gates, ups[i], keep_w, seg, every)
        hidden_mine.append(h0)
        hidden_other.append(h1)
        g_first.append(gf)
        g_bias.append(gb)
        if i == count - 1:
            parts = jnp.concatenate([jnp.concatenate(g_first, axis=1), jnp.concatenate(g_bias, axis=1)], axis=0)
            around = [parts if r == (0, 0) else seq_to(parts, r[0], 0, r[1]) for r in group]
            hidden_came = seq_to(after(jnp.concatenate(hidden_other, axis=1), parts), 0, 1, 0)
        needs = list(around) if i == count - 1 else []
        if i > 0:
            total = over_h(waiting, h_sums)
            needs.append(total)
        waiting_next = weight_parts(gg, gp)
        if needs:
            waiting_next = [(kh, here, after(away, *needs)) for kh, here, away in waiting_next]
        if i > 0:
            w_pairs += [total[1], seq_to(total[0], 0, 1, 0)]
        waiting = waiting_next
        grads.append(gg)
    around = jnp.stack(around)

    full_bias = jnp.sum(around[:, 2], axis=0)
    nexts = []
    for slot in range(2):
        block_id = (h * 2 + (l ^ slot)) * 2 + p + 1
        n_h, n_l, n_p = block_id // 4, block_id // 2 % 2, block_id % 2
        member = ((h - n_h) % heads) * 2 + (p ^ n_p)
        row = lax.dynamic_index_in_dim(around, member, 0, keepdims=False)
        row = lax.dynamic_index_in_dim(row, l ^ n_l, 0, keepdims=False)
        nexts.append(jnp.where(block_id < n, row, jnp.zeros_like(row)))
    nexts = jnp.stack(nexts)
    nexts = [nexts[:, 3 * at : 3 * (at + c)] for at, c in spans]
    bias_half = []
    at = 0
    for c in widths:
        bias_half.append(full_bias[at : at + 3 * c].reshape(3, c))
        at += 3 * c
    bias_half = jnp.concatenate(bias_half, axis=1)
    bias_other = seq_to(bias_half, 0, 1, 0)
    nexts[0] = after(nexts[0], *[v[2] for v in waiting])
    sent1, kept1, sent0, kept0 = input_grads(place, grads, nexts, wide_w)
    p_came = []
    for v in waiting:
        p_came.append(after(seq_to(v[2], 0, 0, 1), *p_came[-1:]))
    sent1, sent0, *_ = lax.optimization_barrier((sent1, sent0, p_came[0], hidden_came, bias_other, *w_pairs))
    c_came1, c_came0 = gate_to(sent1, 0, 1), gate_to(sent0, 0, 1)
    farther = [join([(here, 0), (p_came[k], 0)], LATER) for k, (_, here, _) in enumerate(waiting[:-1])]
    c_came1 = after(c_came1, *farther)
    h_came = [seq_to(v, waiting[k][0], 0, 0) for k, v in enumerate(farther)]
    y_came1 = gate_to(join([(kept1, 1), (c_came1, 1)], LATER), 1, 0)
    total = join([(waiting[-1][1], 0), (p_came[-1], 0)] + [(v, None) for v in h_came], LATER)
    l_total = seq_to(total, 0, 1, 0)
    x_part = join([(kept1, 0), (c_came1, 0), (after(y_came1, total), None)], LATER)
    l_came = seq_to(x_part, 0, 1, 0)
    c_came0 = after(c_came0, x_part)
    y_came0 = gate_to(join([(kept0, 1), (c_came0, 1)], LATER), 1, 0)
    rest = [join([(here, 1), (p_came[k], 1)], LATER) for k, (_, here, _) in enumerate(waiting[:-1])]
    h_rest = [seq_to(after(v, y_came1, total), waiting[k][0], 0, 0) for k, v in enumerate(rest)]
    grad_x = kept0[0].astype(F32) + c_came0[0].astype(F32) + y_came0.astype(F32) + l_came.astype(F32)
    grad_x = grad_x[:, :dl].astype(BF)
    h_rest = [after(v, grad_x) for v in h_rest]
    total = join([(waiting[-1][1], 1), (p_came[-1], 1)] + [(v, None) for v in h_rest], LATER)
    w_pairs += [total, l_total]

    grad_bias = jnp.concatenate(
        [jnp.where(low, bias_half, bias_other), jnp.where(low, bias_other, bias_half)], axis=1
    )
    hidden = unpack_hidden(widths, place, hidden_mine, hidden_came)
    grad_now, grad_prev = unpack_weights(widths, place, w_pairs)
    return hidden, grad_x, grad_now, grad_prev, grad_bias


def solution(mesh):
    tokens, matrix = P("seq", "gate"), P(None, "seq", "gate")
    return jax.shard_map(
        on_device,
        mesh=mesh,
        in_specs=(tokens, P("seq"), matrix, matrix, P(None, "gate"), tokens),
        out_specs=(tokens, tokens, matrix, matrix, P(None, "gate")),
        check_vma=False,
    )
```

```python
import functools

import jax
import jax.numpy as jnp
from jax import lax
from jax.experimental import pallas as pl
from jax.experimental.pallas import tpu as pltpu
from jax.sharding import PartitionSpec as P

F32 = jnp.float32
BF = jnp.bfloat16
SEGS = 8
LANES = 128
TM = 64
ROWS = 256
EDGE = 16
GAP = 8
VMEM = 62 << 20
WIDTHS = (128, 160)


def ceil_to(value, unit):
    return -(-value // unit) * unit


def both(g):
    e = jnp.exp(-jnp.abs(g))
    r = 1.0 / (1.0 + e)
    er = e * r
    pos = g >= 0
    return jnp.where(pos, r, er), jnp.where(pos, er, r)


def group(k, lo, w, count=6):
    return slice(count * lo + k * w, count * lo + (k + 1) * w)


def load_up(ref, rows, lo, w):
    return ref[rows, lo : lo + w].astype(F32)


def spread(row, span):
    return pl.ds(pl.multiple_of(row + row // span * GAP, 8), TM)


def cuts(c):
    return [(i, i * LANES, min(LANES, c - i * LANES)) for i in range(-(-c // LANES))]


def params():
    return pltpu.CompilerParams(vmem_limit_bytes=VMEM)


URGENT, LATER = 100, 50
TINY = pl.CostEstimate(flops=1 << 10, bytes_accessed=1 << 10, transcendentals=0)
SMEM_SPEC = pl.BlockSpec(memory_space=pltpu.SMEM)
VMEM_SPEC = pl.BlockSpec(memory_space=pltpu.VMEM)
ANY_SPEC = pl.BlockSpec(memory_space=pl.ANY)


def offsets(widths):
    at = 0
    for w in widths:
        yield at, w
        at += w


def pack_w_kernel(widths, share, place, now_ref, prev_ref, *outs):
    half = now_ref.shape[2] // 2
    low = place[1] == 0
    for tap, ref in enumerate((now_ref, prev_ref)):
        for k in range(3):
            v = ref[k].astype(F32)
            mine = jnp.where(low, v[:, :half], v[:, half:])
            other = jnp.where(low, v[:, half:], v[:, :half])
            at, c = list(offsets(widths))[share]
            for _, lo, w in cuts(c):
                to = group(tap * 3 + k, lo, w)
                outs[0][:, to] = mine[:, at + lo : at + lo + w].astype(BF)
                outs[1][:, to] = other[:, at + lo : at + lo + w].astype(BF)


def pack_weights(widths, share, place, w_now, w_prev):
    rows, w = w_now.shape[1], widths[share]
    return pl.pallas_call(
        functools.partial(pack_w_kernel, widths, share),
        in_specs=[SMEM_SPEC, VMEM_SPEC, VMEM_SPEC],
        out_shape=[jax.ShapeDtypeStruct((rows, 6 * w), BF)] * 2,
        compiler_params=params(),
        cost_estimate=TINY,
        name="pack_weights",
    )(place, w_now, w_prev)


def pack_up_kernel(widths, place, up_ref, *outs):
    half = up_ref.shape[1] // 2
    low = place[1] == 0

    def body(r, _):
        rows = pl.ds(pl.multiple_of(r * TM, TM), TM)
        v = up_ref[rows, :].astype(F32)
        mine = jnp.where(low, v[:, :half], v[:, half:])
        other = jnp.where(low, v[:, half:], v[:, :half])
        for i, (at, w) in enumerate(offsets(widths)):
            outs[2 * i][rows, :] = mine[:, at : at + w].astype(BF)
            outs[2 * i + 1][rows, :w] = other[:, at : at + w].astype(BF)
        return 0

    lax.fori_loop(0, up_ref.shape[0] // TM, body, 0)


def pack_up(widths, place, grad_out):
    t = grad_out.shape[0]
    return pl.pallas_call(
        functools.partial(pack_up_kernel, widths),
        in_specs=[SMEM_SPEC, VMEM_SPEC],
        out_shape=[jax.ShapeDtypeStruct((t, w), BF) for v in widths for w in (v, ceil_to(v, LANES))],
        compiler_params=params(),
        cost_estimate=TINY,
        name="pack_up",
    )(place, grad_out)


def gates_kernel(plan, place, *refs):
    n, m, dw, dl, t, c, up_at, wrel, xrel = plan
    n_w, n_x = len(wrel) or 1, len(xrel) or 1
    w_in, refs = refs[:n_w], refs[n_w:]
    x_in, refs = refs[:n_x], refs[n_x:]
    if not xrel:
        halo_in, refs = refs[0], refs[1:]
    bias_ref, up0, up1 = refs[:3]
    refs = refs[3:]
    if not xrel:
        keep_w, refs = refs[0], refs[1:]
    g_ref, seg_ref, tot_ref, refs = refs[0], refs[1], refs[2], refs[3:]
    if xrel:
        x_out, halo_out, keep_w, refs = refs[0], refs[1], refs[2], refs[3:]
    w_out, refs = refs[0], refs[1:]
    xs, halo, ws, p_s, d_s, s_s, q_s, seg_s, xsem, hsem, wsem, osem = refs
    pad = ws.shape[1]
    width = ws.shape[2]
    wide = n // m
    h, l, p, a, b = (place[i] for i in range(5))
    heads = n // 4
    copies = []
    if wrel:
        for i, (kh, d_p) in enumerate(wrel):
            for d_l in range(2):
                block = (lax.rem(h - kh + heads, heads) * 2 + (l ^ d_l)) * 2 + (p ^ d_p)
                at = pl.multiple_of(lax.rem(block, wide) * dw, 16)
                copies.append(
                    pltpu.make_async_copy(
                        w_in[i].at[d_l], ws.at[block // wide, pl.ds(at, dw), :], wsem.at[2 * i + d_l]
                    )
                )
        if pad > dl:
            for g in range(m):
                ws[g, dl:, :] = jnp.zeros((pad - dl, width), BF)
    else:
        copies.append(pltpu.make_async_copy(w_in[0], ws, wsem.at[0]))
    xcopies = [[], []]
    if xrel:
        for i, (slot, d_a, d_b) in enumerate(xrel):
            at = pl.multiple_of(((a ^ d_a) * 2 + (b ^ d_b)) * pad, LANES)
            xcopies[slot].append(
                pltpu.make_async_copy(
                    x_in[i].at[pl.ds(0, t)], xs.at[pl.ds(slot * t, t), pl.ds(at, pad)], xsem.at[i]
                )
            )
            copies.append(
                pltpu.make_async_copy(
                    x_in[i].at[pl.ds(t, EDGE)], halo.at[pl.ds(slot * EDGE, EDGE), pl.ds(at, pad)], hsem.at[i]
                )
            )
    else:
        for slot in range(2):
            rows = pl.ds(slot * t, t)
            xcopies[slot].append(pltpu.make_async_copy(x_in[0].at[rows], xs.at[rows], xsem.at[slot]))
        copies.append(pltpu.make_async_copy(halo_in, halo, hsem.at[0]))
    for copy in copies + xcopies[0] + xcopies[1]:
        copy.start()
    for copy in copies:
        copy.wait()
    outs = []
    for g in range(m):
        outs.append(pltpu.make_async_copy(ws.at[g], w_out.at[(a * 2 + b) ^ g], osem.at[g]))
    for copy in outs:
        copy.start()
    lanes = cuts(c)
    weights = ws[...].reshape(m * pad, width)
    if xrel:
        out = pltpu.make_async_copy(halo, halo_out, osem.at[m + 2])
        out.start()
        outs.append(out)
    edge = jnp.dot(halo[...], weights, preferred_element_type=F32)
    for slot, up_ref in enumerate((up0, up1)):
        for copy in xcopies[slot]:
            copy.wait()
        if xrel:
            rows = pl.ds(slot * t, t)
            out = pltpu.make_async_copy(xs.at[rows], x_out.at[rows], osem.at[m + slot])
            out.start()
            outs.append(out)
        p_s[7:8, :] = edge[slot * EDGE : slot * EDGE + 1, :]

        def tile(i, _, slot=slot, up_ref=up_ref):
            base = pl.multiple_of(i * ROWS, ROWS)
            x = xs[pl.ds(pl.multiple_of(slot * t + base, ROWS), ROWS), :]
            p_s[8:, :] = jnp.dot(x, ws[...].reshape(m * pad, width), preferred_element_type=F32)
            for r in range(ROWS // TM):
                rows = pl.ds(pl.multiple_of(base + r * TM, TM), TM)
                full = pl.ds(pl.multiple_of(slot * t + base + r * TM, TM), TM)
                apart = spread(base + r * TM, t // SEGS)
                if xrel:
                    flags = xs[full, dl:pad].astype(F32)
                    keep = jnp.concatenate([flags] * (LANES // (pad - dl)), axis=1)
                    keep_w[full, :] = keep
                else:
                    keep = keep_w[full, :]
                for k_l, lo, w in lanes:
                    g = []
                    for k in range(3):
                        now = p_s[8 + r * TM : 8 + (r + 1) * TM, group(k, lo, w)]
                        before = p_s[7 + r * TM : 7 + (r + 1) * TM, group(3 + k, lo, w)]
                        v = now + keep[:, :w] * before + bias_ref[k : k + 1, lo : lo + w]
                        g_ref[k, full, lo : lo + w] = v
                        g.append(v)
                    f, intake = both(g[1])
                    o, _ = both(g[2])
                    d = keep[:, :w] * f
                    d_s[slot, k_l, apart, :w] = d
                    s_s[slot, k_l, apart, :w] = intake * jnp.tanh(g[0])
                    q_s[slot, k_l, apart, :w] = d * (load_up(up_ref, rows, slot * up_at + lo, w) * o)
            p_s[7:8, :] = p_s[ROWS + 7 : ROWS + 8, :]
            return 0

        lax.fori_loop(0, t // ROWS, tile, 0)
    span = t // SEGS
    chains = [(slot, k_l) for slot in range(2) for k_l, _, _ in lanes]
    one, zero = jnp.ones((SEGS, LANES), F32), jnp.zeros((SEGS, LANES), F32)

    def step(j, carry):
        at, back = pl.ds(j, SEGS, stride=span + GAP), pl.ds(span - 1 - j, SEGS, stride=span + GAP)
        new = []
        for (slot, k_l), (pa, ps, pr) in zip(chains, carry):
            d = d_s[slot, k_l, at, :]
            new.append(
                (
                    pa * d,
                    d * ps + s_s[slot, k_l, at, :],
                    d_s[slot, k_l, back, :] * pr + q_s[slot, k_l, back, :],
                )
            )
        return tuple(new)

    res = lax.fori_loop(0, span, step, tuple((one, zero, zero) for _ in chains), unroll=4)
    for (slot, k_l), triple in zip(chains, res):
        _, lo, w = lanes[k_l]
        for k in range(3):
            seg_s[k] = triple[k]
            seg_ref[slot, k, :, lo : lo + w] = triple[k][:, :w]
        pa, ps, pr = one[:1], zero[:1], zero[:1]
        for k in range(SEGS):
            d = seg_s[0, k : k + 1, :]
            ps = d * ps + seg_s[1, k : k + 1, :]
            pa = pa * d
            r = SEGS - 1 - k
            pr = seg_s[0, r : r + 1, :] * pr + seg_s[2, r : r + 1, :]
        for k, v in enumerate((pa, ps, pr)):
            tot_ref[slot, k : k + 1, lo : lo + w] = v[:, :w]
    for copy in outs:
        copy.wait()


def after(v, *needs):
    return lax.optimization_barrier((v, *needs))[0]


def gates_and_totals(dims, up_at, place, w, wrel, x, xrel, bias, ups, keep_w=None):
    n, m, dw, dl, t, c = dims
    pad = ceil_to(dl, LANES)
    lt = len(cuts(c))
    width = 6 * c
    plan = (n, m, dw, dl, t, c, up_at, tuple(wrel), tuple(xrel))
    shape = jax.ShapeDtypeStruct
    outs = [shape((3, 2 * t, c), F32), shape((2, 3, SEGS, c), F32), shape((2, 3, c), F32)]
    specs = [VMEM_SPEC] * 3
    if xrel:
        outs += [shape((2 * t, m * pad), BF), shape((2 * EDGE, m * pad), BF), shape((2 * t, LANES), F32)]
        specs += [ANY_SPEC, ANY_SPEC, VMEM_SPEC]
    outs.append(shape((m, pad, width), BF))
    specs.append(ANY_SPEC)
    return pl.pallas_call(
        functools.partial(gates_kernel, plan),
        in_specs=[SMEM_SPEC] + [ANY_SPEC] * (len(w) + len(x)) + [VMEM_SPEC] * (3 if xrel else 4),
        out_specs=specs,
        out_shape=outs,
        scratch_shapes=[
            pltpu.VMEM((2 * t, m * pad), BF),
            pltpu.VMEM((2 * EDGE, m * pad), BF),
            pltpu.VMEM((m, pad, width), BF),
            pltpu.VMEM((ROWS + 8, width), F32),
            pltpu.VMEM((2, lt, t + SEGS * GAP, LANES), F32),
            pltpu.VMEM((2, lt, t + SEGS * GAP, LANES), F32),
            pltpu.VMEM((2, lt, t + SEGS * GAP, LANES), F32),
            pltpu.VMEM((3, SEGS, LANES), F32),
            pltpu.SemaphoreType.DMA((max(2, len(x)),)),
            pltpu.SemaphoreType.DMA((max(1, len(x)),)),
            pltpu.SemaphoreType.DMA((2 * len(w),)),
            pltpu.SemaphoreType.DMA((m + 3,)),
        ],
        compiler_params=params(),
        cost_estimate=TINY,
        name="gates_and_totals",
    )(place, *w, *x, bias, *ups, *([] if xrel else [keep_w]))


def finish_kernel(n, up_at, place, g_ref, up0, up1, keep_ref, seg_ref, all_ref, *refs):
    count = len(refs) - 11
    before, refs = refs[:count], refs[count:]
    h0, h1, gg_ref, gf_ref, gp_ref, gb_ref, d_s, s_s, q_s, p_s, c_s = refs
    t, c = up0.shape
    span = t // SEGS
    lanes = cuts(c)
    heads = n // 4
    hh, ll, pp = place[0], place[1], place[2]
    ups, hids = (up0, up1), (h0, h1)
    at = 0
    for ref in before:
        h1[:, at : at + ref.shape[1]] = ref[...]
        at += ref.shape[1]
    firsts_at = (0, at)
    for slot in range(2):

        def act(r, _, slot=slot):
            rows = pl.ds(pl.multiple_of(r * TM, TM), TM)
            full = pl.ds(pl.multiple_of(slot * t + r * TM, TM), TM)
            apart = spread(r * TM, span)
            for k_l, lo, w in lanes:
                ch = slice(lo, lo + w)
                f, i = both(g_ref[1, full, ch])
                o, _ = both(g_ref[2, full, ch])
                d_s[slot, k_l, apart, :w] = keep_ref[full, :w] * f
                s_s[slot, k_l, apart, :w] = i * jnp.tanh(g_ref[0, full, ch])
                q_s[slot, k_l, apart, :w] = load_up(ups[slot], rows, slot * up_at + lo, w) * o
            return 0

        lax.fori_loop(0, t // TM, act, 0)
    zrow = jnp.zeros((1, c), F32)
    mine = [(hh * 2 + (ll ^ slot)) * 2 + pp for slot in range(2)]

    def total(block, k):
        p_b, l_b, h_b = block % 2, block // 2 % 2, block // 4
        member = lax.rem(hh - h_b + heads, heads) * 2 + (pp ^ p_b)
        return all_ref[member, ll ^ l_b, k : k + 1, :]

    h, r = zrow, zrow
    h_in, r_in = [zrow, zrow], [zrow, zrow]
    for k in range(n):
        b = n - 1 - k
        h_in = [jnp.where(mine[s] == k, h, h_in[s]) for s in range(2)]
        r_in = [jnp.where(mine[s] == b, r, r_in[s]) for s in range(2)]
        h = total(k, 0) * h + total(k, 1)
        r = total(b, 0) * r + total(b, 2)
    for slot in range(2):
        h, r = h_in[slot], r_in[slot]
        for k in range(SEGS):
            b = SEGS - 1 - k
            for k_l, lo, w in lanes:
                c_s[0, slot, k_l, k : k + 1, :w] = h[:, lo : lo + w]
                c_s[1, slot, k_l, b : b + 1, :w] = r[:, lo : lo + w]
            h = seg_ref[slot, 0, k : k + 1, :] * h + seg_ref[slot, 1, k : k + 1, :]
            r = seg_ref[slot, 0, b : b + 1, :] * r + seg_ref[slot, 2, b : b + 1, :]
    chains = [(slot, k_l) for slot in range(2) for k_l, _, _ in lanes]

    def step(j, carry):
        at, back = pl.ds(j, SEGS, stride=span + GAP), pl.ds(span - 1 - j, SEGS, stride=span + GAP)
        new = []
        for (slot, k_l), (h, r) in zip(chains, carry):
            dh = d_s[slot, k_l, at, :] * h
            h = dh + s_s[slot, k_l, at, :]
            p_s[slot, k_l, at, :] = dh
            s_s[slot, k_l, at, :] = h
            g = q_s[slot, k_l, back, :] + r
            q_s[slot, k_l, back, :] = g
            new.append((h, d_s[slot, k_l, back, :] * g))
        return tuple(new)

    lax.fori_loop(0, span, step, tuple((c_s[0, s, k_l], c_s[1, s, k_l]) for s, k_l in chains), unroll=4)
    sums = [jnp.zeros((8, w), F32) for _, _, w in lanes for _ in range(3)]
    top = lax.broadcasted_iota(jnp.int32, (EDGE, LANES), 0) == 0
    gp_ref[...] = jnp.zeros(gp_ref.shape, BF)
    for slot in range(2):

        def out(i, state, slot=slot):
            acc, nxt = state
            r = t // TM - 1 - i
            rows = pl.ds(pl.multiple_of(r * TM, TM), TM)
            full = pl.ds(pl.multiple_of(slot * t + r * TM, TM), TM)
            apart = spread(r * TM, span)
            last = lax.broadcasted_iota(jnp.int32, (TM, LANES), 0) == TM - 1
            new, first = [], []
            for k_l, lo, w in lanes:
                ch = slice(lo, lo + w)
                f, intake = both(g_ref[1, full, ch])
                o, cl = both(g_ref[2, full, ch])
                z = jnp.tanh(g_ref[0, full, ch])
                keep = keep_ref[full, :w]
                gs = q_s[slot, k_l, apart, :w]
                oh = o * s_s[slot, k_l, apart, :w]
                hids[slot][rows, firsts_at[slot] + lo : firsts_at[slot] + lo + w] = oh.astype(BF)
                gi = gs * intake
                grads = (
                    gi * (1.0 - z * z),
                    gi * (p_s[slot, k_l, apart, :w] - f * z),
                    load_up(ups[slot], rows, slot * up_at + lo, w) * oh * cl,
                )
                for k, v in enumerate(grads):
                    gg_ref[full, group(k, lo, w)] = v.astype(BF)
                    kept = keep * v
                    moved = jnp.where(last[:, :w], nxt[len(new)], pltpu.roll(kept, TM - 1, 0))
                    gg_ref[full, group(3 + k, lo, w)] = moved.astype(BF)
                    first.append(kept[:1])
                    new.append(acc[len(new)] + jnp.sum(v.reshape(TM // 8, 8, w), axis=0))
            return tuple(new), tuple(first)

        zeros = tuple(jnp.zeros((1, w), F32) for _, _, w in lanes for _ in range(3))
        sums, firsts = lax.fori_loop(0, t // TM, out, (tuple(sums), zeros))
        for k_l, lo, w in lanes:
            for k in range(3):
                gf_ref[slot : slot + 1, group(k, lo, w, 3)] = firsts[3 * k_l + k]
                gp_ref[slot * EDGE : slot * EDGE + EDGE, group(3 + k, lo, w)] = jnp.where(
                    top[:, :w], firsts[3 * k_l + k], 0.0
                ).astype(BF)
    for k_l, lo, w in lanes:
        for k in range(3):
            gb_ref[0:1, k * c + lo : k * c + lo + w] = jnp.sum(sums[3 * k_l + k], axis=0, keepdims=True)


def finish(n, up_at, place, gates, ups, keep_w, seg, every, before=()):
    t, c = ups[0].shape
    lt = len(cuts(c))
    shape = jax.ShapeDtypeStruct
    return pl.pallas_call(
        functools.partial(finish_kernel, n, up_at),
        in_specs=[SMEM_SPEC] + [VMEM_SPEC] * (6 + len(before)),
        out_shape=[
            shape((t, c), BF),
            shape((t, ceil_to(c + sum(v.shape[1] for v in before), LANES if before else 1)), BF),
            shape((2 * t, 6 * c), BF),
            shape((2, 3 * c), F32),
            shape((2 * EDGE, 6 * c), BF),
            shape((1, 3 * c), F32),
        ],
        scratch_shapes=[pltpu.VMEM((2, lt, t + SEGS * GAP, LANES), F32)] * 4 + [pltpu.VMEM((2, 2, lt, SEGS, LANES), F32)],
        compiler_params=params(),
        cost_estimate=TINY,
        name="finish",
    )(place, gates, *ups, keep_w, seg, every, *before)


def wgrad_kernel(dw, place, x_ref, halo_ref, gg_ref, gp_ref, *refs):
    *outs, acc = refs
    over_tokens = (((0,), (0,)), ((), ()))
    v = lax.dot_general(x_ref[...], gg_ref[...], over_tokens, preferred_element_type=F32)
    acc[...] = v + lax.dot_general(halo_ref[...], gp_ref[...], over_tokens, preferred_element_type=F32)
    p = place[2]
    step = pl.program_id(0)
    for k in range(len(outs) // 2):

        @pl.when(step // 2 == k)
        def _(k=k):
            outs[2 * k][0] = acc[pl.ds(pl.multiple_of(p * dw, 16), dw), :].astype(BF)
            outs[2 * k + 1][0] = acc[pl.ds(pl.multiple_of((1 - p) * dw, 16), dw), :].astype(BF)


def weight_grads(heads, dw, pad, place, x_all, halo, gg, gp):
    width = gg.shape[1]

    def lanes(i, at):
        kh = lax.rem(i // 2 + 1, heads)
        return (0, lax.rem(at[0] + kh, heads) * 2 + (at[1] ^ (1 - lax.rem(i, 2))))

    def out(k):
        return pl.BlockSpec((1, dw, width), lambda i, at: (jnp.clip(i - 2 * k, 0, 1), 0, 0))

    whole = lambda i, at: (0, 0)
    res = pl.pallas_call(
        functools.partial(wgrad_kernel, dw),
        grid_spec=pltpu.PrefetchScalarGridSpec(
            num_scalar_prefetch=1,
            grid=(2 * heads,),
            in_specs=[
                pl.BlockSpec((x_all.shape[0], pad), lanes),
                pl.BlockSpec((halo.shape[0], pad), lanes),
                pl.BlockSpec(gg.shape, whole),
                pl.BlockSpec(gp.shape, whole),
            ],
            out_specs=[out(k) for k in range(heads) for _ in range(2)],
            scratch_shapes=[pltpu.VMEM((pad, width), F32)],
        ),
        out_shape=[jax.ShapeDtypeStruct((2, dw, width), BF)] * (2 * heads),
        compiler_params=params(),
        cost_estimate=TINY,
        name="weight_grads",
    )(place, x_all, halo, gg, gp)
    return [((k + 1) % heads, res[2 * k], res[2 * k + 1]) for k in range(heads)]


def xgrad_kernel(place, *refs):
    count = (len(refs) - 5) // 4
    gg_in, nx, w_in = refs[:count], refs[count : 2 * count], refs[2 * count : 3 * count]
    outs = refs[3 * count : 3 * count + 4]
    gg_s, sem = refs[3 * count + 4 : 4 * count + 4], refs[4 * count + 4]
    i, turn = pl.program_id(0), pl.program_id(1)
    t = gg_s[0].shape[0] // 2

    @pl.when((i == 0) & (turn == 0))
    def _():
        copies = [pltpu.make_async_copy(gg_in[k], gg_s[k], sem.at[k]) for k in range(count)]
        for copy in copies:
            copy.start()
        for k, copy in enumerate(copies):
            copy.wait()
            for _, lo, w in cuts(nx[k].shape[1] // 3):
                last = lax.broadcasted_iota(jnp.int32, (EDGE, 3 * w), 0) == EDGE - 1
                there = slice(6 * lo + 3 * w, 6 * lo + 6 * w)
                for slot in range(2):
                    rows = slice((slot + 1) * t - EDGE, (slot + 1) * t)
                    old = gg_s[k][rows, there].astype(F32)
                    new = nx[k][slot : slot + 1, 3 * lo : 3 * lo + 3 * w]
                    gg_s[k][rows, there] = jnp.where(last, new, old).astype(BF)

    rows = pl.ds(pl.multiple_of((1 - turn) * t, t), t)
    v = 0.0
    for k in range(count):
        v = v + lax.dot_general(
            gg_s[k][rows, :], w_in[k][0], (((1,), (1,)), ((), ())), preferred_element_type=F32
        )
    v = v.astype(BF)
    for k in range(4):

        @pl.when((turn == k // 2) & ((i < 2) == (k % 2 == 0)))
        def _(k=k):
            outs[k][0] = v


def input_grads(place, ggs, nexts, ws):
    count = len(ggs)
    t = ggs[0].shape[0] // 2
    m, pad, _ = ws[0].shape
    order = lambda i: jnp.where(i < 2, 2 * i + 1, 2 * i - 4)
    sent = pl.BlockSpec((1, t, pad), lambda i, turn, at: (jnp.minimum(i, 1), 0, 0))
    kept = pl.BlockSpec((1, t, pad), lambda i, turn, at: (jnp.maximum(i - 2, 0), 0, 0))
    return pl.pallas_call(
        xgrad_kernel,
        grid_spec=pltpu.PrefetchScalarGridSpec(
            num_scalar_prefetch=1,
            grid=(m, 2),
            in_specs=[ANY_SPEC] * count
            + [pl.BlockSpec(v.shape, lambda i, turn, at: (0, 0)) for v in nexts]
            + [pl.BlockSpec((1, pad, w.shape[2]), lambda i, turn, at: (order(i), 0, 0)) for w in ws],
            out_specs=[sent, kept, sent, kept],
            scratch_shapes=[pltpu.VMEM(gg.shape, BF) for gg in ggs] + [pltpu.SemaphoreType.DMA((count,))],
        ),
        out_shape=[jax.ShapeDtypeStruct((2, t, pad), BF)] * 4,
        compiler_params=params(),
        cost_estimate=TINY,
        name="input_grads",
    )(place, *ggs, *nexts, *ws)


def join_kernel(*refs):
    *terms, out = refs
    v = terms[0][...].astype(F32)
    for ref in terms[1:]:
        v = v + ref[...].astype(F32)
    out[...] = v.astype(BF)


def join(terms, urgency):
    arrays = [v for v, _ in terms]
    shape = arrays[0].shape[-2:]
    steps = 2 if shape[0] % 32 == 0 else 1
    blocks = shape[0] // steps

    def spec(v, at):
        if at is None:
            return pl.BlockSpec((blocks, shape[1]), lambda i: (i, 0))
        return pl.BlockSpec((None, blocks, shape[1]), lambda i, at=at: (at, i, 0))

    return pl.pallas_call(
        join_kernel,
        grid=(steps,),
        in_specs=[spec(v, at) for v, at in terms],
        out_specs=pl.BlockSpec((blocks, shape[1]), lambda i: (i, 0)),
        out_shape=jax.ShapeDtypeStruct(shape, BF),
        compiler_params=params(),
        cost_estimate=pl.CostEstimate(flops=0, bytes_accessed=urgency * 3690000, transcendentals=0),
        name="join",
    )(*arrays)


def unpack_w_kernel(widths, terms, place, *refs):
    count = len(widths)
    outs = refs[-2:]
    last = [
        ref if at is None else ref.at[at] for ref, at in zip(refs[2 * count - 2 :], terms)
    ]
    pieces = [*refs[: 2 * count - 2], None, refs[2 * count - 2 + len(terms)]]
    low = place[1] == 0
    for tap in range(2):
        for k in range(3):
            mine, other = [], []
            for i, c in enumerate(widths):
                for _, lo, w in cuts(c):
                    cols = group(tap * 3 + k, lo, w)
                    if pieces[2 * i] is None:
                        mine.append(functools.reduce(lambda v, ref: v + ref[:, cols].astype(F32), last, 0.0))
                    else:
                        mine.append(pieces[2 * i][:, cols].astype(F32))
                    other.append(pieces[2 * i + 1][:, cols].astype(F32))
            mine, other = jnp.concatenate(mine, axis=1), jnp.concatenate(other, axis=1)
            outs[tap][k] = jnp.concatenate([jnp.where(low, mine, other), jnp.where(low, other, mine)], axis=1)


def unpack_weights(widths, place, pairs, last, other):
    rows = other.shape[0]
    shape = jax.ShapeDtypeStruct((3, rows, 2 * sum(widths)), F32)

    return pl.pallas_call(
        functools.partial(unpack_w_kernel, widths, tuple(at for _, at in last)),
        in_specs=[SMEM_SPEC] + [VMEM_SPEC] * (len(pairs) + len(last) + 1),
        out_shape=[shape, shape],
        compiler_params=params(),
        cost_estimate=TINY,
        name="unpack_weights",
    )(place, *pairs, *[v for v, _ in last], other)


def unpack_h_kernel(widths, place, *refs):
    out_ref = refs[-1]
    low = place[1] == 0

    def body(r, _):
        rows = pl.ds(pl.multiple_of(r * TM, TM), TM)
        mine = jnp.concatenate([refs[i][rows, :].astype(F32) for i in range(len(widths))], axis=1)
        other = refs[len(widths)][rows, : sum(widths)].astype(F32)
        both_halves = jnp.concatenate([jnp.where(low, mine, other), jnp.where(low, other, mine)], axis=1)
        out_ref[rows, :] = both_halves.astype(BF)
        return 0

    lax.fori_loop(0, out_ref.shape[0] // TM, body, 0)


def unpack_hidden(widths, place, mine, other):
    t = other.shape[0]
    return pl.pallas_call(
        functools.partial(unpack_h_kernel, widths),
        in_specs=[SMEM_SPEC] + [VMEM_SPEC] * (len(mine) + 1),
        out_shape=jax.ShapeDtypeStruct((t, 2 * sum(widths)), BF),
        compiler_params=params(),
        cost_estimate=TINY,
        name="unpack_hidden",
    )(place, *mine, other)


def on_device(layer_input, keep, w_now, w_prev, bias, grad_out):
    n, m = lax.axis_size("seq"), lax.axis_size("gate")
    heads = n // 4
    s, g = lax.axis_index("seq"), lax.axis_index("gate")
    h, l, p, a, b = s // 4, s // 2 % 2, s % 2, g // 2, g % 2
    place = jnp.stack([h, l, p, a, b]).astype(jnp.int32)
    t, dl = layer_input.shape
    dw = w_now.shape[1]
    half = dl // 2
    pad = ceil_to(dl, LANES)
    widths = tuple(w for w in WIDTHS) if sum(WIDTHS) == half else (half,)
    low = l == 0

    def seq_to(v, kh, d_l, d_p):
        route = []
        for i in range(n):
            i_h, i_l, i_p = i // 4, i // 2 % 2, i % 2
            route.append((i, ((i_h + kh) % heads * 2 + (i_l ^ d_l)) * 2 + (i_p ^ d_p)))
        return lax.ppermute(v, "seq", route)

    def gate_to(v, d_a, d_b):
        return lax.ppermute(v, "gate", [(i, i ^ (d_a * 2 + d_b)) for i in range(m)])

    group = [(kh, d_p) for kh in range(heads) for d_p in range(2)]

    packed = pack_weights(widths, 0, place, w_now, w_prev)
    behind = lax.ppermute(layer_input[-1:], "seq", [(i, i + 1) for i in range(n - 1)])
    flags = jnp.broadcast_to(jnp.pad(keep, (0, EDGE)).astype(BF)[:, None], (t + EDGE, pad - dl))
    rows = jnp.concatenate([layer_input, jnp.pad(behind, ((0, EDGE - 1), (0, 0)))], axis=0)
    x0 = after(jnp.concatenate([rows, flags], axis=1), packed[0])
    def share_w(pair, *needs):
        got = {(0, 0): pair, (0, 1): seq_to(pair, 0, 0, 1)}
        for kh in range(1, heads):
            got[kh, 0] = seq_to(after(pair, *needs) if needs else pair, kh, 0, 0)
        return got

    def finish_share(got, *needs):
        for kh in range(1, heads):
            got[kh, 1] = seq_to(after(got[kh, 0], *needs) if needs else got[kh, 0], 0, 0, 1)

    def weights_in(got, c):
        if dw % 16 == 0:
            return [got[r] for r in got], list(got)
        stacked = jnp.stack([got[kh, d_p][d_l] for kh in range(heads) for d_l in range(2) for d_p in range(2)])
        blocks = jnp.arange(n)
        rel = (((h - blocks // 4) % heads) * 2 + (l ^ (blocks // 2 % 2))) * 2 + (p ^ (blocks % 2))
        whole = jnp.take(stacked, rel, axis=0).reshape(m, dl, 6 * c)
        return [jnp.pad(whole, ((0, 0), (0, pad - dl), (0, 0)))], []

    half_bias = jnp.where(low, bias[:, :half], bias[:, half:])
    count = len(widths)
    spans = list(offsets(widths))
    near = seq_to(packed[1], 0, 1, 0)
    got = [share_w(jnp.stack([packed[0], near]))]
    y0 = gate_to(x0, 1, 0)
    x1 = seq_to(after(x0, near), 0, 1, 0)
    first_p = got[0][0, 1]
    up_packed = pack_up(widths, place, after(grad_out, x0))
    ups = [[up_packed[0], seq_to(after(up_packed[1], near), 0, 1, 0)]]
    hop = [got[0][kh, 0] for kh in range(1, heads)]
    c0, cy0 = gate_to(after(x0, y0, first_p, *hop), 0, 1), gate_to(after(y0, first_p, *hop), 0, 1)
    x1_here = after(x1, y0, first_p)
    y1, c1 = gate_to(x1_here, 1, 0), gate_to(x1_here, 0, 1)
    finish_share(got[0])
    for i in range(1, count):
        packed = pack_weights(widths, i, place, after(w_now, near), w_prev)
        near = seq_to(packed[1], 0, 1, 0)
        got.append(share_w(jnp.stack([packed[0], near]), c1, *[got[i - 1][kh, 0] for kh in range(1, heads)]))
        ups.append([up_packed[2 * i], seq_to(after(up_packed[2 * i + 1], near), 0, 1, 0)])
    cy1 = gate_to(after(y1, ups[0][1], *[got[0][kh, 1] for kh in range(1, heads)]), 0, 1)
    xs = {(0, 0, 0): x0, (0, 1, 0): y0, (0, 0, 1): c0, (0, 1, 1): cy0}
    xs |= {(1, 0, 0): x1, (1, 1, 0): y1, (1, 0, 1): c1, (1, 1, 1): cy1}
    hidden_mine, hidden_other, grads, wide_w, g_first, g_bias, w_pairs = [], [], [], [], [], [], []

    def spread_totals(tot):
        return jnp.stack([tot if r == (0, 0) else seq_to(tot, r[0], 0, r[1]) for r in group])

    def weight_parts(gg, gp, *needs):
        if dw % 16 == 0 and n == 2 * m:
            return weight_grads(heads, dw, pad, place, x_all, halo, gg, after(gp, *needs) if needs else gp)
        dots = jnp.einsum("td,tn->dn", x_all, gg, preferred_element_type=F32)
        dots = dots + jnp.einsum("td,tn->dn", halo, gp, preferred_element_type=F32)
        v = dots.astype(BF).reshape(m, pad, -1)[:, :dl].reshape(heads, 2, 2, dw, gg.shape[1])
        away = jnp.where(p == 0, v[:, :, 1], v[:, :, 0])
        here = jnp.where(p == 0, v[:, :, 0], v[:, :, 1])

        def block(v, kh):
            row = lax.dynamic_index_in_dim(v, (h + kh) % heads, 0, keepdims=False)
            return jnp.where(low, row[::-1], row)

        return [(kh, block(here, kh), block(away, kh)) for kh in list(range(1, heads)) + [0]]

    def over_p(parts, *needs):
        came = []
        for _, _, away in parts:
            came.append(after(seq_to(away, 0, 0, 1), *came[-1:], *needs))
        return [here.astype(F32) + v.astype(F32) for (_, here, _), v in zip(parts, came)]

    def over_h(parts, sums, *needs):
        total = sums[-1]
        for (kh, _, _), v in zip(parts[:-1], sums[:-1]):
            total = total + after(seq_to(v.astype(BF), kh, 0, 0), *needs).astype(F32)
        return total.astype(BF)

    waiting = None
    for i, (at, c) in enumerate(spans):
        dims = (n, m, dw, dl, t, c)
        bias_i = half_bias[:, at : at + c]
        if i > 0:
            finish_share(got[i], every, ups[i][1])
        w_in, wrel = weights_in(got[i], c)
        if i == 0:
            xrel = list(xs)
            gates, seg, tot, x_all, halo, keep_w, w_rel = gates_and_totals(
                dims, 0, place, w_in, wrel, [xs[r] for r in xrel], xrel, bias_i, ups[i]
            )
        else:
            w_in[0] = after(w_in[0], *[v[2] for v in waiting[:-1]])
            gates, seg, tot, w_rel = gates_and_totals(
                dims, 0, place, w_in, wrel, [x_all, halo], [], bias_i, ups[i], keep_w
            )
        every = spread_totals(after(tot, *[g[0, 1] for g in got[i + 1 : i + 2]]) if i + 1 < count else tot)
        wide_w.append(w_rel)
        if i > 0:
            (kh0, here0, away0), *others = waiting[::-1]
            others = others[::-1]
            sums = over_p(others, tot)
            every_now = after(every, *sums)
            h_sums = [after(v, every) for v in sums]
            (near_sum,) = over_p([(kh0, here0, after(away0, every))])
            h_sums.append(near_sum)
            every = every_now
        before = hidden_other if i == count - 1 else ()
        h0, h1, gg, gf, gp, gb = finish(n, 0, place, gates, ups[i], keep_w, seg, every, before)
        hidden_mine.append(h0)
        hidden_other.append(h1)
        g_first.append(gf)
        g_bias.append(gb)
        if i == count - 1:
            parts = jnp.concatenate([jnp.concatenate(g_first, axis=1), jnp.concatenate(g_bias, axis=1)], axis=0)
            around = [parts if r == (0, 0) else seq_to(parts, r[0], 0, r[1]) for r in group]
            hidden_came = seq_to(after(h1, parts), 0, 1, 0)
        needs = list(around) if i == count - 1 else []
        if i > 0:
            total = over_h(waiting, h_sums)
            needs.append(total)
        waiting_next = weight_parts(gg, gp)
        if needs:
            waiting_next = [(kh, here, after(away, *needs)) for kh, here, away in waiting_next]
        if i > 0:
            w_pairs += [total[1], seq_to(total[0], 0, 1, 0)]
        waiting = waiting_next
        grads.append(gg)
    around = jnp.stack(around)

    full_bias = jnp.sum(around[:, 2], axis=0)
    nexts = []
    for slot in range(2):
        block_id = (h * 2 + (l ^ slot)) * 2 + p + 1
        n_h, n_l, n_p = block_id // 4, block_id // 2 % 2, block_id % 2
        member = ((h - n_h) % heads) * 2 + (p ^ n_p)
        row = lax.dynamic_index_in_dim(around, member, 0, keepdims=False)
        row = lax.dynamic_index_in_dim(row, l ^ n_l, 0, keepdims=False)
        nexts.append(jnp.where(block_id < n, row, jnp.zeros_like(row)))
    nexts = jnp.stack(nexts)
    nexts = [nexts[:, 3 * at : 3 * (at + c)] for at, c in spans]
    bias_half = []
    at = 0
    for c in widths:
        bias_half.append(full_bias[at : at + 3 * c].reshape(3, c))
        at += 3 * c
    bias_half = jnp.concatenate(bias_half, axis=1)
    bias_other = seq_to(bias_half, 0, 1, 0)
    nexts[0] = after(nexts[0], *[v[2] for v in waiting])
    sent1, kept1, sent0, kept0 = input_grads(place, grads, nexts, wide_w)
    p_came = []
    for v in waiting:
        p_came.append(after(seq_to(v[2], 0, 0, 1), *p_came[-1:]))
    sent1, sent0, *_ = lax.optimization_barrier((sent1, sent0, p_came[0], hidden_came, bias_other, *w_pairs))
    c_came1, c_came0 = gate_to(sent1, 0, 1), gate_to(sent0, 0, 1)
    farther = [join([(here, 0), (p_came[k], 0)], LATER) for k, (_, here, _) in enumerate(waiting[:-1])]
    c_came1 = after(c_came1, *farther)
    h_came = [seq_to(v, waiting[k][0], 0, 0) for k, v in enumerate(farther)]
    y_came1 = gate_to(join([(kept1, 1), (c_came1, 1)], LATER), 1, 0)
    total = join([(waiting[-1][1], 0), (p_came[-1], 0)] + [(v, None) for v in h_came], LATER)
    l_total = seq_to(total, 0, 1, 0)
    x_part = join([(kept1, 0), (c_came1, 0), (after(y_came1, total), None)], LATER)
    l_came = seq_to(x_part, 0, 1, 0)
    c_came0 = after(c_came0, x_part)
    y_came0 = gate_to(join([(kept0, 1), (c_came0, 1)], LATER), 1, 0)
    rest = [join([(here, 1), (p_came[k], 1)], LATER) for k, (_, here, _) in enumerate(waiting[:-1])]
    h_rest = [seq_to(after(v, y_came1, total), waiting[k][0], 0, 0) for k, v in enumerate(rest)]
    grad_x = kept0[0].astype(F32) + c_came0[0].astype(F32) + y_came0.astype(F32) + l_came.astype(F32)
    grad_x = grad_x[:, :dl].astype(BF)
    h_rest = [after(v, grad_x) for v in h_rest]
    last = [(waiting[-1][1], 1), (p_came[-1], 1)] + [(v, None) for v in h_rest]

    grad_bias = jnp.concatenate(
        [jnp.where(low, bias_half, bias_other), jnp.where(low, bias_other, bias_half)], axis=1
    )
    hidden = unpack_hidden(widths, place, hidden_mine, hidden_came)
    grad_now, grad_prev = unpack_weights(widths, place, w_pairs, last, l_total)
    return hidden, grad_x, grad_now, grad_prev, grad_bias


def solution(mesh):
    tokens, matrix = P("seq", "gate"), P(None, "seq", "gate")
    return jax.shard_map(
        on_device,
        mesh=mesh,
        in_specs=(tokens, P("seq"), matrix, matrix, P(None, "gate"), tokens),
        out_specs=(tokens, tokens, matrix, matrix, P(None, "gate")),
        check_vma=False,
    )
```

```python
import functools

import jax
import jax.numpy as jnp
from jax import lax
from jax.experimental import pallas as pl
from jax.experimental.pallas import tpu as pltpu
from jax.sharding import PartitionSpec as P

F32 = jnp.float32
BF = jnp.bfloat16
SEGS = 8
LANES = 128
TM = 64
ROWS = 512
EDGE = 16
GAP = 8
VMEM = 62 << 20
WIDTHS = (128, 160)


def ceil_to(value, unit):
    return -(-value // unit) * unit


def both(g):
    e = jnp.exp(-jnp.abs(g))
    r = 1.0 / (1.0 + e)
    er = e * r
    pos = g >= 0
    return jnp.where(pos, r, er), jnp.where(pos, er, r)


def group(k, lo, w, count=6):
    return slice(count * lo + k * w, count * lo + (k + 1) * w)


def load_up(ref, rows, lo, w):
    return ref[rows, lo : lo + w].astype(F32)


def spread(row, span):
    return pl.ds(pl.multiple_of(row + row // span * GAP, 8), TM)


def cuts(c):
    return [(i, i * LANES, min(LANES, c - i * LANES)) for i in range(-(-c // LANES))]


def params():
    return pltpu.CompilerParams(vmem_limit_bytes=VMEM)


URGENT, LATER = 100, 50
TINY = pl.CostEstimate(flops=1 << 10, bytes_accessed=1 << 10, transcendentals=0)
SMEM_SPEC = pl.BlockSpec(memory_space=pltpu.SMEM)
VMEM_SPEC = pl.BlockSpec(memory_space=pltpu.VMEM)
ANY_SPEC = pl.BlockSpec(memory_space=pl.ANY)


def offsets(widths):
    at = 0
    for w in widths:
        yield at, w
        at += w


def pack_w_kernel(widths, share, place, now_ref, prev_ref, *outs):
    half = now_ref.shape[2] // 2
    low = place[1] == 0
    for tap, ref in enumerate((now_ref, prev_ref)):
        for k in range(3):
            v = ref[k].astype(F32)
            mine = jnp.where(low, v[:, :half], v[:, half:])
            other = jnp.where(low, v[:, half:], v[:, :half])
            at, c = list(offsets(widths))[share]
            for _, lo, w in cuts(c):
                to = group(tap * 3 + k, lo, w)
                outs[0][:, to] = mine[:, at + lo : at + lo + w].astype(BF)
                outs[1][:, to] = other[:, at + lo : at + lo + w].astype(BF)


def pack_weights(widths, share, place, w_now, w_prev):
    rows, w = w_now.shape[1], widths[share]
    return pl.pallas_call(
        functools.partial(pack_w_kernel, widths, share),
        in_specs=[SMEM_SPEC, VMEM_SPEC, VMEM_SPEC],
        out_shape=[jax.ShapeDtypeStruct((rows, 6 * w), BF)] * 2,
        compiler_params=params(),
        cost_estimate=TINY,
        name="pack_weights",
    )(place, w_now, w_prev)


def pack_up_kernel(widths, place, up_ref, *outs):
    half = up_ref.shape[1] // 2
    low = place[1] == 0

    def body(r, _):
        rows = pl.ds(pl.multiple_of(r * TM, TM), TM)
        v = up_ref[rows, :].astype(F32)
        mine = jnp.where(low, v[:, :half], v[:, half:])
        other = jnp.where(low, v[:, half:], v[:, :half])
        for i, (at, w) in enumerate(offsets(widths)):
            outs[2 * i][rows, :] = mine[:, at : at + w].astype(BF)
            outs[2 * i + 1][rows, :w] = other[:, at : at + w].astype(BF)
        return 0

    lax.fori_loop(0, up_ref.shape[0] // TM, body, 0)


def pack_up(widths, place, grad_out):
    t = grad_out.shape[0]
    return pl.pallas_call(
        functools.partial(pack_up_kernel, widths),
        in_specs=[SMEM_SPEC, VMEM_SPEC],
        out_shape=[jax.ShapeDtypeStruct((t, w), BF) for v in widths for w in (v, ceil_to(v, LANES))],
        compiler_params=params(),
        cost_estimate=TINY,
        name="pack_up",
    )(place, grad_out)


def gates_kernel(plan, place, *refs):
    n, m, dw, dl, t, c, up_at, wrel, xrel = plan
    n_w, n_x = len(wrel) or 1, len(xrel) or 1
    w_in, refs = refs[:n_w], refs[n_w:]
    x_in, refs = refs[:n_x], refs[n_x:]
    if not xrel:
        halo_in, refs = refs[0], refs[1:]
    bias_ref, up0, up1 = refs[:3]
    refs = refs[3:]
    if not xrel:
        keep_w, refs = refs[0], refs[1:]
    g_ref, seg_ref, tot_ref, refs = refs[0], refs[1], refs[2], refs[3:]
    if xrel:
        x_out, halo_out, keep_w, refs = refs[0], refs[1], refs[2], refs[3:]
    w_out, refs = refs[0], refs[1:]
    xs, halo, ws, p_s, d_s, s_s, q_s, seg_s, xsem, hsem, wsem, osem = refs
    pad = ws.shape[1]
    width = ws.shape[2]
    wide = n // m
    h, l, p, a, b = (place[i] for i in range(5))
    heads = n // 4
    copies = []
    if wrel:
        for i, (kh, d_p) in enumerate(wrel):
            for d_l in range(2):
                block = (lax.rem(h - kh + heads, heads) * 2 + (l ^ d_l)) * 2 + (p ^ d_p)
                at = pl.multiple_of(lax.rem(block, wide) * dw, 16)
                copies.append(
                    pltpu.make_async_copy(
                        w_in[i].at[d_l], ws.at[block // wide, pl.ds(at, dw), :], wsem.at[2 * i + d_l]
                    )
                )
        if pad > dl:
            for g in range(m):
                ws[g, dl:, :] = jnp.zeros((pad - dl, width), BF)
    else:
        copies.append(pltpu.make_async_copy(w_in[0], ws, wsem.at[0]))
    xcopies = [[], []]
    if xrel:
        for i, (slot, d_a, d_b) in enumerate(xrel):
            at = pl.multiple_of(((a ^ d_a) * 2 + (b ^ d_b)) * pad, LANES)
            xcopies[slot].append(
                pltpu.make_async_copy(
                    x_in[i].at[pl.ds(0, t)], xs.at[pl.ds(slot * t, t), pl.ds(at, pad)], xsem.at[i]
                )
            )
            copies.append(
                pltpu.make_async_copy(
                    x_in[i].at[pl.ds(t, EDGE)], halo.at[pl.ds(slot * EDGE, EDGE), pl.ds(at, pad)], hsem.at[i]
                )
            )
    else:
        for slot in range(2):
            rows = pl.ds(slot * t, t)
            xcopies[slot].append(pltpu.make_async_copy(x_in[0].at[rows], xs.at[rows], xsem.at[slot]))
        copies.append(pltpu.make_async_copy(halo_in, halo, hsem.at[0]))
    for copy in copies + xcopies[0] + xcopies[1]:
        copy.start()
    for copy in copies:
        copy.wait()
    outs = []
    for g in range(m):
        outs.append(pltpu.make_async_copy(ws.at[g], w_out.at[(a * 2 + b) ^ g], osem.at[g]))
    for copy in outs:
        copy.start()
    lanes = cuts(c)
    weights = ws[...].reshape(m * pad, width)
    if xrel:
        out = pltpu.make_async_copy(halo, halo_out, osem.at[m + 2])
        out.start()
        outs.append(out)
    edge = jnp.dot(halo[...], weights, preferred_element_type=F32)
    for slot, up_ref in enumerate((up0, up1)):
        for copy in xcopies[slot]:
            copy.wait()
        if xrel:
            rows = pl.ds(slot * t, t)
            out = pltpu.make_async_copy(xs.at[rows], x_out.at[rows], osem.at[m + slot])
            out.start()
            outs.append(out)
        p_s[7:8, :] = edge[slot * EDGE : slot * EDGE + 1, :]

        def tile(i, _, slot=slot, up_ref=up_ref):
            base = pl.multiple_of(i * ROWS, ROWS)
            x = xs[pl.ds(pl.multiple_of(slot * t + base, ROWS), ROWS), :]
            p_s[8:, :] = jnp.dot(x, ws[...].reshape(m * pad, width), preferred_element_type=F32)
            for r in range(ROWS // TM):
                rows = pl.ds(pl.multiple_of(base + r * TM, TM), TM)
                full = pl.ds(pl.multiple_of(slot * t + base + r * TM, TM), TM)
                apart = spread(base + r * TM, t // SEGS)
                if xrel:
                    flags = xs[full, dl:pad].astype(F32)
                    keep = jnp.concatenate([flags] * (LANES // (pad - dl)), axis=1)
                    keep_w[full, :] = keep
                else:
                    keep = keep_w[full, :]
                for k_l, lo, w in lanes:
                    g = []
                    for k in range(3):
                        now = p_s[8 + r * TM : 8 + (r + 1) * TM, group(k, lo, w)]
                        before = p_s[7 + r * TM : 7 + (r + 1) * TM, group(3 + k, lo, w)]
                        v = now + keep[:, :w] * before + bias_ref[k : k + 1, lo : lo + w]
                        g_ref[k, full, lo : lo + w] = v
                        g.append(v)
                    f, intake = both(g[1])
                    o, _ = both(g[2])
                    d = keep[:, :w] * f
                    d_s[slot, k_l, apart, :w] = d
                    s_s[slot, k_l, apart, :w] = intake * jnp.tanh(g[0])
                    q_s[slot, k_l, apart, :w] = d * (load_up(up_ref, rows, slot * up_at + lo, w) * o)
            p_s[7:8, :] = p_s[ROWS + 7 : ROWS + 8, :]
            return 0

        lax.fori_loop(0, t // ROWS, tile, 0)
    span = t // SEGS
    chains = [(slot, k_l) for slot in range(2) for k_l, _, _ in lanes]
    one, zero = jnp.ones((SEGS, LANES), F32), jnp.zeros((SEGS, LANES), F32)

    def step(j, carry):
        at, back = pl.ds(j, SEGS, stride=span + GAP), pl.ds(span - 1 - j, SEGS, stride=span + GAP)
        new = []
        for (slot, k_l), (pa, ps, pr) in zip(chains, carry):
            d = d_s[slot, k_l, at, :]
            new.append(
                (
                    pa * d,
                    d * ps + s_s[slot, k_l, at, :],
                    d_s[slot, k_l, back, :] * pr + q_s[slot, k_l, back, :],
                )
            )
        return tuple(new)

    res = lax.fori_loop(0, span, step, tuple((one, zero, zero) for _ in chains), unroll=4)
    for (slot, k_l), triple in zip(chains, res):
        _, lo, w = lanes[k_l]
        for k in range(3):
            seg_s[k] = triple[k]
            seg_ref[slot, k, :, lo : lo + w] = triple[k][:, :w]
        pa, ps, pr = one[:1], zero[:1], zero[:1]
        for k in range(SEGS):
            d = seg_s[0, k : k + 1, :]
            ps = d * ps + seg_s[1, k : k + 1, :]
            pa = pa * d
            r = SEGS - 1 - k
            pr = seg_s[0, r : r + 1, :] * pr + seg_s[2, r : r + 1, :]
        for k, v in enumerate((pa, ps, pr)):
            tot_ref[slot, k : k + 1, lo : lo + w] = v[:, :w]
    for copy in outs:
        copy.wait()


def after(v, *needs):
    return lax.optimization_barrier((v, *needs))[0]


def gates_and_totals(dims, up_at, place, w, wrel, x, xrel, bias, ups, keep_w=None):
    n, m, dw, dl, t, c = dims
    pad = ceil_to(dl, LANES)
    lt = len(cuts(c))
    width = 6 * c
    plan = (n, m, dw, dl, t, c, up_at, tuple(wrel), tuple(xrel))
    shape = jax.ShapeDtypeStruct
    outs = [shape((3, 2 * t, c), F32), shape((2, 3, SEGS, c), F32), shape((2, 3, c), F32)]
    specs = [VMEM_SPEC] * 3
    if xrel:
        outs += [shape((2 * t, m * pad), BF), shape((2 * EDGE, m * pad), BF), shape((2 * t, LANES), F32)]
        specs += [ANY_SPEC, ANY_SPEC, VMEM_SPEC]
    outs.append(shape((m, pad, width), BF))
    specs.append(ANY_SPEC)
    return pl.pallas_call(
        functools.partial(gates_kernel, plan),
        in_specs=[SMEM_SPEC] + [ANY_SPEC] * (len(w) + len(x)) + [VMEM_SPEC] * (3 if xrel else 4),
        out_specs=specs,
        out_shape=outs,
        scratch_shapes=[
            pltpu.VMEM((2 * t, m * pad), BF),
            pltpu.VMEM((2 * EDGE, m * pad), BF),
            pltpu.VMEM((m, pad, width), BF),
            pltpu.VMEM((ROWS + 8, width), F32),
            pltpu.VMEM((2, lt, t + SEGS * GAP, LANES), F32),
            pltpu.VMEM((2, lt, t + SEGS * GAP, LANES), F32),
            pltpu.VMEM((2, lt, t + SEGS * GAP, LANES), F32),
            pltpu.VMEM((3, SEGS, LANES), F32),
            pltpu.SemaphoreType.DMA((max(2, len(x)),)),
            pltpu.SemaphoreType.DMA((max(1, len(x)),)),
            pltpu.SemaphoreType.DMA((2 * len(w),)),
            pltpu.SemaphoreType.DMA((m + 3,)),
        ],
        compiler_params=params(),
        cost_estimate=TINY,
        name="gates_and_totals",
    )(place, *w, *x, bias, *ups, *([] if xrel else [keep_w]))


def finish_kernel(n, up_at, place, g_ref, up0, up1, keep_ref, seg_ref, all_ref, *refs):
    count = len(refs) - 11
    before, refs = refs[:count], refs[count:]
    h0, h1, gg_ref, gf_ref, gp_ref, gb_ref, d_s, s_s, q_s, p_s, c_s = refs
    t, c = up0.shape
    span = t // SEGS
    lanes = cuts(c)
    heads = n // 4
    hh, ll, pp = place[0], place[1], place[2]
    ups, hids = (up0, up1), (h0, h1)
    at = 0
    for ref in before:
        h1[:, at : at + ref.shape[1]] = ref[...]
        at += ref.shape[1]
    firsts_at = (0, at)
    for slot in range(2):

        def act(r, _, slot=slot):
            rows = pl.ds(pl.multiple_of(r * TM, TM), TM)
            full = pl.ds(pl.multiple_of(slot * t + r * TM, TM), TM)
            apart = spread(r * TM, span)
            for k_l, lo, w in lanes:
                ch = slice(lo, lo + w)
                f, i = both(g_ref[1, full, ch])
                o, _ = both(g_ref[2, full, ch])
                d_s[slot, k_l, apart, :w] = keep_ref[full, :w] * f
                s_s[slot, k_l, apart, :w] = i * jnp.tanh(g_ref[0, full, ch])
                q_s[slot, k_l, apart, :w] = load_up(ups[slot], rows, slot * up_at + lo, w) * o
            return 0

        lax.fori_loop(0, t // TM, act, 0)
    zrow = jnp.zeros((1, c), F32)
    mine = [(hh * 2 + (ll ^ slot)) * 2 + pp for slot in range(2)]

    def total(block, k):
        p_b, l_b, h_b = block % 2, block // 2 % 2, block // 4
        member = lax.rem(hh - h_b + heads, heads) * 2 + (pp ^ p_b)
        return all_ref[member, ll ^ l_b, k : k + 1, :]

    h, r = zrow, zrow
    h_in, r_in = [zrow, zrow], [zrow, zrow]
    for k in range(n):
        b = n - 1 - k
        h_in = [jnp.where(mine[s] == k, h, h_in[s]) for s in range(2)]
        r_in = [jnp.where(mine[s] == b, r, r_in[s]) for s in range(2)]
        h = total(k, 0) * h + total(k, 1)
        r = total(b, 0) * r + total(b, 2)
    for slot in range(2):
        h, r = h_in[slot], r_in[slot]
        for k in range(SEGS):
            b = SEGS - 1 - k
            for k_l, lo, w in lanes:
                c_s[0, slot, k_l, k : k + 1, :w] = h[:, lo : lo + w]
                c_s[1, slot, k_l, b : b + 1, :w] = r[:, lo : lo + w]
            h = seg_ref[slot, 0, k : k + 1, :] * h + seg_ref[slot, 1, k : k + 1, :]
            r = seg_ref[slot, 0, b : b + 1, :] * r + seg_ref[slot, 2, b : b + 1, :]
    chains = [(slot, k_l) for slot in range(2) for k_l, _, _ in lanes]

    def step(j, carry):
        at, back = pl.ds(j, SEGS, stride=span + GAP), pl.ds(span - 1 - j, SEGS, stride=span + GAP)
        new = []
        for (slot, k_l), (h, r) in zip(chains, carry):
            dh = d_s[slot, k_l, at, :] * h
            h = dh + s_s[slot, k_l, at, :]
            p_s[slot, k_l, at, :] = dh
            s_s[slot, k_l, at, :] = h
            g = q_s[slot, k_l, back, :] + r
            q_s[slot, k_l, back, :] = g
            new.append((h, d_s[slot, k_l, back, :] * g))
        return tuple(new)

    lax.fori_loop(0, span, step, tuple((c_s[0, s, k_l], c_s[1, s, k_l]) for s, k_l in chains), unroll=4)
    sums = [jnp.zeros((8, w), F32) for _, _, w in lanes for _ in range(3)]
    top = lax.broadcasted_iota(jnp.int32, (EDGE, LANES), 0) == 0
    gp_ref[...] = jnp.zeros(gp_ref.shape, BF)
    for slot in range(2):

        def out(i, state, slot=slot):
            acc, nxt = state
            r = t // TM - 1 - i
            rows = pl.ds(pl.multiple_of(r * TM, TM), TM)
            full = pl.ds(pl.multiple_of(slot * t + r * TM, TM), TM)
            apart = spread(r * TM, span)
            last = lax.broadcasted_iota(jnp.int32, (TM, LANES), 0) == TM - 1
            new, first = [], []
            for k_l, lo, w in lanes:
                ch = slice(lo, lo + w)
                f, intake = both(g_ref[1, full, ch])
                o, cl = both(g_ref[2, full, ch])
                z = jnp.tanh(g_ref[0, full, ch])
                keep = keep_ref[full, :w]
                gs = q_s[slot, k_l, apart, :w]
                oh = o * s_s[slot, k_l, apart, :w]
                hids[slot][rows, firsts_at[slot] + lo : firsts_at[slot] + lo + w] = oh.astype(BF)
                gi = gs * intake
                grads = (
                    gi * (1.0 - z * z),
                    gi * (p_s[slot, k_l, apart, :w] - f * z),
                    load_up(ups[slot], rows, slot * up_at + lo, w) * oh * cl,
                )
                for k, v in enumerate(grads):
                    gg_ref[full, group(k, lo, w)] = v.astype(BF)
                    kept = keep * v
                    moved = jnp.where(last[:, :w], nxt[len(new)], pltpu.roll(kept, TM - 1, 0))
                    gg_ref[full, group(3 + k, lo, w)] = moved.astype(BF)
                    first.append(kept[:1])
                    new.append(acc[len(new)] + jnp.sum(v.reshape(TM // 8, 8, w), axis=0))
            return tuple(new), tuple(first)

        zeros = tuple(jnp.zeros((1, w), F32) for _, _, w in lanes for _ in range(3))
        sums, firsts = lax.fori_loop(0, t // TM, out, (tuple(sums), zeros))
        for k_l, lo, w in lanes:
            for k in range(3):
                gf_ref[slot : slot + 1, group(k, lo, w, 3)] = firsts[3 * k_l + k]
                gp_ref[slot * EDGE : slot * EDGE + EDGE, group(3 + k, lo, w)] = jnp.where(
                    top[:, :w], firsts[3 * k_l + k], 0.0
                ).astype(BF)
    for k_l, lo, w in lanes:
        for k in range(3):
            gb_ref[0:1, k * c + lo : k * c + lo + w] = jnp.sum(sums[3 * k_l + k], axis=0, keepdims=True)


def finish(n, up_at, place, gates, ups, keep_w, seg, every, before=()):
    t, c = ups[0].shape
    lt = len(cuts(c))
    shape = jax.ShapeDtypeStruct
    return pl.pallas_call(
        functools.partial(finish_kernel, n, up_at),
        in_specs=[SMEM_SPEC] + [VMEM_SPEC] * (6 + len(before)),
        out_shape=[
            shape((t, c), BF),
            shape((t, ceil_to(c + sum(v.shape[1] for v in before), LANES if before else 1)), BF),
            shape((2 * t, 6 * c), BF),
            shape((2, 3 * c), F32),
            shape((2 * EDGE, 6 * c), BF),
            shape((1, 3 * c), F32),
        ],
        scratch_shapes=[pltpu.VMEM((2, lt, t + SEGS * GAP, LANES), F32)] * 4 + [pltpu.VMEM((2, 2, lt, SEGS, LANES), F32)],
        compiler_params=params(),
        cost_estimate=TINY,
        name="finish",
    )(place, gates, *ups, keep_w, seg, every, *before)


def wgrad_kernel(dw, place, x_ref, halo_ref, gg_ref, gp_ref, *refs):
    *outs, acc = refs
    over_tokens = (((0,), (0,)), ((), ()))
    v = lax.dot_general(x_ref[...], gg_ref[...], over_tokens, preferred_element_type=F32)
    acc[...] = v + lax.dot_general(halo_ref[...], gp_ref[...], over_tokens, preferred_element_type=F32)
    p = place[2]
    step = pl.program_id(0)
    for k in range(len(outs) // 2):

        @pl.when(step // 2 == k)
        def _(k=k):
            outs[2 * k][0] = acc[pl.ds(pl.multiple_of(p * dw, 16), dw), :].astype(BF)
            outs[2 * k + 1][0] = acc[pl.ds(pl.multiple_of((1 - p) * dw, 16), dw), :].astype(BF)


def weight_grads(heads, dw, pad, place, x_all, halo, gg, gp):
    width = gg.shape[1]

    def lanes(i, at):
        kh = lax.rem(i // 2 + 1, heads)
        return (0, lax.rem(at[0] + kh, heads) * 2 + (at[1] ^ (1 - lax.rem(i, 2))))

    def out(k):
        return pl.BlockSpec((1, dw, width), lambda i, at: (jnp.clip(i - 2 * k, 0, 1), 0, 0))

    whole = lambda i, at: (0, 0)
    res = pl.pallas_call(
        functools.partial(wgrad_kernel, dw),
        grid_spec=pltpu.PrefetchScalarGridSpec(
            num_scalar_prefetch=1,
            grid=(2 * heads,),
            in_specs=[
                pl.BlockSpec((x_all.shape[0], pad), lanes),
                pl.BlockSpec((halo.shape[0], pad), lanes),
                pl.BlockSpec(gg.shape, whole),
                pl.BlockSpec(gp.shape, whole),
            ],
            out_specs=[out(k) for k in range(heads) for _ in range(2)],
            scratch_shapes=[pltpu.VMEM((pad, width), F32)],
        ),
        out_shape=[jax.ShapeDtypeStruct((2, dw, width), BF)] * (2 * heads),
        compiler_params=params(),
        cost_estimate=TINY,
        name="weight_grads",
    )(place, x_all, halo, gg, gp)
    return [((k + 1) % heads, res[2 * k], res[2 * k + 1]) for k in range(heads)]


def xgrad_kernel(place, *refs):
    count = (len(refs) - 5) // 4
    gg_in, nx, w_in = refs[:count], refs[count : 2 * count], refs[2 * count : 3 * count]
    outs = refs[3 * count : 3 * count + 4]
    gg_s, sem = refs[3 * count + 4 : 4 * count + 4], refs[4 * count + 4]
    i, turn = pl.program_id(0), pl.program_id(1)
    t = gg_s[0].shape[0] // 2

    @pl.when((i == 0) & (turn == 0))
    def _():
        copies = [pltpu.make_async_copy(gg_in[k], gg_s[k], sem.at[k]) for k in range(count)]
        for copy in copies:
            copy.start()
        for k, copy in enumerate(copies):
            copy.wait()
            for _, lo, w in cuts(nx[k].shape[1] // 3):
                last = lax.broadcasted_iota(jnp.int32, (EDGE, 3 * w), 0) == EDGE - 1
                there = slice(6 * lo + 3 * w, 6 * lo + 6 * w)
                for slot in range(2):
                    rows = slice((slot + 1) * t - EDGE, (slot + 1) * t)
                    old = gg_s[k][rows, there].astype(F32)
                    new = nx[k][slot : slot + 1, 3 * lo : 3 * lo + 3 * w]
                    gg_s[k][rows, there] = jnp.where(last, new, old).astype(BF)

    rows = pl.ds(pl.multiple_of((1 - turn) * t, t), t)
    v = 0.0
    for k in range(count):
        v = v + lax.dot_general(
            gg_s[k][rows, :], w_in[k][0], (((1,), (1,)), ((), ())), preferred_element_type=F32
        )
    v = v.astype(BF)
    for k in range(4):

        @pl.when((turn == k // 2) & ((i < 2) == (k % 2 == 0)))
        def _(k=k):
            outs[k][0] = v


def input_grads(place, ggs, nexts, ws):
    count = len(ggs)
    t = ggs[0].shape[0] // 2
    m, pad, _ = ws[0].shape
    order = lambda i: jnp.where(i < 2, 2 * i + 1, 2 * i - 4)
    sent = pl.BlockSpec((1, t, pad), lambda i, turn, at: (jnp.minimum(i, 1), 0, 0))
    kept = pl.BlockSpec((1, t, pad), lambda i, turn, at: (jnp.maximum(i - 2, 0), 0, 0))
    return pl.pallas_call(
        xgrad_kernel,
        grid_spec=pltpu.PrefetchScalarGridSpec(
            num_scalar_prefetch=1,
            grid=(m, 2),
            in_specs=[ANY_SPEC] * count
            + [pl.BlockSpec(v.shape, lambda i, turn, at: (0, 0)) for v in nexts]
            + [pl.BlockSpec((1, pad, w.shape[2]), lambda i, turn, at: (order(i), 0, 0)) for w in ws],
            out_specs=[sent, kept, sent, kept],
            scratch_shapes=[pltpu.VMEM(gg.shape, BF) for gg in ggs] + [pltpu.SemaphoreType.DMA((count,))],
        ),
        out_shape=[jax.ShapeDtypeStruct((2, t, pad), BF)] * 4,
        compiler_params=params(),
        cost_estimate=TINY,
        name="input_grads",
    )(place, *ggs, *nexts, *ws)


def join_kernel(*refs):
    *terms, out = refs
    v = terms[0][...].astype(F32)
    for ref in terms[1:]:
        v = v + ref[...].astype(F32)
    out[...] = v.astype(BF)


def join(terms, urgency):
    arrays = [v for v, _ in terms]
    shape = arrays[0].shape[-2:]
    steps = 2 if shape[0] % 32 == 0 else 1
    blocks = shape[0] // steps

    def spec(v, at):
        if at is None:
            return pl.BlockSpec((blocks, shape[1]), lambda i: (i, 0))
        return pl.BlockSpec((None, blocks, shape[1]), lambda i, at=at: (at, i, 0))

    return pl.pallas_call(
        join_kernel,
        grid=(steps,),
        in_specs=[spec(v, at) for v, at in terms],
        out_specs=pl.BlockSpec((blocks, shape[1]), lambda i: (i, 0)),
        out_shape=jax.ShapeDtypeStruct(shape, BF),
        compiler_params=params(),
        cost_estimate=pl.CostEstimate(flops=0, bytes_accessed=urgency * 3690000, transcendentals=0),
        name="join",
    )(*arrays)


def unpack_w_kernel(widths, terms, place, *refs):
    count = len(widths)
    outs = refs[-2:]
    last = [
        ref if at is None else ref.at[at] for ref, at in zip(refs[2 * count - 2 :], terms)
    ]
    pieces = [*refs[: 2 * count - 2], None, refs[2 * count - 2 + len(terms)]]
    low = place[1] == 0
    for tap in range(2):
        for k in range(3):
            mine, other = [], []
            for i, c in enumerate(widths):
                for _, lo, w in cuts(c):
                    cols = group(tap * 3 + k, lo, w)
                    if pieces[2 * i] is None:
                        mine.append(functools.reduce(lambda v, ref: v + ref[:, cols].astype(F32), last, 0.0))
                    else:
                        mine.append(pieces[2 * i][:, cols].astype(F32))
                    other.append(pieces[2 * i + 1][:, cols].astype(F32))
            mine, other = jnp.concatenate(mine, axis=1), jnp.concatenate(other, axis=1)
            outs[tap][k] = jnp.concatenate([jnp.where(low, mine, other), jnp.where(low, other, mine)], axis=1)


def unpack_weights(widths, place, pairs, last, other):
    rows = other.shape[0]
    shape = jax.ShapeDtypeStruct((3, rows, 2 * sum(widths)), F32)

    return pl.pallas_call(
        functools.partial(unpack_w_kernel, widths, tuple(at for _, at in last)),
        in_specs=[SMEM_SPEC] + [VMEM_SPEC] * (len(pairs) + len(last) + 1),
        out_shape=[shape, shape],
        compiler_params=params(),
        cost_estimate=TINY,
        name="unpack_weights",
    )(place, *pairs, *[v for v, _ in last], other)


def unpack_h_kernel(widths, place, *refs):
    out_ref = refs[-1]
    low = place[1] == 0

    def body(r, _):
        rows = pl.ds(pl.multiple_of(r * TM, TM), TM)
        mine = jnp.concatenate([refs[i][rows, :].astype(F32) for i in range(len(widths))], axis=1)
        other = refs[len(widths)][rows, : sum(widths)].astype(F32)
        both_halves = jnp.concatenate([jnp.where(low, mine, other), jnp.where(low, other, mine)], axis=1)
        out_ref[rows, :] = both_halves.astype(BF)
        return 0

    lax.fori_loop(0, out_ref.shape[0] // TM, body, 0)


def unpack_hidden(widths, place, mine, other):
    t = other.shape[0]
    return pl.pallas_call(
        functools.partial(unpack_h_kernel, widths),
        in_specs=[SMEM_SPEC] + [VMEM_SPEC] * (len(mine) + 1),
        out_shape=jax.ShapeDtypeStruct((t, 2 * sum(widths)), BF),
        compiler_params=params(),
        cost_estimate=TINY,
        name="unpack_hidden",
    )(place, *mine, other)


def on_device(layer_input, keep, w_now, w_prev, bias, grad_out):
    n, m = lax.axis_size("seq"), lax.axis_size("gate")
    heads = n // 4
    s, g = lax.axis_index("seq"), lax.axis_index("gate")
    h, l, p, a, b = s // 4, s // 2 % 2, s % 2, g // 2, g % 2
    place = jnp.stack([h, l, p, a, b]).astype(jnp.int32)
    t, dl = layer_input.shape
    dw = w_now.shape[1]
    half = dl // 2
    pad = ceil_to(dl, LANES)
    widths = tuple(w for w in WIDTHS) if sum(WIDTHS) == half else (half,)
    low = l == 0

    def seq_to(v, kh, d_l, d_p):
        route = []
        for i in range(n):
            i_h, i_l, i_p = i // 4, i // 2 % 2, i % 2
            route.append((i, ((i_h + kh) % heads * 2 + (i_l ^ d_l)) * 2 + (i_p ^ d_p)))
        return lax.ppermute(v, "seq", route)

    def gate_to(v, d_a, d_b):
        return lax.ppermute(v, "gate", [(i, i ^ (d_a * 2 + d_b)) for i in range(m)])

    group = [(kh, d_p) for kh in range(heads) for d_p in range(2)]

    packed = pack_weights(widths, 0, place, w_now, w_prev)
    behind = lax.ppermute(layer_input[-1:], "seq", [(i, i + 1) for i in range(n - 1)])
    flags = jnp.broadcast_to(jnp.pad(keep, (0, EDGE)).astype(BF)[:, None], (t + EDGE, pad - dl))
    rows = jnp.concatenate([layer_input, jnp.pad(behind, ((0, EDGE - 1), (0, 0)))], axis=0)
    x0 = after(jnp.concatenate([rows, flags], axis=1), packed[0])
    def share_w(pair, *needs):
        got = {(0, 0): pair, (0, 1): seq_to(pair, 0, 0, 1)}
        for kh in range(1, heads):
            got[kh, 0] = seq_to(after(pair, *needs) if needs else pair, kh, 0, 0)
        return got

    def finish_share(got, *needs):
        for kh in range(1, heads):
            got[kh, 1] = seq_to(after(got[kh, 0], *needs) if needs else got[kh, 0], 0, 0, 1)

    def weights_in(got, c):
        if dw % 16 == 0:
            return [got[r] for r in got], list(got)
        stacked = jnp.stack([got[kh, d_p][d_l] for kh in range(heads) for d_l in range(2) for d_p in range(2)])
        blocks = jnp.arange(n)
        rel = (((h - blocks // 4) % heads) * 2 + (l ^ (blocks // 2 % 2))) * 2 + (p ^ (blocks % 2))
        whole = jnp.take(stacked, rel, axis=0).reshape(m, dl, 6 * c)
        return [jnp.pad(whole, ((0, 0), (0, pad - dl), (0, 0)))], []

    half_bias = jnp.where(low, bias[:, :half], bias[:, half:])
    count = len(widths)
    spans = list(offsets(widths))
    near = seq_to(packed[1], 0, 1, 0)
    got = [share_w(jnp.stack([packed[0], near]))]
    y0 = gate_to(x0, 1, 0)
    x1 = seq_to(after(x0, near), 0, 1, 0)
    first_p = got[0][0, 1]
    up_packed = pack_up(widths, place, after(grad_out, x0))
    ups = [[up_packed[0], seq_to(after(up_packed[1], near), 0, 1, 0)]]
    hop = [got[0][kh, 0] for kh in range(1, heads)]
    c0, cy0 = gate_to(after(x0, y0, first_p, *hop), 0, 1), gate_to(after(y0, first_p, *hop), 0, 1)
    x1_here = after(x1, y0, first_p)
    y1, c1 = gate_to(x1_here, 1, 0), gate_to(x1_here, 0, 1)
    finish_share(got[0])
    for i in range(1, count):
        packed = pack_weights(widths, i, place, after(w_now, near), w_prev)
        near = seq_to(packed[1], 0, 1, 0)
        got.append(share_w(jnp.stack([packed[0], near]), c1, *[got[i - 1][kh, 0] for kh in range(1, heads)]))
        ups.append([up_packed[2 * i], seq_to(after(up_packed[2 * i + 1], near), 0, 1, 0)])
    cy1 = gate_to(after(y1, ups[0][1], *[got[0][kh, 1] for kh in range(1, heads)]), 0, 1)
    xs = {(0, 0, 0): x0, (0, 1, 0): y0, (0, 0, 1): c0, (0, 1, 1): cy0}
    xs |= {(1, 0, 0): x1, (1, 1, 0): y1, (1, 0, 1): c1, (1, 1, 1): cy1}
    hidden_mine, hidden_other, grads, wide_w, g_first, g_bias, w_pairs = [], [], [], [], [], [], []

    def spread_totals(tot):
        return jnp.stack([tot if r == (0, 0) else seq_to(tot, r[0], 0, r[1]) for r in group])

    def weight_parts(gg, gp, *needs):
        if dw % 16 == 0 and n == 2 * m:
            return weight_grads(heads, dw, pad, place, x_all, halo, gg, after(gp, *needs) if needs else gp)
        dots = jnp.einsum("td,tn->dn", x_all, gg, preferred_element_type=F32)
        dots = dots + jnp.einsum("td,tn->dn", halo, gp, preferred_element_type=F32)
        v = dots.astype(BF).reshape(m, pad, -1)[:, :dl].reshape(heads, 2, 2, dw, gg.shape[1])
        away = jnp.where(p == 0, v[:, :, 1], v[:, :, 0])
        here = jnp.where(p == 0, v[:, :, 0], v[:, :, 1])

        def block(v, kh):
            row = lax.dynamic_index_in_dim(v, (h + kh) % heads, 0, keepdims=False)
            return jnp.where(low, row[::-1], row)

        return [(kh, block(here, kh), block(away, kh)) for kh in list(range(1, heads)) + [0]]

    def over_p(parts, *needs):
        came = []
        for _, _, away in parts:
            came.append(after(seq_to(away, 0, 0, 1), *came[-1:], *needs))
        return [here.astype(F32) + v.astype(F32) for (_, here, _), v in zip(parts, came)]

    def over_h(parts, sums, *needs):
        total = sums[-1]
        for (kh, _, _), v in zip(parts[:-1], sums[:-1]):
            total = total + after(seq_to(v.astype(BF), kh, 0, 0), *needs).astype(F32)
        return total.astype(BF)

    waiting = None
    for i, (at, c) in enumerate(spans):
        dims = (n, m, dw, dl, t, c)
        bias_i = half_bias[:, at : at + c]
        if i > 0:
            finish_share(got[i], every, ups[i][1])
        w_in, wrel = weights_in(got[i], c)
        if i == 0:
            xrel = list(xs)
            gates, seg, tot, x_all, halo, keep_w, w_rel = gates_and_totals(
                dims, 0, place, w_in, wrel, [xs[r] for r in xrel], xrel, bias_i, ups[i]
            )
        else:
            w_in[0] = after(w_in[0], *[v[2] for v in waiting[:-1]])
            gates, seg, tot, w_rel = gates_and_totals(
                dims, 0, place, w_in, wrel, [x_all, halo], [], bias_i, ups[i], keep_w
            )
        every = spread_totals(after(tot, *[g[0, 1] for g in got[i + 1 : i + 2]]) if i + 1 < count else tot)
        wide_w.append(w_rel)
        if i > 0:
            (kh0, here0, away0), *others = waiting[::-1]
            others = others[::-1]
            sums = over_p(others, tot)
            every_now = after(every, *sums)
            h_sums = [after(v, every) for v in sums]
            (near_sum,) = over_p([(kh0, here0, after(away0, every))])
            h_sums.append(near_sum)
            every = every_now
        before = hidden_other if i == count - 1 else ()
        h0, h1, gg, gf, gp, gb = finish(n, 0, place, gates, ups[i], keep_w, seg, every, before)
        hidden_mine.append(h0)
        hidden_other.append(h1)
        g_first.append(gf)
        g_bias.append(gb)
        if i == count - 1:
            parts = jnp.concatenate([jnp.concatenate(g_first, axis=1), jnp.concatenate(g_bias, axis=1)], axis=0)
            around = [parts if r == (0, 0) else seq_to(parts, r[0], 0, r[1]) for r in group]
            hidden_came = seq_to(after(h1, parts), 0, 1, 0)
        needs = list(around) if i == count - 1 else []
        if i > 0:
            total = over_h(waiting, h_sums)
            needs.append(total)
        waiting_next = weight_parts(gg, gp)
        if needs:
            waiting_next = [(kh, here, after(away, *needs)) for kh, here, away in waiting_next]
        if i > 0:
            w_pairs += [total[1], seq_to(total[0], 0, 1, 0)]
        waiting = waiting_next
        grads.append(gg)
    around = jnp.stack(around)

    full_bias = jnp.sum(around[:, 2], axis=0)
    nexts = []
    for slot in range(2):
        block_id = (h * 2 + (l ^ slot)) * 2 + p + 1
        n_h, n_l, n_p = block_id // 4, block_id // 2 % 2, block_id % 2
        member = ((h - n_h) % heads) * 2 + (p ^ n_p)
        row = lax.dynamic_index_in_dim(around, member, 0, keepdims=False)
        row = lax.dynamic_index_in_dim(row, l ^ n_l, 0, keepdims=False)
        nexts.append(jnp.where(block_id < n, row, jnp.zeros_like(row)))
    nexts = jnp.stack(nexts)
    nexts = [nexts[:, 3 * at : 3 * (at + c)] for at, c in spans]
    bias_half = []
    at = 0
    for c in widths:
        bias_half.append(full_bias[at : at + 3 * c].reshape(3, c))
        at += 3 * c
    bias_half = jnp.concatenate(bias_half, axis=1)
    bias_other = seq_to(bias_half, 0, 1, 0)
    nexts[0] = after(nexts[0], *[v[2] for v in waiting])
    sent1, kept1, sent0, kept0 = input_grads(place, grads, nexts, wide_w)
    p_came = []
    for v in waiting:
        p_came.append(after(seq_to(v[2], 0, 0, 1), *p_came[-1:]))
    sent1, sent0, *_ = lax.optimization_barrier((sent1, sent0, p_came[0], hidden_came, bias_other, *w_pairs))
    c_came1, c_came0 = gate_to(sent1, 0, 1), gate_to(sent0, 0, 1)
    farther = [join([(here, 0), (p_came[k], 0)], LATER) for k, (_, here, _) in enumerate(waiting[:-1])]
    c_came1 = after(c_came1, *farther)
    h_came = [seq_to(v, waiting[k][0], 0, 0) for k, v in enumerate(farther)]
    y_came1 = gate_to(join([(kept1, 1), (c_came1, 1)], LATER), 1, 0)
    total = join([(waiting[-1][1], 0), (p_came[-1], 0)] + [(v, None) for v in h_came], LATER)
    l_total = seq_to(total, 0, 1, 0)
    x_part = join([(kept1, 0), (c_came1, 0), (after(y_came1, total), None)], LATER)
    l_came = seq_to(x_part, 0, 1, 0)
    c_came0 = after(c_came0, x_part)
    y_came0 = gate_to(join([(kept0, 1), (c_came0, 1)], LATER), 1, 0)
    rest = [join([(here, 1), (p_came[k], 1)], LATER) for k, (_, here, _) in enumerate(waiting[:-1])]
    h_rest = [seq_to(after(v, y_came1, total), waiting[k][0], 0, 0) for k, v in enumerate(rest)]
    grad_x = kept0[0].astype(F32) + c_came0[0].astype(F32) + y_came0.astype(F32) + l_came.astype(F32)
    grad_x = grad_x[:, :dl].astype(BF)
    h_rest = [after(v, grad_x) for v in h_rest]
    last = [(waiting[-1][1], 1), (p_came[-1], 1)] + [(v, None) for v in h_rest]

    grad_bias = jnp.concatenate(
        [jnp.where(low, bias_half, bias_other), jnp.where(low, bias_other, bias_half)], axis=1
    )
    hidden = unpack_hidden(widths, place, hidden_mine, hidden_came)
    grad_now, grad_prev = unpack_weights(widths, place, w_pairs, last, l_total)
    return hidden, grad_x, grad_now, grad_prev, grad_bias


def solution(mesh):
    tokens, matrix = P("seq", "gate"), P(None, "seq", "gate")
    return jax.shard_map(
        on_device,
        mesh=mesh,
        in_specs=(tokens, P("seq"), matrix, matrix, P(None, "gate"), tokens),
        out_specs=(tokens, tokens, matrix, matrix, P(None, "gate")),
        check_vma=False,
    )
```
